32 devices in a mesh: dp: 4 (over y, x), fsdp: 8 (over z, core).
Axes of the slice: x: 2, y: 2, z: 4, core: 2. Of those that a mesh axis runs over, the one named last changes fastest.
Arguments:
- tokens: bfloat16 [32768, 512], P(('dp', 'fsdp')), may hold values from -6 to 6
- encoded: bfloat16 [32768, 512], P(('dp', 'fsdp')), may hold values from -6 to 6
- cotangent: bfloat16 [32768, 512], P(('dp', 'fsdp')), may hold values from -6 to 6
- target_ids: int32 [32, 1024], P(('dp', 'fsdp')), may hold values from 0 to 9, never falling along the last dimension, each value on 1 to 200 neighbouring positions
- source_ids: int32 [32, 1024], P(('dp', 'fsdp')), may hold values from 0 to 9, never falling along the last dimension, each value on 1 to 200 neighbouring positions
- qkv_master: float32 [6, 512, 512], P(None, ('dp', 'fsdp')), may hold values from -0.25 to 0.25
- qkv_first: float32 [6, 512, 512], P(None, ('dp', 'fsdp')), may hold values from -16 to 16
- qkv_second: float32 [6, 512, 512], P(None, ('dp', 'fsdp')), may hold values from 0 to 100, as said below
- out_master: float32 [2, 512, 512], P(None, ('dp', 'fsdp')), may hold values from -1.75 to 1.75
- out_first: float32 [2, 512, 512], P(None, ('dp', 'fsdp')), may hold values from -16 to 16
- out_second: float32 [2, 512, 512], P(None, ('dp', 'fsdp')), may hold values from 0 to 100, as said below
- ffn_in_master: float32 [512, 2048], P(('dp', 'fsdp')), may hold values from -0.25 to 0.25
- ffn_in_first: float32 [512, 2048], P(('dp', 'fsdp')), may hold values from -16 to 16
- ffn_in_second: float32 [512, 2048], P(('dp', 'fsdp')), may hold values from 0 to 100, as said below
- ffn_out_master: float32 [2048, 512], P(('dp', 'fsdp')), may hold values from -0.125 to 0.125
- ffn_out_first: float32 [2048, 512], P(('dp', 'fsdp')), may hold values from -16 to 16
- ffn_out_second: float32 [2048, 512], P(('dp', 'fsdp')), may hold values from 0 to 100, as said below
- vector_master: float32 [17, 512], P(None, ('dp', 'fsdp')), may hold values from -3 to 3
- vector_first: float32 [17, 512], P(None, ('dp', 'fsdp')), may hold values from -16 to 16
- vector_second: float32 [17, 512], P(None, ('dp', 'fsdp')), may hold values from 0 to 120, as said below
Outputs:
- layer_out: bfloat16 [32768, 512], P(('dp', 'fsdp'))
- tokens_grad: float32 [32768, 512], P(('dp', 'fsdp'))
- encoded_grad: float32 [32768, 512], P(('dp', 'fsdp'))
- qkv_first_new: float32 [6, 512, 512], P(None, ('dp', 'fsdp'))
- qkv_second_new: float32 [6, 512, 512], P(None, ('dp', 'fsdp'))
- qkv_master_new: float32 [6, 512, 512], P(None, ('dp', 'fsdp'))
- qkv_copy: bfloat16 [6, 512, 512], P(None, ('dp', 'fsdp'))
- out_first_new: float32 [2, 512, 512], P(None, ('dp', 'fsdp'))
- out_second_new: float32 [2, 512, 512], P(None, ('dp', 'fsdp'))
- out_master_new: float32 [2, 512, 512], P(None, ('dp', 'fsdp'))
- out_copy: bfloat16 [2, 512, 512], P(None, ('dp', 'fsdp'))
- ffn_in_first_new: float32 [512, 2048], P(('dp', 'fsdp'))
- ffn_in_second_new: float32 [512, 2048], P(('dp', 'fsdp'))
- ffn_in_master_new: float32 [512, 2048], P(('dp', 'fsdp'))
- ffn_in_copy: bfloat16 [512, 2048], P(('dp', 'fsdp'))
- ffn_out_first_new: float32 [2048, 512], P(('dp', 'fsdp'))
- ffn_out_second_new: float32 [2048, 512], P(('dp', 'fsdp'))
- ffn_out_master_new: float32 [2048, 512], P(('dp', 'fsdp'))
- ffn_out_copy: bfloat16 [2048, 512], P(('dp', 'fsdp'))
- vector_first_new: float32 [17, 512], P(None, ('dp', 'fsdp'))
- vector_second_new: float32 [17, 512], P(None, ('dp', 'fsdp'))
- vector_master_new: float32 [17, 512], P(None, ('dp', 'fsdp'))
- vector_copy: bfloat16 [17, 512], P(None, ('dp', 'fsdp'))
The draws below stay inside these ranges and needn't reach their ends.
Inputs may be any that keep to these rules, and one draw needn't show every extreme that they name: `target_ids`: in each row (one group) ids never fall and every id of 0 to 9 occurs, in a run of 1 to 200 positions; one run has exactly 200. `source_ids`: in each row (one group) ids never fall and every id of 0 to 9 occurs, in a run of 1 to 200 positions; one run has exactly 200. `qkv_second`: positive. `out_second`: positive. `ffn_in_second`: positive. `ffn_out_second`: positive. `vector_second`: positive.
All inputs are finite; a program needn't handle non-finite values.
Results may differ from the reference program's by a relative error of at most 0.02.
The reference program's roundings to bfloat16 on the way count: a program that leaves them out, or rounds other values in their place, can miss the bound.
Values may be sent and summed in bfloat16 or wider, within the bound.
No kernel may reach another device: no remote copies, remote signals or barrier semaphores. Data moves between devices by JAX's collectives and lax.ppermute only.
A program may use at most 192 MiB of HBM per device.

```python
import math
import jax
import jax.numpy as jnp
import numpy as np
from jax import lax

D = 512
HEADS = 8
FF = 2048
VEC = 17
TOK_DEV = 1024
SEG_MOST = 200
SEGS = 10
STEP = 5
TOKENS = 32768
DEVICES = 32


def attention_size():
    return 6.0 / math.sqrt(TOK_DEV / SEGS)


def value_bias_size():
    return 0.8 * math.sqrt(40.0)


def out_size():
    return 0.8 * math.sqrt(0.04 + SEGS / TOK_DEV)


def ffn_in_size():
    return 0.56


def vector_sizes():
    attn_value = attention_size()
    bias_value = value_bias_size()
    resid_value = 0.8
    leading = [attn_value, bias_value, resid_value, attn_value, bias_value, resid_value, resid_value] + [resid_value] * 6
    trailing = [ffn_in_size()] * (FF // D)
    return jnp.array(leading + trailing, jnp.float32)[:, None]


def signed_moment(key, shape, grad_size):
    return jnp.clip(jax.random.normal(key, shape, jnp.float32), -3.0, 3.0) * grad_size


def square_moment(key, shape, grad_size):
    unit_draw = jax.random.uniform(key, shape, jnp.float32)
    return grad_size * grad_size * jnp.exp(unit_draw * math.log(4.0))


def draw_qkv_first(key, part):
    return signed_moment(key, (6, D, D), attention_size())


def draw_qkv_second(key, part):
    return square_moment(key, (6, D, D), attention_size())


def draw_out_first(key, part):
    return signed_moment(key, (2, D, D), out_size())


def draw_out_second(key, part):
    return square_moment(key, (2, D, D), out_size())


def draw_ffn_in_first(key, part):
    return signed_moment(key, (D, FF), ffn_in_size())


def draw_ffn_in_second(key, part):
    return square_moment(key, (D, FF), ffn_in_size())


def draw_ffn_out_first(key, part):
    return signed_moment(key, (FF, D), 0.5)


def draw_ffn_out_second(key, part):
    return square_moment(key, (FF, D), 0.5)


def draw_vector_first(key, part):
    return signed_moment(key, (VEC, D), vector_sizes())


def draw_vector_second(key, part):
    return square_moment(key, (VEC, D), vector_sizes())


def block_scale(own_key, shape, cuts, low, high):
    level, own = 1.0, jax.random.fold_in(own_key, 6)
    for dim, blocks in cuts:
        heights = jnp.exp(jax.random.uniform(jax.random.fold_in(own, dim), (blocks,), jnp.float32, low / len(cuts), high / len(cuts)))
        level = level * jnp.repeat(heights, shape[dim] // blocks).reshape([-1 if axis == dim else 1 for axis in range(len(shape))])
    return level


def profile(amount, total, bound, lean):
    portions = [(1 << 20) // math.isqrt(grade ** lean) + 1 for grade in range(2, amount + 1)]
    surplus, counts = total - bound - (amount - 1), [1] * (amount - 1)
    while surplus > 0:
        candidates = [i for i in range(amount - 1) if counts[i] < bound]
        mass, left = sum([portions[i] for i in candidates]), surplus
        for i in candidates:
            addition = min(bound - counts[i], max(1, left * portions[i] // mass), surplus)
            counts[i] = counts[i] + addition
            surplus = surplus - addition
    return np.array([bound] + counts)


def uneven(stream_key, count, total, reach, lean):
    if count == 2:
        one = jax.random.randint(stream_key, (), max(1, total - reach), min(reach, total - 1) + 1)
        return jnp.stack([one, total - one])
    lengths = jnp.asarray(profile(count, total, reach, lean), jnp.int32)
    couples = (count - 1) // 2
    source_of, taker = lengths[1:1 + 2 * couples:2], lengths[2:2 + 2 * couples:2]
    margin = jnp.minimum(source_of - 1, reach - taker)
    moved = jax.random.randint(jax.random.fold_in(stream_key, 1), (couples,), 0, 1 << 20) % (margin + 1)
    lengths = lengths.at[1:1 + 2 * couples:2].set(source_of - moved).at[2:2 + 2 * couples:2].set(taker + moved)
    return lengths[jax.random.permutation(jax.random.fold_in(stream_key, 2), count)]


def gaussian(stream_key, dims, width, bound, cuts=(), held_as=jnp.bfloat16):
    level = block_scale(stream_key, dims, cuts, -0.22, 0.18) if cuts else 1.0
    result = jax.random.normal(stream_key, dims, jnp.float32) * width * level
    return jnp.minimum(jnp.maximum(result, -bound), bound).astype(held_as)


def setup_inputs(seed: int = 0) -> dict:
    streams_of = jax.random.split(jax.random.key(seed), 21)
    return {
        "tokens": gaussian(streams_of[0], (TOKENS, D), 1.0, 6.0, ((0, 32),)),
        "encoded": gaussian(streams_of[1], (TOKENS, D), 1.0, 6.0, ((0, 32),)),
        "cotangent": gaussian(streams_of[2], (TOKENS, D), 1.0, 6.0, ((0, 32),)),
        "target_ids": jax.vmap(lambda own: jnp.searchsorted(jnp.cumsum(uneven(own, SEGS, TOK_DEV, SEG_MOST, 1)), jnp.arange(TOK_DEV), side="right"))(jax.random.split(streams_of[3], DEVICES)).reshape((DEVICES, TOK_DEV)).astype(jnp.int32),
        "source_ids": jax.vmap(lambda own: jnp.searchsorted(jnp.cumsum(uneven(own, SEGS, TOK_DEV, SEG_MOST, 1)), jnp.arange(TOK_DEV), side="right"))(jax.random.split(streams_of[4], DEVICES)).reshape((DEVICES, TOK_DEV)).astype(jnp.int32),
        "qkv_master": gaussian(streams_of[5], (6, D, D), D ** -0.5, 0.25, ((1, 32),), jnp.float32),
        "qkv_first": draw_qkv_first(jax.random.fold_in(streams_of[20], 71), 0),
        "qkv_second": draw_qkv_second(jax.random.fold_in(streams_of[20], 71), 0),
        "out_master": gaussian(streams_of[8], (2, D, D), (D // 40) ** -0.5, 1.75, ((1, 32),), jnp.float32),
        "out_first": draw_out_first(jax.random.fold_in(streams_of[20], 71), 0),
        "out_second": draw_out_second(jax.random.fold_in(streams_of[20], 71), 0),
        "ffn_in_master": gaussian(streams_of[11], (D, FF), D ** -0.5, 0.25, ((0, 32),), jnp.float32),
        "ffn_in_first": draw_ffn_in_first(jax.random.fold_in(streams_of[20], 71), 0),
        "ffn_in_second": draw_ffn_in_second(jax.random.fold_in(streams_of[20], 71), 0),
        "ffn_out_master": gaussian(streams_of[14], (FF, D), FF ** -0.5, 0.125, ((0, 32),), jnp.float32),
        "ffn_out_first": draw_ffn_out_first(jax.random.fold_in(streams_of[20], 71), 0),
        "ffn_out_second": draw_ffn_out_second(jax.random.fold_in(streams_of[20], 71), 0),
        "vector_master": gaussian(streams_of[17], (VEC, D), 0.2, 3.0, ((1, 32),), jnp.float32),
        "vector_first": draw_vector_first(jax.random.fold_in(streams_of[20], 71), 0),
        "vector_second": draw_vector_second(jax.random.fold_in(streams_of[20], 71), 0),
    }


@jax.custom_vjp
def low(v):
    return lax.optimization_barrier(v.astype(jnp.bfloat16)).astype(jnp.float32)

@jax.custom_vjp
def low_back(v):
    return v

def low_keep(v):
    return (low(v), None)

def low_pass(kept, grad):
    return (grad,)

def back_keep(v):
    return (v, None)

def back_low(kept, grad):
    return (low(grad),)
low.defvjp(low_keep, low_pass)
low_back.defvjp(back_keep, back_low)
highest = lax.Precision.HIGHEST
norm_eps = 1e-05
beta_first = 0.5
beta_second = 0.5
adam_eps = 1e-08
weight_decay = 0.01

def rounded(value):
    return low(low_back(value))

def product(left, right):
    return jnp.dot(left, right, precision=highest)

def gelu_unit(values):
    return jax.nn.gelu(values, approximate=True)

def layer_norm(values, gain, shift):
    center = values - lax.optimization_barrier(jnp.mean(values, axis=-1, keepdims=True))
    spread = lax.optimization_barrier(jnp.mean(center * center, axis=-1, keepdims=True))
    return center * lax.rsqrt(spread + norm_eps) * (1.0 + gain) + shift

def attention(queries, key_rows, value_rows, same_mask):
    count_rows = queries.shape[0]
    count_cols = key_rows.shape[0]
    head_width = queries.shape[1] // HEADS
    factor = 1.0 / math.sqrt(head_width)
    query_heads = queries.reshape(count_rows, HEADS, head_width)
    key_heads = key_rows.reshape(count_cols, HEADS, head_width)
    value_heads = value_rows.reshape(count_cols, HEADS, head_width)
    scores = jnp.einsum('thd,shd->hts', query_heads, key_heads, precision=highest) * factor
    scores = low_back(scores)
    scores = jnp.where(same_mask[None], scores, -1000000000.0)
    probs = low(jax.nn.softmax(scores, axis=-1))
    mixed = jnp.einsum('hts,shd->thd', probs, value_heads, precision=highest)
    return mixed.reshape(count_rows, HEADS * head_width)

def decoder_block(inputs, encoder_rows, target_row, source_row, params):
    qkv_weights, out_weights, ffn_first, ffn_second, vector_rows = params
    ffn_bias = vector_rows[13:].reshape(-1)
    self_mask = target_row[:, None] == target_row[None, :]
    cross_mask = target_row[:, None] == source_row[None, :]
    queries = rounded(product(inputs, qkv_weights[0]) + vector_rows[0])
    key_rows = rounded(product(inputs, qkv_weights[1]))
    value_rows = rounded(product(inputs, qkv_weights[2]) + vector_rows[1])
    mixed = rounded(attention(queries, key_rows, value_rows, self_mask))
    branch = low_back(product(mixed, out_weights[0]) + vector_rows[2])
    first_norm = layer_norm(inputs + branch, vector_rows[7], vector_rows[10])
    first_low = low(first_norm)
    cross_queries = rounded(product(first_low, qkv_weights[3]) + vector_rows[3])
    cross_keys = rounded(product(encoder_rows, qkv_weights[4]))
    cross_values = rounded(product(encoder_rows, qkv_weights[5]) + vector_rows[4])
    cross_mixed = rounded(attention(cross_queries, cross_keys, cross_values, cross_mask))
    cross_branch = low_back(product(cross_mixed, out_weights[1]) + vector_rows[5])
    second_norm = layer_norm(first_norm + cross_branch, vector_rows[8], vector_rows[11])
    second_low = low(second_norm)
    hidden = low(gelu_unit(low_back(product(second_low, ffn_first) + ffn_bias)))
    ffn_branch = low_back(product(hidden, ffn_second) + vector_rows[6])
    return layer_norm(second_norm + ffn_branch, vector_rows[9], vector_rows[12])

def adamw(master, grad, first, second, rate):
    first_new = beta_first * first + (1.0 - beta_first) * grad
    second_new = beta_second * second + (1.0 - beta_second) * grad * grad
    first_hat = first_new / (1.0 - beta_first ** STEP)
    second_hat = second_new / (1.0 - beta_second ** STEP)
    master_new = master - rate * (first_hat / (jnp.sqrt(second_hat) + adam_eps) + weight_decay * master)
    return (first_new, second_new, master_new, master_new.astype(jnp.bfloat16))

def reference(tokens, encoded, cotangent, target_ids, source_ids, qkv_master, qkv_first, qkv_second, out_master, out_first, out_second, ffn_in_master, ffn_in_first, ffn_in_second, ffn_out_master, ffn_out_first, ffn_out_second, vector_master, vector_first, vector_second):
    groups = target_ids.shape[0]
    model_width = tokens.shape[1]
    masters = (qkv_master, out_master, ffn_in_master, ffn_out_master, vector_master)
    params = tuple((item.astype(jnp.bfloat16).astype(jnp.float32) for item in masters))
    inputs = tokens.astype(jnp.float32).reshape(groups, -1, model_width)
    encoder_rows = encoded.astype(jnp.float32).reshape(groups, -1, model_width)

    def forward(inputs_all, encoder_all, params_all):

        def single(pieces):
            return decoder_block(pieces[0], pieces[1], pieces[2], pieces[3], params_all)
        return lax.map(jax.checkpoint(single), (inputs_all, encoder_all, target_ids, source_ids))
    layer_value, pullback = jax.vjp(forward, inputs, encoder_rows, params)
    grads_input, grads_encoder, grads_params = pullback(cotangent.astype(jnp.float32).reshape(groups, -1, model_width))
    grad_scale = 1.0 / math.sqrt(TOKENS)
    scaled = tuple((item * grad_scale for item in grads_params))
    layer_out = layer_value.reshape(-1, model_width).astype(jnp.bfloat16)
    tokens_grad = grads_input.reshape(-1, model_width)
    encoded_grad = grads_encoder.reshape(-1, model_width)
    qkv_first_new, qkv_second_new, qkv_master_new, qkv_copy = adamw(qkv_master, scaled[0], qkv_first, qkv_second, 0.04)
    out_first_new, out_second_new, out_master_new, out_copy = adamw(out_master, scaled[1], out_first, out_second, 0.3)
    ffn_in_first_new, ffn_in_second_new, ffn_in_master_new, ffn_in_copy = adamw(ffn_in_master, scaled[2], ffn_in_first, ffn_in_second, 0.04)
    ffn_out_first_new, ffn_out_second_new, ffn_out_master_new, ffn_out_copy = adamw(ffn_out_master, scaled[3], ffn_out_first, ffn_out_second, 0.02)
    vector_first_new, vector_second_new, vector_master_new, vector_copy = adamw(vector_master, scaled[4], vector_first, vector_second, 0.35)
    return (layer_out, tokens_grad, encoded_grad, qkv_first_new, qkv_second_new, qkv_master_new, qkv_copy, out_first_new, out_second_new, out_master_new, out_copy, ffn_in_first_new, ffn_in_second_new, ffn_in_master_new, ffn_in_copy, ffn_out_first_new, ffn_out_second_new, ffn_out_master_new, ffn_out_copy, vector_first_new, vector_second_new, vector_master_new, vector_copy)
```

```python
import math

import jax
import jax.numpy as jnp
from jax import lax
from jax.sharding import PartitionSpec as P

HEADS = 8
STEP = 5


norm_eps = 1e-05
beta_first = 0.5
beta_second = 0.5
adam_eps = 1e-08
weight_decay = 0.01
mask_fill = -1000000000.0


def matmul(left, right):
    return jnp.dot(left, right, preferred_element_type=jnp.float32)


def product_left(left, right):
    return lax.dot_general(
        left, right, (((0,), (0,)), ((), ())), preferred_element_type=jnp.float32
    )


def product_right(left, right):
    return lax.dot_general(
        left, right, (((1,), (1,)), ((), ())), preferred_element_type=jnp.float32
    )


def column_sums(values):
    return jnp.sum(values.astype(jnp.float32), axis=0)


def gelu_unit(values):
    return jax.nn.gelu(values, approximate=True)


def layer_norm(values, gain, shift):
    center = values - jnp.mean(values, axis=-1, keepdims=True)
    spread = jnp.mean(center * center, axis=-1, keepdims=True)
    return center * lax.rsqrt(spread + norm_eps) * (1.0 + gain) + shift


def block_scores(query_heads, key_heads, id_block, col_ids, factor):
    scores = (
        jnp.einsum("thd,shd->hts", query_heads, key_heads, preferred_element_type=jnp.float32)
        * factor
    )
    same_mask = (id_block[:, None] == col_ids[None, :])[None]
    return jnp.where(same_mask, scores, mask_fill)


def attend_forward(queries, key_rows, value_rows, row_ids, col_ids):
    total_rows = queries.shape[0]
    block_rows = min(512, total_rows)
    block_count = total_rows // block_rows
    head_width = queries.shape[1] // HEADS
    factor = 1.0 / math.sqrt(head_width)
    key_heads = key_rows.reshape(-1, HEADS, head_width)
    value_heads = value_rows.reshape(-1, HEADS, head_width)

    def block_step(pieces):
        query_block, id_block = pieces
        query_heads = query_block.reshape(block_rows, HEADS, head_width)
        scores = block_scores(query_heads, key_heads, id_block, col_ids, factor)
        largest = jnp.max(scores, axis=-1, keepdims=True)
        expo_values = jnp.exp(scores - largest)
        totals = jnp.sum(expo_values, axis=-1, keepdims=True)
        probs_low = (expo_values / totals).astype(jnp.bfloat16)
        mixed = jnp.einsum(
            "hts,shd->thd", probs_low, value_heads, preferred_element_type=jnp.float32
        )
        log_sums = (largest + jnp.log(totals))[..., 0]
        return (mixed.reshape(block_rows, -1), log_sums)

    mixed_blocks, log_sums = lax.map(
        block_step,
        (queries.reshape(block_count, block_rows, -1), row_ids.reshape(block_count, block_rows)),
    )
    return (mixed_blocks.reshape(total_rows, -1), log_sums)


def attend_backward(queries, key_rows, value_rows, row_ids, col_ids, log_sums, grad_mixed):
    total_rows = queries.shape[0]
    key_count = key_rows.shape[0]
    block_rows = min(512, total_rows)
    block_count = total_rows // block_rows
    head_width = queries.shape[1] // HEADS
    factor = 1.0 / math.sqrt(head_width)
    key_heads = key_rows.reshape(-1, HEADS, head_width)
    value_heads = value_rows.reshape(-1, HEADS, head_width)

    def block_step(carry, pieces):
        grad_keys, grad_values = carry
        query_block, id_block, sum_block, grad_block = pieces
        query_heads = query_block.reshape(block_rows, HEADS, head_width)
        grad_heads = grad_block.reshape(block_rows, HEADS, head_width)
        scores = block_scores(query_heads, key_heads, id_block, col_ids, factor)
        probs = jnp.exp(scores - sum_block[..., None])
        probs_low = probs.astype(jnp.bfloat16)
        grad_values = grad_values + jnp.einsum(
            "hts,thd->shd", probs_low, grad_heads, preferred_element_type=jnp.float32
        )
        grad_probs = jnp.einsum(
            "thd,shd->hts", grad_heads, value_heads, preferred_element_type=jnp.float32
        )
        inner = jnp.sum(probs * grad_probs, axis=-1, keepdims=True)
        grad_scores = (probs * (grad_probs - inner)).astype(jnp.bfloat16)
        grad_query = (
            jnp.einsum("hts,shd->thd", grad_scores, key_heads, preferred_element_type=jnp.float32)
            * factor
        )
        grad_keys = (
            grad_keys
            + jnp.einsum(
                "hts,thd->shd", grad_scores, query_heads, preferred_element_type=jnp.float32
            )
            * factor
        )
        return ((grad_keys, grad_values), grad_query.reshape(block_rows, -1))

    start = (
        jnp.zeros((key_count, HEADS, head_width), jnp.float32),
        jnp.zeros((key_count, HEADS, head_width), jnp.float32),
    )
    carried, grad_queries = lax.scan(
        block_step,
        start,
        (
            queries.reshape(block_count, block_rows, -1),
            row_ids.reshape(block_count, block_rows),
            log_sums,
            grad_mixed.reshape(block_count, block_rows, -1),
        ),
    )
    grad_keys, grad_values = carried
    return (
        grad_queries.reshape(total_rows, -1),
        grad_keys.reshape(key_count, -1),
        grad_values.reshape(key_count, -1),
    )


def adamw(master, grad, first, second, rate):
    first_new = beta_first * first + (1.0 - beta_first) * grad
    second_new = beta_second * second + (1.0 - beta_second) * grad * grad
    first_hat = first_new / (1.0 - beta_first**STEP)
    second_hat = second_new / (1.0 - beta_second**STEP)
    master_new = master - rate * (
        first_hat / (jnp.sqrt(second_hat) + adam_eps) + weight_decay * master
    )
    return (first_new, second_new, master_new, master_new.astype(jnp.bfloat16))


AXES = ("dp", "fsdp")


def exchange(values, offset):
    count = lax.axis_size("dp") * lax.axis_size("fsdp")
    return lax.ppermute(values, AXES, [(i, i ^ offset) for i in range(count)])


def gather_pieces(piece):
    dp_count, fsdp_count = lax.axis_size("dp"), lax.axis_size("fsdp")
    depth = fsdp_count // 2
    stack = jnp.stack([piece] + [exchange(piece, 2 * k) for k in range(1, depth)])
    near = [stack] + [exchange(stack, fsdp_count * k) for k in range(1, dp_count)]
    far = [exchange(item, 1) for item in near]
    return near, far


def own_index():
    return lax.axis_index("dp") * lax.axis_size("fsdp") + lax.axis_index("fsdp")


def ordered(near, far):
    count = lax.axis_size("dp") * lax.axis_size("fsdp")
    both = jnp.stack([jnp.stack(near), jnp.stack(far)], axis=2)
    flat = both.reshape((count,) + both.shape[3:])
    return flat[jnp.arange(count) ^ own_index()]


def pick(values, index, axis):
    return lax.dynamic_index_in_dim(values, index, axis, keepdims=False)


def scatter_sum(grad):
    dp_count, fsdp_count = lax.axis_size("dp"), lax.axis_size("fsdp")
    depth = fsdp_count // 2
    place_dp, place_fsdp = lax.axis_index("dp"), lax.axis_index("fsdp")
    core, layer = place_fsdp % 2, place_fsdp // 2
    low = jnp.bfloat16
    grad = grad.reshape((dp_count, depth, 2) + grad.shape[1:])
    received = exchange(pick(grad, 1 - core, 2).astype(low), 1)
    pair = pick(grad, core, 2).astype(jnp.float32) + received.astype(jnp.float32)
    square = pick(pair, place_dp, 0)
    for k in range(1, dp_count):
        part = exchange(pick(pair, place_dp ^ k, 0).astype(low), fsdp_count * k)
        square = square + part.astype(jnp.float32)
    total = pick(square, layer, 0)
    for k in range(1, depth):
        part = exchange(pick(square, layer ^ k, 0).astype(low), 2 * k)
        total = total + part.astype(jnp.float32)
    return total


def body(
    tokens,
    encoded,
    cotangent,
    target_ids,
    source_ids,
    qkv_master,
    qkv_first,
    qkv_second,
    out_master,
    out_first,
    out_second,
    ffn_in_master,
    ffn_in_first,
    ffn_in_second,
    ffn_out_master,
    ffn_out_first,
    ffn_out_second,
    vector_master,
    vector_first,
    vector_second,
):
    low_qkv = qkv_master.astype(jnp.bfloat16)
    low_out = out_master.astype(jnp.bfloat16)
    low_ffn_in = ffn_in_master.astype(jnp.bfloat16)
    low_ffn_out = ffn_out_master.astype(jnp.bfloat16)
    low_vector = vector_master.astype(jnp.bfloat16)
    width = tokens.shape[1]
    count = lax.axis_size("dp") * lax.axis_size("fsdp")
    rows = width // count
    vector_count = low_vector.shape[0]
    vector_row = jnp.pad(low_vector.reshape(1, -1), ((0, 7), (0, width - low_vector.size)))
    first_set = ordered(
        *gather_pieces(jnp.concatenate([low_qkv[:3].reshape(-1, width), vector_row]))
    )
    second_set = ordered(
        *gather_pieces(
            jnp.concatenate([low_qkv[3:].reshape(-1, width), low_out.reshape(-1, width)])
        )
    )
    in_piece = low_ffn_in.reshape(rows, -1, width).transpose(1, 0, 2).reshape(-1, width)
    third_set = ordered(*gather_pieces(jnp.concatenate([in_piece, low_ffn_out])))

    def whole(part):
        return part.reshape(count, -1, rows, width).transpose(1, 0, 2, 3).reshape(-1, width, width)

    qkv_full = [*whole(first_set[:, : 3 * rows]), *whole(second_set[:, : 3 * rows])]
    out_full = whole(second_set[:, 3 * rows :])
    in_rows = in_piece.shape[0]
    ffn_in_full = (
        third_set[:, :in_rows].reshape(count, -1, rows, width).transpose(0, 2, 1, 3)
    ).reshape(width, -1)
    ffn_out_full = third_set[:, in_rows:].reshape(-1, width)
    vector_full = (
        first_set[:, 3 * rows, : low_vector.size]
        .reshape(count, vector_count, -1)
        .transpose(1, 0, 2)
        .reshape(vector_count, width)
    )
    qkv_back, out_back, ffn_in_back, ffn_out_back = qkv_full, out_full, ffn_in_full, ffn_out_full
    vectors = vector_full.astype(jnp.float32)
    model_width = vectors.shape[1]
    ffn_bias = vectors[13:].reshape(-1)
    row_ids = target_ids[0]
    source_row = source_ids[0]
    inputs = tokens.astype(jnp.float32)
    queries = (matmul(tokens, qkv_full[0]) + vectors[0]).astype(jnp.bfloat16)
    key_rows = matmul(tokens, qkv_full[1]).astype(jnp.bfloat16)
    value_rows = (matmul(tokens, qkv_full[2]) + vectors[1]).astype(jnp.bfloat16)
    mixed_raw, self_sums = attend_forward(queries, key_rows, value_rows, row_ids, row_ids)
    mixed = mixed_raw.astype(jnp.bfloat16)
    first_sum = inputs + matmul(mixed, out_full[0]) + vectors[2]
    first_norm, first_back = jax.vjp(layer_norm, first_sum, vectors[7], vectors[10])
    first_low = first_norm.astype(jnp.bfloat16)
    cross_queries = (matmul(first_low, qkv_full[3]) + vectors[3]).astype(jnp.bfloat16)
    cross_keys = matmul(encoded, qkv_full[4]).astype(jnp.bfloat16)
    cross_values = (matmul(encoded, qkv_full[5]) + vectors[4]).astype(jnp.bfloat16)
    cross_raw, cross_sums = attend_forward(
        cross_queries, cross_keys, cross_values, row_ids, source_row
    )
    cross_mixed = cross_raw.astype(jnp.bfloat16)
    second_sum = first_norm + matmul(cross_mixed, out_full[1]) + vectors[5]
    second_norm, second_back = jax.vjp(layer_norm, second_sum, vectors[8], vectors[11])
    second_low = second_norm.astype(jnp.bfloat16)
    hidden_pre = matmul(second_low, ffn_in_full) + ffn_bias
    hidden_value, gelu_back = jax.vjp(gelu_unit, hidden_pre)
    hidden = hidden_value.astype(jnp.bfloat16)
    third_sum = second_norm + matmul(hidden, ffn_out_full) + vectors[6]
    layer_value, third_back = jax.vjp(layer_norm, third_sum, vectors[9], vectors[12])
    layer_out = layer_value.astype(jnp.bfloat16)
    grad_third, grad_gain_three, grad_shift_three = third_back(cotangent.astype(jnp.float32))
    grad_ffn = grad_third.astype(jnp.bfloat16)
    grad_ffn_out = product_left(hidden, grad_ffn)
    grad_bias_two = column_sums(grad_ffn)
    grad_hidden = product_right(grad_ffn, ffn_out_back)
    grad_pre = gelu_back(grad_hidden)[0].astype(jnp.bfloat16)
    grad_ffn_in = product_left(second_low, grad_pre)
    grad_bias_one = column_sums(grad_pre)
    grad_second = grad_third + product_right(grad_pre, ffn_in_back)
    grad_second_sum, grad_gain_two, grad_shift_two = second_back(grad_second)
    grad_cross_out = grad_second_sum.astype(jnp.bfloat16)
    grad_weight_cross_out = product_left(cross_mixed, grad_cross_out)
    grad_bias_cross_out = column_sums(grad_cross_out)
    grad_cross_mixed = product_right(grad_cross_out, out_back[1]).astype(jnp.bfloat16)
    cross_query_grad, cross_key_grad, cross_value_grad = attend_backward(
        cross_queries, cross_keys, cross_values, row_ids, source_row, cross_sums, grad_cross_mixed
    )
    cross_query_low = cross_query_grad.astype(jnp.bfloat16)
    cross_key_low = cross_key_grad.astype(jnp.bfloat16)
    cross_value_low = cross_value_grad.astype(jnp.bfloat16)
    grad_weight_cross_query = product_left(first_low, cross_query_low)
    grad_weight_cross_key = product_left(encoded, cross_key_low)
    grad_weight_cross_value = product_left(encoded, cross_value_low)
    grad_bias_cross_query = column_sums(cross_query_low)
    grad_bias_cross_value = column_sums(cross_value_low)
    encoded_grad = product_right(cross_key_low, qkv_back[4]) + product_right(
        cross_value_low, qkv_back[5]
    )
    grad_first = grad_second_sum + product_right(cross_query_low, qkv_back[3])
    grad_first_sum, grad_gain_one, grad_shift_one = first_back(grad_first)
    grad_self_out = grad_first_sum.astype(jnp.bfloat16)
    grad_weight_self_out = product_left(mixed, grad_self_out)
    grad_bias_self_out = column_sums(grad_self_out)
    grad_mixed = product_right(grad_self_out, out_back[0]).astype(jnp.bfloat16)
    self_query_grad, self_key_grad, self_value_grad = attend_backward(
        queries, key_rows, value_rows, row_ids, row_ids, self_sums, grad_mixed
    )
    self_query_low = self_query_grad.astype(jnp.bfloat16)
    self_key_low = self_key_grad.astype(jnp.bfloat16)
    self_value_low = self_value_grad.astype(jnp.bfloat16)
    grad_weight_query = product_left(tokens, self_query_low)
    grad_weight_key = product_left(tokens, self_key_low)
    grad_weight_value = product_left(tokens, self_value_low)
    grad_bias_query = column_sums(self_query_low)
    grad_bias_value = column_sums(self_value_low)
    tokens_grad = (
        grad_first_sum
        + product_right(self_query_low, qkv_back[0])
        + product_right(self_key_low, qkv_back[1])
        + product_right(self_value_low, qkv_back[2])
    )
    small_rows = jnp.stack(
        [
            grad_bias_query,
            grad_bias_value,
            grad_bias_self_out,
            grad_bias_cross_query,
            grad_bias_cross_value,
            grad_bias_cross_out,
            grad_bias_two,
            grad_gain_one,
            grad_gain_two,
            grad_gain_three,
            grad_shift_one,
            grad_shift_two,
            grad_shift_three,
        ]
    )
    grad_vector = jnp.concatenate([small_rows, grad_bias_one.reshape(-1, model_width)], axis=0)

    def split(parts):
        return jnp.concatenate([part.reshape(count, -1, width) for part in parts], axis=1)

    in_split = grad_ffn_in.reshape(count, rows, -1, width).transpose(0, 2, 1, 3)
    ffn_total = scatter_sum(split([in_split, grad_ffn_out]))
    cross_total = scatter_sum(
        split(
            [
                grad_weight_cross_query,
                grad_weight_cross_key,
                grad_weight_cross_value,
                grad_weight_cross_out,
            ]
        )
    )
    vector_split = grad_vector.reshape(vector_count, count, -1).transpose(1, 0, 2).reshape(count, -1)
    vector_split = jnp.pad(vector_split, ((0, 0), (0, width - vector_split.shape[1])))
    self_total = scatter_sum(
        split(
            [
                grad_weight_query,
                grad_weight_key,
                grad_weight_value,
                grad_weight_self_out,
                vector_split[:, None],
            ]
        )
    )
    summed_qkv = jnp.concatenate([self_total[: 3 * rows], cross_total[: 3 * rows]])
    summed_qkv = summed_qkv.reshape(6, rows, width)
    summed_out = jnp.stack([self_total[3 * rows : 4 * rows], cross_total[3 * rows :]])
    summed_ffn_in = ffn_total[:in_rows].reshape(-1, rows, width).transpose(1, 0, 2).reshape(rows, -1)
    summed_ffn_out = ffn_total[in_rows:]
    summed_vector = self_total[4 * rows, : low_vector.size].reshape(vector_count, -1)
    total_tokens = tokens.shape[0] * lax.axis_size("dp") * lax.axis_size("fsdp")
    grad_scale = 1.0 / math.sqrt(total_tokens)
    qkv_first_new, qkv_second_new, qkv_master_new, qkv_copy = adamw(
        qkv_master, summed_qkv * grad_scale, qkv_first, qkv_second, 0.04
    )
    out_first_new, out_second_new, out_master_new, out_copy = adamw(
        out_master, summed_out * grad_scale, out_first, out_second, 0.3
    )
    ffn_in_first_new, ffn_in_second_new, ffn_in_master_new, ffn_in_copy = adamw(
        ffn_in_master, summed_ffn_in * grad_scale, ffn_in_first, ffn_in_second, 0.04
    )
    ffn_out_first_new, ffn_out_second_new, ffn_out_master_new, ffn_out_copy = adamw(
        ffn_out_master, summed_ffn_out * grad_scale, ffn_out_first, ffn_out_second, 0.02
    )
    vector_first_new, vector_second_new, vector_master_new, vector_copy = adamw(
        vector_master, summed_vector * grad_scale, vector_first, vector_second, 0.35
    )
    return (
        layer_out,
        tokens_grad,
        encoded_grad,
        qkv_first_new,
        qkv_second_new,
        qkv_master_new,
        qkv_copy,
        out_first_new,
        out_second_new,
        out_master_new,
        out_copy,
        ffn_in_first_new,
        ffn_in_second_new,
        ffn_in_master_new,
        ffn_in_copy,
        ffn_out_first_new,
        ffn_out_second_new,
        ffn_out_master_new,
        ffn_out_copy,
        vector_first_new,
        vector_second_new,
        vector_master_new,
        vector_copy,
    )


def solution(mesh):
    return jax.shard_map(
        body,
        mesh=mesh,
        in_specs=(
            P(("dp", "fsdp"), None),
            P(("dp", "fsdp"), None),
            P(("dp", "fsdp"), None),
            P(("dp", "fsdp"), None),
            P(("dp", "fsdp"), None),
            P(None, ("dp", "fsdp"), None),
            P(None, ("dp", "fsdp"), None),
            P(None, ("dp", "fsdp"), None),
            P(None, ("dp", "fsdp"), None),
            P(None, ("dp", "fsdp"), None),
            P(None, ("dp", "fsdp"), None),
            P(("dp", "fsdp"), None),
            P(("dp", "fsdp"), None),
            P(("dp", "fsdp"), None),
            P(("dp", "fsdp"), None),
            P(("dp", "fsdp"), None),
            P(("dp", "fsdp"), None),
            P(None, ("dp", "fsdp")),
            P(None, ("dp", "fsdp")),
            P(None, ("dp", "fsdp")),
        ),
        out_specs=(
            P(("dp", "fsdp"), None),
            P(("dp", "fsdp"), None),
            P(("dp", "fsdp"), None),
            P(None, ("dp", "fsdp"), None),
            P(None, ("dp", "fsdp"), None),
            P(None, ("dp", "fsdp"), None),
            P(None, ("dp", "fsdp"), None),
            P(None, ("dp", "fsdp"), None),
            P(None, ("dp", "fsdp"), None),
            P(None, ("dp", "fsdp"), None),
            P(None, ("dp", "fsdp"), None),
            P(("dp", "fsdp"), None),
            P(("dp", "fsdp"), None),
            P(("dp", "fsdp"), None),
            P(("dp", "fsdp"), None),
            P(("dp", "fsdp"), None),
            P(("dp", "fsdp"), None),
            P(("dp", "fsdp"), None),
            P(("dp", "fsdp"), None),
            P(None, ("dp", "fsdp")),
            P(None, ("dp", "fsdp")),
            P(None, ("dp", "fsdp")),
            P(None, ("dp", "fsdp")),
        ),
        check_vma=False,
    )
```

```python
import math

import jax
import jax.numpy as jnp
from jax import lax
from jax.experimental import pallas as pl
from jax.experimental.pallas import tpu as pltpu
from jax.sharding import PartitionSpec as P

HEADS = 8
STEP = 5

SEGMENTS = 10

norm_eps = 1e-05
beta_first = 0.5
beta_second = 0.5
adam_eps = 1e-08
weight_decay = 0.01
mask_fill = -1000000000.0
LOW = jnp.bfloat16
FULL = jnp.float32


def dot_nn(left, right):
    return lax.dot_general(left, right, (((1,), (0,)), ((), ())), preferred_element_type=FULL)


def dot_nt(left, right):
    return lax.dot_general(left, right, (((1,), (1,)), ((), ())), preferred_element_type=FULL)


def head_masks(width, group, factor):
    lane = lax.broadcasted_iota(jnp.int32, (1, group * width), 1) // width
    return [jnp.where(lane == h, factor, 0.0).astype(LOW) for h in range(group)]


def window(start, size, total):
    return pl.multiple_of(jnp.minimum(start // 16 * 16, total - size), 16)


def inside(base, size, begin, end):
    place = lax.broadcasted_iota(jnp.int32, (size, 1), 0) + base
    return (place >= begin) & (place < end)


def attend_forward(row_starts, col_starts, q_ref, k_ref, v_ref, out_ref, sums_ref):
    total, model = q_ref.shape
    width = model // HEADS
    group = 256 // width
    span = 256
    scales = head_masks(width, group, 1.0 / math.sqrt(width))

    def segment(s, carry):
        row_begin, row_end = row_starts[s], row_starts[s + 1]
        col_begin, col_end = col_starts[s], col_starts[s + 1]
        row_base, col_base = window(row_begin, span, total), window(col_begin, span, total)
        rows, cols = pl.ds(row_base, span), pl.ds(col_base, span)
        row_mask = inside(row_base, span, row_begin, row_end)
        col_mask = inside(col_base, span, col_begin, col_end)
        for g in range(HEADS // group):
            lanes = slice(g * 256, (g + 1) * 256)
            query, keys, values = q_ref[rows, lanes], k_ref[cols, lanes], v_ref[cols, lanes]
            stacked = jnp.concatenate([query * scale for scale in scales], axis=0)
            scores = jnp.where(col_mask, dot_nt(keys, stacked), mask_fill)
            largest = jnp.max(scores, axis=0, keepdims=True)
            expo = jnp.exp(scores - largest)
            totals = jnp.sum(expo, axis=0, keepdims=True)
            sums_ref[s, g] = largest + jnp.log(totals)
            probs = (expo * (1.0 / totals)).astype(LOW)
            turned = values.T
            parts = [
                dot_nn(turned[h * width : (h + 1) * width], probs[:, h * span : (h + 1) * span])
                for h in range(group)
            ]
            mixed = jnp.concatenate(parts, axis=0).T
            old = out_ref[rows, lanes].astype(FULL)
            out_ref[rows, lanes] = jnp.where(row_mask, mixed, old).astype(LOW)
        return carry

    lax.fori_loop(0, SEGMENTS, segment, 0)


def attend_backward(
    row_starts, col_starts, q_ref, k_ref, v_ref, grad_ref, sums_ref, dq_ref, dk_ref, dv_ref
):
    total, model = q_ref.shape
    width = model // HEADS
    group = 256 // width
    span = 256
    factor = 1.0 / math.sqrt(width)
    scales = head_masks(width, group, factor)
    picks = head_masks(width, group, 1.0)

    def segment(s, carry):
        row_begin, row_end = row_starts[s], row_starts[s + 1]
        col_begin, col_end = col_starts[s], col_starts[s + 1]
        row_base, col_base = window(row_begin, span, total), window(col_begin, span, total)
        rows, cols = pl.ds(row_base, span), pl.ds(col_base, span)
        row_mask = inside(row_base, span, row_begin, row_end)
        col_mask = inside(col_base, span, col_begin, col_end)
        for g in range(HEADS // group):
            lanes = slice(g * 256, (g + 1) * 256)
            query, keys, values = q_ref[rows, lanes], k_ref[cols, lanes], v_ref[cols, lanes]
            grad = jnp.where(row_mask, grad_ref[rows, lanes].astype(FULL), 0.0).astype(LOW)
            stacked = jnp.concatenate([query * scale for scale in scales], axis=0)
            grads = jnp.concatenate([grad * item for item in picks], axis=0)
            scores = jnp.where(col_mask, dot_nt(keys, stacked), mask_fill)
            probs = jnp.exp(scores - sums_ref[s, g])
            grad_values = dot_nn(probs.astype(LOW), grads)
            weighted = probs * dot_nt(values, grads)
            inner = jnp.sum(weighted, axis=0, keepdims=True)
            grad_scores = (weighted - probs * inner).astype(LOW)
            grad_keys = dot_nn(grad_scores, stacked)
            turned = keys.T
            parts = [
                dot_nn(
                    turned[h * width : (h + 1) * width], grad_scores[:, h * span : (h + 1) * span]
                )
                for h in range(group)
            ]
            grad_query = jnp.concatenate(parts, axis=0).T * factor
            for ref, place, mask, value in (
                (dq_ref, rows, row_mask, grad_query),
                (dk_ref, cols, col_mask, grad_keys),
                (dv_ref, cols, col_mask, grad_values),
            ):
                old = ref[place, lanes].astype(FULL)
                ref[place, lanes] = jnp.where(mask, value, old).astype(LOW)
        return carry

    lax.fori_loop(0, SEGMENTS, segment, 0)


def normalize(values):
    center = values - jnp.mean(values, axis=-1, keepdims=True)
    inverse = lax.rsqrt(jnp.mean(center * center, axis=-1, keepdims=True) + norm_eps)
    return center * inverse, inverse


def normalize_back(grad, gain, unit, inverse):
    scaled = grad * (1.0 + gain)
    mean = jnp.mean(scaled, axis=-1, keepdims=True)
    along = jnp.mean(scaled * unit, axis=-1, keepdims=True)
    return (scaled - mean - unit * along) * inverse


def column_sum(values):
    return jnp.sum(values.astype(FULL), axis=0, keepdims=True)


STEP_ROWS = 256


def row_steps(total, step):
    def run(i, carry):
        step(pl.ds(pl.multiple_of(i * STEP_ROWS, STEP_ROWS), STEP_ROWS))
        return carry

    lax.fori_loop(0, total // STEP_ROWS, run, 0)


def self_forward_kernel(
    row_starts, tokens, weights, vectors, queries, keys, values, mixed, sums
):
    def project(rows):
        block = tokens[rows, :]
        queries[rows, :] = (dot_nn(block, weights[0]) + vectors[0:1, :]).astype(LOW)
        keys[rows, :] = dot_nn(block, weights[1]).astype(LOW)
        values[rows, :] = (dot_nn(block, weights[2]) + vectors[1:2, :]).astype(LOW)

    row_steps(tokens.shape[0], project)
    attend_forward(row_starts, row_starts, queries, keys, values, mixed, sums)


def cross_forward_kernel(
    row_starts, col_starts, tokens, encoded, mixed, weights, out_weights, vectors,
    unit_one, inverse_one, first_low, queries, keys, values, cross_mixed, sums, unit_two, inverse_two,
):
    def project(rows):
        block = encoded[rows, :]
        keys[rows, :] = dot_nn(block, weights[1]).astype(LOW)
        values[rows, :] = (dot_nn(block, weights[2]) + vectors[4:5, :]).astype(LOW)
        summed = tokens[rows, :].astype(FULL) + dot_nn(mixed[rows, :], out_weights[0])
        unit, inverse = normalize(summed + vectors[2:3, :])
        unit_one[rows, :] = unit
        inverse_one[rows, :] = inverse
        low = (unit * (1.0 + vectors[7:8, :]) + vectors[10:11, :]).astype(LOW)
        first_low[rows, :] = low
        queries[rows, :] = (dot_nn(low, weights[0]) + vectors[3:4, :]).astype(LOW)

    total = tokens.shape[0]
    row_steps(total, project)
    attend_forward(row_starts, col_starts, queries, keys, values, cross_mixed, sums)

    def finish(rows):
        first = unit_one[rows, :] * (1.0 + vectors[7:8, :]) + vectors[10:11, :]
        summed = first + dot_nn(cross_mixed[rows, :], out_weights[1]) + vectors[5:6, :]
        unit, inverse = normalize(summed)
        unit_two[rows, :] = unit
        inverse_two[rows, :] = inverse

    row_steps(total, finish)


gelu_scale = math.sqrt(2.0 / math.pi)
gelu_cubic = 0.044715


def ffn_kernel(
    unit_two, inverse_two, cotangent, first_weights, second_weights, cross_out, vectors, bias,
    layer_out, second_low, hidden, grad_ffn, grad_pre, grad_sum, grad_out, grad_mixed, sums, bias_sums,
    slopes,
):
    step = pl.program_id(0)

    @pl.when(step == 0)
    def _():
        sums[...] = jnp.zeros_like(sums)
        bias_sums[...] = jnp.zeros_like(bias_sums)

    unit = unit_two[...]
    second = unit * (1.0 + vectors[8:9, :]) + vectors[11:12, :]
    low = second.astype(LOW)
    second_low[...] = low
    model = low.shape[1]
    pieces = first_weights.shape[1] // model
    total = second + vectors[6:7, :]
    for j in range(pieces):
        lanes = slice(j * model, (j + 1) * model)
        pre = dot_nn(low, first_weights[:, lanes]) + bias[:, lanes]
        square = pre * pre
        bend = jnp.tanh(gelu_scale * pre * (1.0 + gelu_cubic * square))
        half = 0.5 * (1.0 + bend)
        value = (pre * half).astype(LOW)
        hidden[:, lanes] = value
        inner = gelu_scale * (1.0 + 3.0 * gelu_cubic * square)
        slopes[:, lanes] = half + 0.5 * pre * (1.0 - bend * bend) * inner
        total = total + dot_nn(value, second_weights[lanes, :])
    unit_three, inverse_three = normalize(total)
    layer_out[...] = (unit_three * (1.0 + vectors[9:10, :]) + vectors[12:13, :]).astype(LOW)
    upper = cotangent[...].astype(FULL)
    third = normalize_back(upper, vectors[9:10, :], unit_three, inverse_three)
    third_low = third.astype(LOW)
    grad_ffn[...] = third_low
    sums[0:1, :] += column_sum(third_low)
    sums[1:2, :] += column_sum(upper * unit_three)
    sums[2:3, :] += column_sum(upper)
    below = third
    for j in range(pieces):
        lanes = slice(j * model, (j + 1) * model)
        pre = (dot_nt(third_low, second_weights[lanes, :]) * slopes[:, lanes]).astype(LOW)
        grad_pre[:, lanes] = pre
        bias_sums[0:1, lanes] += column_sum(pre)
        below = below + dot_nt(pre, first_weights[:, lanes])
    sums[3:4, :] += column_sum(below * unit)
    sums[4:5, :] += column_sum(below)
    second_sum = normalize_back(below, vectors[8:9, :], unit, inverse_two[...])
    grad_sum[...] = second_sum
    out_low = second_sum.astype(LOW)
    grad_out[...] = out_low
    sums[5:6, :] += column_sum(out_low)
    grad_mixed[...] = dot_nt(out_low, cross_out[...]).astype(LOW)


def cross_backward_kernel(
    row_starts, col_starts, queries, keys, values, grad_mixed_in, sums_in, weights, self_out, vectors,
    grad_sum, unit_one, inverse_one,
    dq, dk, dv, encoded_grad, first_sum, self_low, grad_mixed, sums,
):
    attend_backward(
        row_starts, col_starts, queries, keys, values, grad_mixed_in, sums_in, dq, dk, dv
    )
    sums[...] = jnp.zeros_like(sums)

    def finish(rows):
        query, key, value = dq[rows, :], dk[rows, :], dv[rows, :]
        sums[0:1, :] += column_sum(query)
        sums[1:2, :] += column_sum(value)
        encoded_grad[rows, :] = dot_nt(key, weights[1]) + dot_nt(value, weights[2])
        upper = grad_sum[rows, :] + dot_nt(query, weights[0])
        unit = unit_one[rows, :]
        sums[2:3, :] += column_sum(upper * unit)
        sums[3:4, :] += column_sum(upper)
        below = normalize_back(upper, vectors[7:8, :], unit, inverse_one[rows, :])
        first_sum[rows, :] = below
        low = below.astype(LOW)
        self_low[rows, :] = low
        sums[4:5, :] += column_sum(low)
        grad_mixed[rows, :] = dot_nt(low, self_out[...]).astype(LOW)

    row_steps(queries.shape[0], finish)


def self_backward_kernel(
    row_starts, queries, keys, values, grad_mixed, sums_in, weights, first_sum,
    dq, dk, dv, tokens_grad, sums,
):
    attend_backward(
        row_starts, row_starts, queries, keys, values, grad_mixed, sums_in, dq, dk, dv
    )
    sums[...] = jnp.zeros_like(sums)

    def finish(rows):
        query, key, value = dq[rows, :], dk[rows, :], dv[rows, :]
        sums[0:1, :] += column_sum(query)
        sums[1:2, :] += column_sum(value)
        below = first_sum[rows, :] + dot_nt(query, weights[0])
        tokens_grad[rows, :] = below + dot_nt(key, weights[1]) + dot_nt(value, weights[2])

    row_steps(queries.shape[0], finish)


PARAMS = pltpu.CompilerParams(vmem_limit_bytes=56 << 20)


def call(kernel, name, scalars, arrays, outs, flops, expo):
    specs = [pl.BlockSpec(memory_space=pltpu.SMEM)] * len(scalars)
    specs += [pl.BlockSpec(memory_space=pltpu.VMEM)] * len(arrays)
    shapes = [jax.ShapeDtypeStruct(*item) for item in outs]
    moved = sum(item.size * item.dtype.itemsize for item in [*arrays, *shapes])
    return pl.pallas_call(
        kernel,
        out_shape=shapes,
        in_specs=specs,
        out_specs=[pl.BlockSpec(memory_space=pltpu.VMEM)] * len(outs),
        compiler_params=PARAMS,
        cost_estimate=pl.CostEstimate(flops=flops, transcendentals=expo, bytes_accessed=moved),
        name=name,
    )(*scalars, *arrays)


def local_step(tokens, encoded, cotangent, row_starts, col_starts, qkv, out, ffn_in, ffn_out, vectors):
    total, model = tokens.shape
    hidden_width = ffn_in.shape[1]
    bias = vectors[13:].reshape(1, -1)
    wide = ((total, model), LOW)
    tall = ((total, model), FULL)
    thin = ((total, 1), FULL)
    groups = HEADS * (model // HEADS) // 256
    log_sums = ((SEGMENTS, groups, 1, 1024), FULL)
    small = ((8, model), FULL)
    unit_flops = 2 * total * model * model
    attend_flops = 2 * SEGMENTS * HEADS * 256 * 256 * 256
    queries, keys, values, mixed, self_sums = call(
        self_forward_kernel, "self_forward", [row_starts], [tokens, qkv[:3], vectors],
        [wide, wide, wide, wide, log_sums], 3 * unit_flops + 2 * attend_flops, 0,
    )
    (
        unit_one, inverse_one, first_low, cross_queries, cross_keys, cross_values,
        cross_mixed, cross_sums, unit_two, inverse_two,
    ) = call(
        cross_forward_kernel, "cross_forward", [row_starts, col_starts],
        [tokens, encoded, mixed, qkv[3:], out, vectors],
        [tall, thin, wide, wide, wide, wide, wide, log_sums, tall, thin],
        5 * unit_flops + 2 * attend_flops, 0,
    )
    steps = total // STEP_ROWS
    block = pl.BlockSpec((STEP_ROWS, model), lambda i: (i, 0))
    block_wide = pl.BlockSpec((STEP_ROWS, hidden_width), lambda i: (i, 0))
    block_thin = pl.BlockSpec((STEP_ROWS, 1), lambda i: (i, 0))

    def fixed(shape):
        return pl.BlockSpec(shape, lambda i: (0,) * len(shape))

    hid = ((total, hidden_width), LOW)
    (
        layer_out, second_low, hidden, grad_ffn, grad_pre, grad_sum, grad_cross_out,
        grad_cross_mixed, ffn_sums, bias_sums,
    ) = pl.pallas_call(
        ffn_kernel,
        grid=(steps,),
        out_shape=[
            jax.ShapeDtypeStruct(*item)
            for item in (wide, wide, hid, wide, hid, tall, wide, wide, small, ((8, hidden_width), FULL))
        ],
        in_specs=[
            block, block_thin, block, fixed(ffn_in.shape), fixed(ffn_out.shape),
            fixed((model, model)), fixed(vectors.shape), fixed(bias.shape),
        ],
        out_specs=[
            block, block, block_wide, block, block_wide, block, block, block,
            fixed((8, model)), fixed((8, hidden_width)),
        ],
        scratch_shapes=[pltpu.VMEM((STEP_ROWS, hidden_width), FULL)],
        compiler_params=PARAMS,
        cost_estimate=pl.CostEstimate(
            flops=17 * unit_flops, transcendentals=total * hidden_width, bytes_accessed=24 << 20
        ),
        name="ffn",
    )(unit_two, inverse_two, cotangent, ffn_in, ffn_out, out[1], vectors, bias)
    (
        cross_dq, cross_dk, cross_dv, encoded_grad, first_sum, grad_self_out, grad_mixed, cross_vec,
    ) = call(
        cross_backward_kernel, "cross_backward", [row_starts, col_starts],
        [
            cross_queries, cross_keys, cross_values, grad_cross_mixed, cross_sums, qkv[3:], out[0],
            vectors, grad_sum, unit_one, inverse_one,
        ],
        [wide, wide, wide, tall, tall, wide, wide, small], 4 * unit_flops + 5 * attend_flops, 0,
    )
    self_dq, self_dk, self_dv, tokens_grad, self_vec = call(
        self_backward_kernel, "self_backward", [row_starts],
        [queries, keys, values, grad_mixed, self_sums, qkv[:3], first_sum],
        [wide, wide, wide, tall, small], 3 * unit_flops + 5 * attend_flops, 0,
    )

    def weight_grad(left, right):
        return lax.dot_general(
            left, right, (((0,), (0,)), ((), ())), preferred_element_type=FULL
        )

    grads = dict(
        ffn_out=weight_grad(hidden, grad_ffn),
        ffn_in=weight_grad(second_low, grad_pre),
        cross_out=weight_grad(cross_mixed, grad_cross_out),
        cross_query=weight_grad(first_low, cross_dq),
        cross_key=weight_grad(encoded, cross_dk),
        cross_value=weight_grad(encoded, cross_dv),
        self_out=weight_grad(mixed, grad_self_out),
        query=weight_grad(tokens, self_dq),
        key=weight_grad(tokens, self_dk),
        value=weight_grad(tokens, self_dv),
    )
    small_rows = [
        self_vec[0:2], cross_vec[4:5], cross_vec[0:2], ffn_sums[5:6], ffn_sums[0:1],
        cross_vec[2:3], ffn_sums[3:4], ffn_sums[1:2], cross_vec[3:4], ffn_sums[4:5], ffn_sums[2:3],
    ]
    grads["vector"] = jnp.concatenate(small_rows + [bias_sums[0].reshape(-1, model)], axis=0)
    return layer_out, tokens_grad, encoded_grad, grads


def segment_starts(ids):
    marks = jnp.arange(SEGMENTS + 1, dtype=ids.dtype)
    return jnp.sum((ids[None, :] < marks[:, None]).astype(jnp.int32), axis=1)


def adamw(master, grad, first, second, rate):
    first_new = beta_first * first + (1.0 - beta_first) * grad
    second_new = beta_second * second + (1.0 - beta_second) * grad * grad
    first_hat = first_new / (1.0 - beta_first**STEP)
    second_hat = second_new / (1.0 - beta_second**STEP)
    master_new = master - rate * (
        first_hat / (jnp.sqrt(second_hat) + adam_eps) + weight_decay * master
    )
    return (first_new, second_new, master_new, master_new.astype(jnp.bfloat16))


AXES = ("dp", "fsdp")


def exchange(values, offset):
    count = lax.axis_size("dp") * lax.axis_size("fsdp")
    return lax.ppermute(values, AXES, [(i, i ^ offset) for i in range(count)])


def gather_pieces(piece):
    dp_count, fsdp_count = lax.axis_size("dp"), lax.axis_size("fsdp")
    depth = fsdp_count // 2
    stack = jnp.stack([piece] + [exchange(piece, 2 * k) for k in range(1, depth)])
    near = [stack] + [exchange(stack, fsdp_count * k) for k in range(1, dp_count)]
    far = [exchange(item, 1) for item in near]
    return near, far


def own_index():
    return lax.axis_index("dp") * lax.axis_size("fsdp") + lax.axis_index("fsdp")


def ordered(near, far):
    count = lax.axis_size("dp") * lax.axis_size("fsdp")
    both = jnp.stack([jnp.stack(near), jnp.stack(far)], axis=2)
    flat = both.reshape((count,) + both.shape[3:])
    return flat[jnp.arange(count) ^ own_index()]


def pick(values, index, axis):
    return lax.dynamic_index_in_dim(values, index, axis, keepdims=False)


def scatter_sum(grad):
    dp_count, fsdp_count = lax.axis_size("dp"), lax.axis_size("fsdp")
    depth = fsdp_count // 2
    place_dp, place_fsdp = lax.axis_index("dp"), lax.axis_index("fsdp")
    core, layer = place_fsdp % 2, place_fsdp // 2
    low = jnp.bfloat16
    grad = grad.reshape((dp_count, depth, 2) + grad.shape[1:])
    received = exchange(pick(grad, 1 - core, 2).astype(low), 1)
    pair = pick(grad, core, 2).astype(jnp.float32) + received.astype(jnp.float32)
    square = pick(pair, place_dp, 0)
    for k in range(1, dp_count):
        part = exchange(pick(pair, place_dp ^ k, 0).astype(low), fsdp_count * k)
        square = square + part.astype(jnp.float32)
    total = pick(square, layer, 0)
    for k in range(1, depth):
        part = exchange(pick(square, layer ^ k, 0).astype(low), 2 * k)
        total = total + part.astype(jnp.float32)
    return total


def body(
    tokens,
    encoded,
    cotangent,
    target_ids,
    source_ids,
    qkv_master,
    qkv_first,
    qkv_second,
    out_master,
    out_first,
    out_second,
    ffn_in_master,
    ffn_in_first,
    ffn_in_second,
    ffn_out_master,
    ffn_out_first,
    ffn_out_second,
    vector_master,
    vector_first,
    vector_second,
):
    low_qkv = qkv_master.astype(jnp.bfloat16)
    low_out = out_master.astype(jnp.bfloat16)
    low_ffn_in = ffn_in_master.astype(jnp.bfloat16)
    low_ffn_out = ffn_out_master.astype(jnp.bfloat16)
    low_vector = vector_master.astype(jnp.bfloat16)
    width = tokens.shape[1]
    count = lax.axis_size("dp") * lax.axis_size("fsdp")
    rows = width // count
    vector_count = low_vector.shape[0]
    vector_row = jnp.pad(low_vector.reshape(1, -1), ((0, 7), (0, width - low_vector.size)))
    first_set = ordered(
        *gather_pieces(jnp.concatenate([low_qkv[:3].reshape(-1, width), vector_row]))
    )
    second_set = ordered(
        *gather_pieces(
            jnp.concatenate([low_qkv[3:].reshape(-1, width), low_out.reshape(-1, width)])
        )
    )
    in_piece = low_ffn_in.reshape(rows, -1, width).transpose(1, 0, 2).reshape(-1, width)
    third_set = ordered(*gather_pieces(jnp.concatenate([in_piece, low_ffn_out])))

    def whole(part):
        return part.reshape(count, -1, rows, width).transpose(1, 0, 2, 3).reshape(-1, width, width)

    qkv_full = [*whole(first_set[:, : 3 * rows]), *whole(second_set[:, : 3 * rows])]
    out_full = whole(second_set[:, 3 * rows :])
    in_rows = in_piece.shape[0]
    ffn_in_full = (
        third_set[:, :in_rows].reshape(count, -1, rows, width).transpose(0, 2, 1, 3)
    ).reshape(width, -1)
    ffn_out_full = third_set[:, in_rows:].reshape(-1, width)
    vector_full = (
        first_set[:, 3 * rows, : low_vector.size]
        .reshape(count, vector_count, -1)
        .transpose(1, 0, 2)
        .reshape(vector_count, width)
    )
    vectors = vector_full.astype(jnp.float32)
    layer_out, tokens_grad, encoded_grad, grads = local_step(
        tokens,
        encoded,
        cotangent,
        segment_starts(target_ids[0]),
        segment_starts(source_ids[0]),
        jnp.stack(qkv_full),
        out_full,
        ffn_in_full,
        ffn_out_full,
        vectors,
    )

    def split(parts):
        return jnp.concatenate([part.reshape(count, -1, width) for part in parts], axis=1)

    in_split = grads["ffn_in"].reshape(count, rows, -1, width).transpose(0, 2, 1, 3)
    ffn_total = scatter_sum(split([in_split, grads["ffn_out"]]))
    cross_total = scatter_sum(
        split(
            [
                grads["cross_query"],
                grads["cross_key"],
                grads["cross_value"],
                grads["cross_out"],
            ]
        )
    )
    vector_split = grads["vector"].reshape(vector_count, count, -1).transpose(1, 0, 2).reshape(count, -1)
    vector_split = jnp.pad(vector_split, ((0, 0), (0, width - vector_split.shape[1])))
    self_total = scatter_sum(
        split(
            [
                grads["query"],
                grads["key"],
                grads["value"],
                grads["self_out"],
                vector_split[:, None],
            ]
        )
    )
    summed_qkv = jnp.concatenate([self_total[: 3 * rows], cross_total[: 3 * rows]])
    summed_qkv = summed_qkv.reshape(6, rows, width)
    summed_out = jnp.stack([self_total[3 * rows : 4 * rows], cross_total[3 * rows :]])
    summed_ffn_in = ffn_total[:in_rows].reshape(-1, rows, width).transpose(1, 0, 2).reshape(rows, -1)
    summed_ffn_out = ffn_total[in_rows:]
    summed_vector = self_total[4 * rows, : low_vector.size].reshape(vector_count, -1)
    total_tokens = tokens.shape[0] * lax.axis_size("dp") * lax.axis_size("fsdp")
    grad_scale = 1.0 / math.sqrt(total_tokens)
    qkv_first_new, qkv_second_new, qkv_master_new, qkv_copy = adamw(
        qkv_master, summed_qkv * grad_scale, qkv_first, qkv_second, 0.04
    )
    out_first_new, out_second_new, out_master_new, out_copy = adamw(
        out_master, summed_out * grad_scale, out_first, out_second, 0.3
    )
    ffn_in_first_new, ffn_in_second_new, ffn_in_master_new, ffn_in_copy = adamw(
        ffn_in_master, summed_ffn_in * grad_scale, ffn_in_first, ffn_in_second, 0.04
    )
    ffn_out_first_new, ffn_out_second_new, ffn_out_master_new, ffn_out_copy = adamw(
        ffn_out_master, summed_ffn_out * grad_scale, ffn_out_first, ffn_out_second, 0.02
    )
    vector_first_new, vector_second_new, vector_master_new, vector_copy = adamw(
        vector_master, summed_vector * grad_scale, vector_first, vector_second, 0.35
    )
    return (
        layer_out,
        tokens_grad,
        encoded_grad,
        qkv_first_new,
        qkv_second_new,
        qkv_master_new,
        qkv_copy,
        out_first_new,
        out_second_new,
        out_master_new,
        out_copy,
        ffn_in_first_new,
        ffn_in_second_new,
        ffn_in_master_new,
        ffn_in_copy,
        ffn_out_first_new,
        ffn_out_second_new,
        ffn_out_master_new,
        ffn_out_copy,
        vector_first_new,
        vector_second_new,
        vector_master_new,
        vector_copy,
    )


def solution(mesh):
    return jax.shard_map(
        body,
        mesh=mesh,
        in_specs=(
            P(("dp", "fsdp"), None),
            P(("dp", "fsdp"), None),
            P(("dp", "fsdp"), None),
            P(("dp", "fsdp"), None),
            P(("dp", "fsdp"), None),
            P(None, ("dp", "fsdp"), None),
            P(None, ("dp", "fsdp"), None),
            P(None, ("dp", "fsdp"), None),
            P(None, ("dp", "fsdp"), None),
            P(None, ("dp", "fsdp"), None),
            P(None, ("dp", "fsdp"), None),
            P(("dp", "fsdp"), None),
            P(("dp", "fsdp"), None),
            P(("dp", "fsdp"), None),
            P(("dp", "fsdp"), None),
            P(("dp", "fsdp"), None),
            P(("dp", "fsdp"), None),
            P(None, ("dp", "fsdp")),
            P(None, ("dp", "fsdp")),
            P(None, ("dp", "fsdp")),
        ),
        out_specs=(
            P(("dp", "fsdp"), None),
            P(("dp", "fsdp"), None),
            P(("dp", "fsdp"), None),
            P(None, ("dp", "fsdp"), None),
            P(None, ("dp", "fsdp"), None),
            P(None, ("dp", "fsdp"), None),
            P(None, ("dp", "fsdp"), None),
            P(None, ("dp", "fsdp"), None),
            P(None, ("dp", "fsdp"), None),
            P(None, ("dp", "fsdp"), None),
            P(None, ("dp", "fsdp"), None),
            P(("dp", "fsdp"), None),
            P(("dp", "fsdp"), None),
            P(("dp", "fsdp"), None),
            P(("dp", "fsdp"), None),
            P(("dp", "fsdp"), None),
            P(("dp", "fsdp"), None),
            P(("dp", "fsdp"), None),
            P(("dp", "fsdp"), None),
            P(None, ("dp", "fsdp")),
            P(None, ("dp", "fsdp")),
            P(None, ("dp", "fsdp")),
            P(None, ("dp", "fsdp")),
        ),
        check_vma=False,
    )
```

```python
import functools
import math

import jax
import jax.numpy as jnp
from jax import lax
from jax.experimental import pallas as pl
from jax.experimental.pallas import tpu as pltpu
from jax.sharding import PartitionSpec as P

HEADS = 8
STEP = 5
SEGMENTS = 10
norm_eps = 1e-05
beta_first = 0.5
beta_second = 0.5
adam_eps = 1e-08
weight_decay = 0.01
mask_fill = -1000000000.0
LOW = jnp.bfloat16
FULL = jnp.float32


def dot_nn(left, right):
    return lax.dot_general(left, right, (((1,), (0,)), ((), ())), preferred_element_type=FULL)


def dot_nt(left, right):
    return lax.dot_general(left, right, (((1,), (1,)), ((), ())), preferred_element_type=FULL)


def dot_tn(left, right):
    return lax.dot_general(left, right, (((0,), (0,)), ((), ())), preferred_element_type=FULL)


def head_masks(width, group, factor):
    lane = lax.broadcasted_iota(jnp.int32, (1, group * width), 1) // width
    return [jnp.where(lane == h, factor, 0.0).astype(LOW) for h in range(group)]


def window(start, size, total):
    return pl.multiple_of(jnp.minimum(start // 16 * 16, total - size), 16)


def inside(base, size, begin, end):
    place = lax.broadcasted_iota(jnp.int32, (size, 1), 0) + base
    return (place >= begin) & (place < end)


def attend_forward(row_starts, col_starts, q_ref, k_ref, v_ref, out_ref, sums_ref):
    total, model = q_ref.shape
    width = model // HEADS
    group = 256 // width
    span = 256
    scales = head_masks(width, group, 1.0 / math.sqrt(width))

    def segment(s, carry):
        row_begin, row_end = row_starts[s], row_starts[s + 1]
        col_begin, col_end = col_starts[s], col_starts[s + 1]
        row_base, col_base = window(row_begin, span, total), window(col_begin, span, total)
        rows, cols = pl.ds(row_base, span), pl.ds(col_base, span)
        row_mask = inside(row_base, span, row_begin, row_end)
        col_mask = inside(col_base, span, col_begin, col_end)
        for g in range(HEADS // group):
            lanes = slice(g * 256, (g + 1) * 256)
            query, keys, values = q_ref[rows, lanes], k_ref[cols, lanes], v_ref[cols, lanes]
            stacked = jnp.concatenate([query * scale for scale in scales], axis=0)
            scores = jnp.where(col_mask, dot_nt(keys, stacked), mask_fill)
            largest = jnp.max(scores, axis=0, keepdims=True)
            expo = jnp.exp(scores - largest)
            totals = jnp.sum(expo, axis=0, keepdims=True)
            sums_ref[s, g] = largest + jnp.log(totals)
            probs = (expo * (1.0 / totals)).astype(LOW)
            turned = values.T
            parts = [
                dot_nn(turned[h * width : (h + 1) * width], probs[:, h * span : (h + 1) * span])
                for h in range(group)
            ]
            mixed = jnp.concatenate(parts, axis=0).T
            old = out_ref[rows, lanes].astype(FULL)
            out_ref[rows, lanes] = jnp.where(row_mask, mixed, old).astype(LOW)
        return carry

    lax.fori_loop(0, SEGMENTS, segment, 0)


def attend_backward(
    row_starts, col_starts, q_ref, k_ref, v_ref, grad_ref, sums_ref, dq_ref, dk_ref, dv_ref
):
    total, model = q_ref.shape
    width = model // HEADS
    group = 256 // width
    span = 256
    factor = 1.0 / math.sqrt(width)
    scales = head_masks(width, group, factor)
    picks = head_masks(width, group, 1.0)

    def segment(s, carry):
        row_begin, row_end = row_starts[s], row_starts[s + 1]
        col_begin, col_end = col_starts[s], col_starts[s + 1]
        row_base, col_base = window(row_begin, span, total), window(col_begin, span, total)
        rows, cols = pl.ds(row_base, span), pl.ds(col_base, span)
        row_mask = inside(row_base, span, row_begin, row_end)
        col_mask = inside(col_base, span, col_begin, col_end)
        for g in range(HEADS // group):
            lanes = slice(g * 256, (g + 1) * 256)
            query, keys, values = q_ref[rows, lanes], k_ref[cols, lanes], v_ref[cols, lanes]
            grad = jnp.where(row_mask, grad_ref[rows, lanes].astype(FULL), 0.0).astype(LOW)
            stacked = jnp.concatenate([query * scale for scale in scales], axis=0)
            grads = jnp.concatenate([grad * item for item in picks], axis=0)
            scores = jnp.where(col_mask, dot_nt(keys, stacked), mask_fill)
            probs = jnp.exp(scores - sums_ref[s, g])
            grad_values = dot_nn(probs.astype(LOW), grads)
            weighted = probs * dot_nt(values, grads)
            inner = jnp.sum(weighted, axis=0, keepdims=True)
            grad_scores = (weighted - probs * inner).astype(LOW)
            grad_keys = dot_nn(grad_scores, stacked)
            turned = keys.T
            parts = [
                dot_nn(
                    turned[h * width : (h + 1) * width], grad_scores[:, h * span : (h + 1) * span]
                )
                for h in range(group)
            ]
            grad_query = jnp.concatenate(parts, axis=0).T * factor
            for ref, place, mask, value in (
                (dq_ref, rows, row_mask, grad_query),
                (dk_ref, cols, col_mask, grad_keys),
                (dv_ref, cols, col_mask, grad_values),
            ):
                old = ref[place, lanes].astype(FULL)
                ref[place, lanes] = jnp.where(mask, value, old).astype(LOW)
        return carry

    lax.fori_loop(0, SEGMENTS, segment, 0)


def normalize(values):
    center = values - jnp.mean(values, axis=-1, keepdims=True)
    inverse = lax.rsqrt(jnp.mean(center * center, axis=-1, keepdims=True) + norm_eps)
    return center * inverse, inverse


def normalize_back(grad, gain, unit, inverse):
    scaled = grad * (1.0 + gain)
    mean = jnp.mean(scaled, axis=-1, keepdims=True)
    along = jnp.mean(scaled * unit, axis=-1, keepdims=True)
    return (scaled - mean - unit * along) * inverse


def column_sum(values):
    return jnp.sum(values.astype(FULL), axis=0, keepdims=True)


STEP_ROWS = 256


def row_steps(total, step):
    def run(i, carry):
        step(pl.ds(pl.multiple_of(i * STEP_ROWS, STEP_ROWS), STEP_ROWS))
        return carry

    lax.fori_loop(0, total // STEP_ROWS, run, 0)


def load_weights(place, depth, sources, targets, semaphores):
    if len(sources) == 1:
        offset = 0
        for target, semaphore in zip(targets, semaphores):
            source = sources[0].at[:, offset : offset + target.shape[1]]
            offset += target.shape[1]
            pltpu.make_async_copy(source, target, semaphore).start()
        return
    half = len(sources) // 2
    for k, source in enumerate(sources):
        base = (k % half) * 2 * depth + k // half
        for layer in range(depth):
            other = place ^ (base + 2 * layer)
            offset = 0
            for target, semaphore in zip(targets, semaphores):
                rows = source.shape[1]
                span = target.shape[1]
                to_rows = pl.ds(pl.multiple_of(other * rows, rows), rows)
                pltpu.make_async_copy(
                    source.at[layer, :, offset : offset + span], target.at[to_rows, :], semaphore
                ).start()
                offset += span


def await_weights(target, semaphore):
    pltpu.make_async_copy(target, target, semaphore).wait()


def store_grad(refs, core, lanes, value):
    value = value.astype(LOW)
    if len(refs) == 1:
        refs[0][:, lanes] = value
        return
    sent, kept = refs
    chips, rows = kept.shape[0], kept.shape[1]
    parts = value.reshape(chips, 2, rows, value.shape[1])
    first = core == 0
    kept[:, :, lanes] = jnp.where(first, parts[:, 0], parts[:, 1])
    sent[:, :, lanes] = jnp.where(first, parts[:, 1], parts[:, 0])


def self_forward_kernel(count, depth, place, row_starts, tokens, *rest):
    sources = rest[:count]
    weights, vectors, queries, keys, values, mixed, sums, semaphores = rest[count:]
    model = tokens.shape[1]
    load_weights(place[0], depth, sources, [weights], [semaphores.at[0]])
    await_weights(weights, semaphores.at[0])
    turned = weights[:, 3 * model : 3 * model + 128].astype(FULL).T
    vectors[...] = turned[: vectors.shape[0]]

    def project(rows):
        block = tokens[rows, :]
        queries[rows, :] = (dot_nn(block, weights[:, :model]) + vectors[0:1, :]).astype(LOW)
        keys[rows, :] = dot_nn(block, weights[:, model : 2 * model]).astype(LOW)
        values[rows, :] = (
            dot_nn(block, weights[:, 2 * model : 3 * model]) + vectors[1:2, :]
        ).astype(LOW)

    row_steps(tokens.shape[0], project)
    attend_forward(row_starts, row_starts, queries, keys, values, mixed, sums)


def cross_forward_kernel(
    count, depth, place, row_starts, col_starts, tokens, encoded, mixed, vectors, *rest
):
    sources = rest[:count]
    (
        weights, unit_one, inverse_one, first_low, queries, keys, values, cross_mixed, sums, semaphores,
    ) = rest[count:]
    model = tokens.shape[1]
    load_weights(place[0], depth, sources, [weights], [semaphores.at[0]])
    await_weights(weights, semaphores.at[0])

    def project(rows):
        block = encoded[rows, :]
        keys[rows, :] = dot_nn(block, weights[:, 2 * model : 3 * model]).astype(LOW)
        values[rows, :] = (
            dot_nn(block, weights[:, 3 * model : 4 * model]) + vectors[4:5, :]
        ).astype(LOW)
        summed = tokens[rows, :].astype(FULL) + dot_nn(mixed[rows, :], weights[:, :model])
        unit, inverse = normalize(summed + vectors[2:3, :])
        unit_one[rows, :] = unit
        inverse_one[rows, :] = inverse
        low = (unit * (1.0 + vectors[7:8, :]) + vectors[10:11, :]).astype(LOW)
        first_low[rows, :] = low
        queries[rows, :] = (dot_nn(low, weights[:, model : 2 * model]) + vectors[3:4, :]).astype(LOW)

    row_steps(tokens.shape[0], project)
    attend_forward(row_starts, col_starts, queries, keys, values, cross_mixed, sums)


def cross_finish_kernel(unit_one, cross_mixed, weights, vectors, unit_two, inverse_two):
    first = unit_one[...] * (1.0 + vectors[7:8, :]) + vectors[10:11, :]
    summed = first + dot_nn(cross_mixed[...], weights[...]) + vectors[5:6, :]
    unit, inverse = normalize(summed)
    unit_two[...] = unit
    inverse_two[...] = inverse


gelu_scale = math.sqrt(2.0 / math.pi)
gelu_cubic = 0.044715


def ffn_kernel(count, depth, place, unit_two, inverse_two, cotangent, cross_out, vectors, *rest):
    sources = rest[:count]
    (
        layer_out, grad_sum, grad_out, grad_mixed, sums, bias_sums, *grads,
        first_weights, second_weights, second_low, hidden, grad_ffn, grad_pre, slopes, semaphores,
    ) = rest[count:]
    step = pl.program_id(0)
    model = unit_two.shape[1]
    pieces = first_weights.shape[1] // model
    rows = pl.ds(pl.multiple_of(step * STEP_ROWS, STEP_ROWS), STEP_ROWS)

    @pl.when(step == 0)
    def _():
        sums[...] = jnp.zeros_like(sums)
        bias_sums[...] = jnp.zeros_like(bias_sums)
        load_ffn(place[0], depth, sources, first_weights, second_weights, semaphores)
        await_weights(first_weights, semaphores.at[0])
        await_weights(second_weights, semaphores.at[1])

    unit = unit_two[...]
    second = unit * (1.0 + vectors[8:9, :]) + vectors[11:12, :]
    low = second.astype(LOW)
    second_low[rows, :] = low
    total = second + vectors[6:7, :]
    for j in range(pieces):
        lanes = slice(j * model, (j + 1) * model)
        pre = dot_nn(low, first_weights[:, lanes]) + vectors[13 + j : 14 + j, :]
        square = pre * pre
        bend = jnp.tanh(gelu_scale * pre * (1.0 + gelu_cubic * square))
        half = 0.5 * (1.0 + bend)
        value = (pre * half).astype(LOW)
        hidden[rows, lanes] = value
        inner = gelu_scale * (1.0 + 3.0 * gelu_cubic * square)
        slopes[:, lanes] = half + 0.5 * pre * (1.0 - bend * bend) * inner
        total = total + dot_nn(value, second_weights[lanes, :])
    unit_three, inverse_three = normalize(total)
    layer_out[...] = (unit_three * (1.0 + vectors[9:10, :]) + vectors[12:13, :]).astype(LOW)
    upper = cotangent[...].astype(FULL)
    third = normalize_back(upper, vectors[9:10, :], unit_three, inverse_three)
    third_low = third.astype(LOW)
    grad_ffn[rows, :] = third_low
    sums[0:1, :] += column_sum(third_low)
    sums[1:2, :] += column_sum(upper * unit_three)
    sums[2:3, :] += column_sum(upper)
    below = third
    for j in range(pieces):
        lanes = slice(j * model, (j + 1) * model)
        pre = (dot_nt(third_low, second_weights[lanes, :]) * slopes[:, lanes]).astype(LOW)
        grad_pre[rows, lanes] = pre
        bias_sums[j : j + 1, :] += column_sum(pre)
        below = below + dot_nt(pre, first_weights[:, lanes])
    sums[3:4, :] += column_sum(below * unit)
    sums[4:5, :] += column_sum(below)
    second_sum = normalize_back(below, vectors[8:9, :], unit, inverse_two[...])
    grad_sum[...] = second_sum
    out_low = second_sum.astype(LOW)
    grad_out[...] = out_low
    sums[5:6, :] += column_sum(out_low)
    grad_mixed[...] = dot_nt(out_low, cross_out[...]).astype(LOW)

    @pl.when(step == pl.num_programs(0) - 1)
    def _():
        core = place[0] % 2
        for j in range(pieces):
            lanes = slice(j * model, (j + 1) * model)
            store_grad(grads, core, lanes, dot_tn(second_low[...], grad_pre[:, lanes]))
        span = second_weights.shape[0] // pieces
        for j in range(pieces):
            value = dot_tn(hidden[:, j * span : (j + 1) * span], grad_ffn[...])
            store_ffn_out(grads, core, j, pieces, value)


def load_ffn(place, depth, sources, first_weights, second_weights, semaphores):
    first_width = first_weights.shape[1]
    if len(sources) == 1:
        pltpu.make_async_copy(
            sources[0].at[:, :first_width], first_weights, semaphores.at[0]
        ).start()
        pieces = first_width // first_weights.shape[0]
        model = first_weights.shape[0]
        for j in range(pieces):
            pltpu.make_async_copy(
                sources[0].at[:, first_width + j * model : first_width + (j + 1) * model],
                second_weights.at[pl.ds(j * model, model), :],
                semaphores.at[1],
            ).start()
        return
    half = len(sources) // 2
    model = second_weights.shape[1]
    for k, source in enumerate(sources):
        base = (k % half) * 2 * depth + k // half
        rows = source.shape[1]
        for layer in range(depth):
            other = place ^ (base + 2 * layer)
            to_rows = pl.ds(pl.multiple_of(other * rows, rows), rows)
            pltpu.make_async_copy(
                source.at[layer, :, :first_width], first_weights.at[to_rows, :], semaphores.at[0]
            ).start()
            pieces = first_width // model
            for j in range(pieces):
                start = pl.multiple_of((other * pieces + j) * rows, rows)
                pltpu.make_async_copy(
                    source.at[layer, :, first_width + j * model : first_width + (j + 1) * model],
                    second_weights.at[pl.ds(start, rows), :],
                    semaphores.at[1],
                ).start()


def store_ffn_out(refs, core, block, pieces, value):
    value = value.astype(LOW)
    model = value.shape[1]
    if len(refs) == 1:
        offset = (pieces + block) * model
        refs[0][:, offset : offset + model] = value
        return
    sent, kept = refs
    rows = kept.shape[1]
    chips = kept.shape[0] // pieces
    parts = value.reshape(chips, 2, pieces, rows, model)
    first = core == 0
    for j in range(pieces):
        lanes = slice((pieces + j) * model, (pieces + j + 1) * model)
        place = slice(block * chips, (block + 1) * chips)
        kept[place, :, lanes] = jnp.where(first, parts[:, 0, j], parts[:, 1, j])
        sent[place, :, lanes] = jnp.where(first, parts[:, 1, j], parts[:, 0, j])


def cross_backward_kernel(
    row_starts, col_starts, queries, keys, values, grad_mixed, sums_in, dq, dk, dv
):
    attend_backward(row_starts, col_starts, queries, keys, values, grad_mixed, sums_in, dq, dk, dv)


def cross_grads_kernel(
    place, dq, dk, dv, weights, vectors, grad_sum, unit_one, inverse_one,
    first_low, encoded, cross_mixed, grad_out, first_sum, self_low, grad_mixed, sums, *grads,
):
    model = dq.shape[1]
    sums[...] = jnp.zeros_like(sums)

    def finish(rows):
        query, value = dq[rows, :], dv[rows, :]
        sums[0:1, :] += column_sum(query)
        sums[1:2, :] += column_sum(value)
        upper = grad_sum[rows, :] + dot_nt(query, weights[:, model : 2 * model])
        unit = unit_one[rows, :]
        sums[2:3, :] += column_sum(upper * unit)
        sums[3:4, :] += column_sum(upper)
        below = normalize_back(upper, vectors[7:8, :], unit, inverse_one[rows, :])
        first_sum[rows, :] = below
        low = below.astype(LOW)
        self_low[rows, :] = low
        sums[4:5, :] += column_sum(low)
        grad_mixed[rows, :] = dot_nt(low, weights[:, :model]).astype(LOW)

    row_steps(dq.shape[0], finish)
    core = place[0] % 2
    pairs = ((first_low, dq), (encoded, dk), (encoded, dv), (cross_mixed, grad_out))
    for j, (left, right) in enumerate(pairs):
        lanes = slice(j * model, (j + 1) * model)
        store_grad(grads, core, lanes, dot_tn(left[...], right[...]))


def encoded_grad_kernel(dk, dv, key_weights, value_weights, encoded_grad):
    encoded_grad[...] = dot_nt(dk[...], key_weights[...]) + dot_nt(dv[...], value_weights[...])


def self_backward_kernel(row_starts, queries, keys, values, grad_mixed, sums_in, dq, dk, dv):
    attend_backward(row_starts, row_starts, queries, keys, values, grad_mixed, sums_in, dq, dk, dv)


def self_grads_kernel(
    place, tokens, mixed, dq, dk, dv, self_low, cross_sums, ffn_sums, bias_sums, *rest
):
    *grads, stack = rest
    model = dq.shape[1]
    core = place[0] % 2
    pairs = ((tokens, dq), (tokens, dk), (tokens, dv), (mixed, self_low))
    for j, (left, right) in enumerate(pairs):
        lanes = slice(j * model, (j + 1) * model)
        store_grad(grads, core, lanes, dot_tn(left[...], right[...]))
    stack[...] = jnp.zeros_like(stack)
    stack[0:1, :] = column_sum(dq[...])
    stack[1:2, :] = column_sum(dv[...])
    order = (
        (2, cross_sums, 4), (3, cross_sums, 0), (4, cross_sums, 1), (5, ffn_sums, 5),
        (6, ffn_sums, 0), (7, cross_sums, 2), (8, ffn_sums, 3), (9, ffn_sums, 1),
        (10, cross_sums, 3), (11, ffn_sums, 4), (12, ffn_sums, 2),
    )
    for to, ref, at in order:
        stack[to : to + 1, :] = ref[at : at + 1, :]
    extra = bias_sums.shape[0]
    stack[13 : 13 + extra, :] = bias_sums[...]
    start = len(pairs) * model
    store_grad(grads, core, slice(start, start + 128), stack[...].T)


def tokens_grad_kernel(dq, dk, dv, first_sum, weights, tokens_grad):
    model = dq.shape[1]
    below = first_sum[...] + dot_nt(dq[...], weights[:, :model])
    below = below + dot_nt(dk[...], weights[:, model : 2 * model])
    tokens_grad[...] = below + dot_nt(dv[...], weights[:, 2 * model : 3 * model])


PARAMS = pltpu.CompilerParams(vmem_limit_bytes=58 << 20)
ANY = pl.BlockSpec(memory_space=pl.ANY)


def call(kernel, name, scalars, arrays, outs, flops, sources=(), scratch=()):
    specs = [pl.BlockSpec(memory_space=pltpu.SMEM)] * len(scalars)
    specs += [pl.BlockSpec(memory_space=pltpu.VMEM)] * len(arrays)
    specs += [ANY] * len(sources)
    shapes = [jax.ShapeDtypeStruct(*item) for item in outs]
    moved = sum(item.size * item.dtype.itemsize for item in [*arrays, *sources, *shapes])
    return pl.pallas_call(
        kernel,
        out_shape=shapes,
        in_specs=specs,
        out_specs=[pl.BlockSpec(memory_space=pltpu.VMEM)] * len(outs),
        scratch_shapes=list(scratch),
        compiler_params=PARAMS,
        cost_estimate=pl.CostEstimate(flops=flops, transcendentals=0, bytes_accessed=moved),
        name=name,
    )(*scalars, *arrays, *sources)


def blocked(kernel, name, arrays, fixed, outs, flops, scalars=(), sources=(), fixed_outs=(), scratch=()):
    total = arrays[0].shape[0]
    specs = [pl.BlockSpec(memory_space=pltpu.SMEM)] * len(scalars)
    specs += [pl.BlockSpec((STEP_ROWS, item.shape[1]), lambda i: (i, 0)) for item in arrays]
    for item, shape, index in fixed:
        specs.append(pl.BlockSpec(shape, lambda i, index=index: index))
    specs += [ANY] * len(sources)
    shapes = [jax.ShapeDtypeStruct(*item) for item in [*outs, *fixed_outs]]
    out_specs = [pl.BlockSpec((STEP_ROWS, item[0][1]), lambda i: (i, 0)) for item in outs]
    for item in fixed_outs:
        out_specs.append(pl.BlockSpec(item[0], lambda i, size=len(item[0]): (0,) * size))
    inputs = [*arrays, *[item[0] for item in fixed]]
    moved = sum(item.size * item.dtype.itemsize for item in [*arrays, *sources, *shapes])
    return pl.pallas_call(
        kernel,
        grid=(total // STEP_ROWS,),
        out_shape=shapes,
        in_specs=specs,
        out_specs=out_specs,
        scratch_shapes=list(scratch),
        compiler_params=PARAMS,
        cost_estimate=pl.CostEstimate(flops=flops, transcendentals=0, bytes_accessed=moved),
        name=name,
    )(*scalars, *inputs, *sources)


def segment_starts(ids):
    marks = jnp.arange(SEGMENTS + 1, dtype=ids.dtype)
    return jnp.sum((ids[None, :] < marks[:, None]).astype(jnp.int32), axis=1)


def adamw(master, grad, first, second, rate):
    first_new = beta_first * first + (1.0 - beta_first) * grad
    second_new = beta_second * second + (1.0 - beta_second) * grad * grad
    first_hat = first_new / (1.0 - beta_first**STEP)
    second_hat = second_new / (1.0 - beta_second**STEP)
    master_new = master - rate * (
        first_hat / (jnp.sqrt(second_hat) + adam_eps) + weight_decay * master
    )
    return (first_new, second_new, master_new, master_new.astype(jnp.bfloat16))


AXES = ("dp", "fsdp")


def exchange(values, offset):
    count = lax.axis_size("dp") * lax.axis_size("fsdp")
    return lax.ppermute(values, AXES, [(i, i ^ offset) for i in range(count)])


def after(value, *others):
    return lax.optimization_barrier((value, *others))[0]


def layer_stack(piece):
    depth = lax.axis_size("fsdp") // 2
    return jnp.stack([piece] + [exchange(piece, 2 * k) for k in range(1, depth)])


def square_list(stack):
    dp_count, fsdp_count = lax.axis_size("dp"), lax.axis_size("fsdp")
    return [stack] + [exchange(stack, fsdp_count * k) for k in range(1, dp_count)]


def core_list(near):
    return near + [exchange(item, 1) for item in near]


def ordered(parts, place):
    half = len(parts) // 2
    both = jnp.stack([jnp.stack(parts[:half]), jnp.stack(parts[half:])], axis=2)
    flat = both.reshape((-1,) + both.shape[3:])
    return flat[jnp.arange(flat.shape[0]) ^ place]


def pick(values, index, axis):
    return lax.dynamic_index_in_dim(values, index, axis, keepdims=False)


def split_core(grads):
    if len(grads) == 2:
        return grads
    dp_count, fsdp_count = lax.axis_size("dp"), lax.axis_size("fsdp")
    count = dp_count * fsdp_count
    core = lax.axis_index("fsdp") % 2
    parts = grads[0].reshape((count // 2, 2, -1) + grads[0].shape[1:])
    return pick(parts, 1 - core, 1), pick(parts, core, 1)


def sum_core(kept, received):
    dp_count = lax.axis_size("dp")
    shape = (dp_count, kept.shape[0] // dp_count) + kept.shape[1:]
    return kept.reshape(shape).astype(FULL) + received.reshape(shape).astype(FULL)


def sum_square(pair):
    dp_count, fsdp_count = lax.axis_size("dp"), lax.axis_size("fsdp")
    place = lax.axis_index("dp")
    moved = [
        exchange(pick(pair, place ^ k, 0).astype(LOW), fsdp_count * k) for k in range(1, dp_count)
    ]
    return pick(pair, place, 0), moved


def sum_layers(square):
    depth = lax.axis_size("fsdp") // 2
    place = lax.axis_index("fsdp") // 2
    moved = [exchange(pick(square, place ^ k, 0).astype(LOW), 2 * k) for k in range(1, depth)]
    return pick(square, place, 0), moved


def add_all(kept, moved):
    for item in moved:
        kept = kept + item.astype(FULL)
    return kept


def body(
    tokens,
    encoded,
    cotangent,
    target_ids,
    source_ids,
    qkv_master,
    qkv_first,
    qkv_second,
    out_master,
    out_first,
    out_second,
    ffn_in_master,
    ffn_in_first,
    ffn_in_second,
    ffn_out_master,
    ffn_out_first,
    ffn_out_second,
    vector_master,
    vector_first,
    vector_second,
):
    total, model = tokens.shape
    dp_count, fsdp_count = lax.axis_size("dp"), lax.axis_size("fsdp")
    count, depth = dp_count * fsdp_count, fsdp_count // 2
    rows = model // count
    aligned = rows % 16 == 0
    place = lax.axis_index("dp") * fsdp_count + lax.axis_index("fsdp")
    spot = place.reshape(1).astype(jnp.int32)
    low_qkv, low_out = qkv_master.astype(LOW), out_master.astype(LOW)
    low_vector = jnp.pad(vector_master.astype(LOW).T, ((0, 0), (0, 128 - vector_master.shape[0])))
    pieces = ffn_in_master.shape[1] // model

    def to_columns(values):
        return values.reshape(-1, rows, model).transpose(1, 0, 2).reshape(rows, -1)

    self_piece = jnp.concatenate([low_qkv[0], low_qkv[1], low_qkv[2], low_vector], axis=1)
    cross_piece = jnp.concatenate([low_out[0], low_qkv[3], low_qkv[4], low_qkv[5], low_out[1]], axis=1)
    ffn_piece = jnp.concatenate(
        [ffn_in_master.astype(LOW), to_columns(ffn_out_master.astype(LOW))], axis=1
    )
    row_starts, col_starts = segment_starts(target_ids[0]), segment_starts(source_ids[0])

    def sources_of(parts):
        if aligned:
            return parts
        flat = ordered(parts, place)
        return [flat.reshape(model, -1)]

    def ffn_sources_of(parts):
        if aligned:
            return parts
        flat = ordered(parts, place)
        width = pieces * model
        second = flat[:, :, width:].reshape(count, rows, pieces, model).transpose(0, 2, 1, 3)
        second = second.reshape(pieces, model, model).transpose(1, 0, 2).reshape(model, -1)
        return [jnp.concatenate([flat[:, :, :width].reshape(model, -1), second], axis=1)]

    wide, tall, thin = ((total, model), LOW), ((total, model), FULL), ((total, 1), FULL)
    log_sums = ((SEGMENTS, model // 256, 1, 1024), FULL)
    small = ((8, model), FULL)
    unit = 2 * total * model * model
    attend = 2 * SEGMENTS * HEADS * 256 * 256 * 256
    wait_one, wait_two = pltpu.SemaphoreType.DMA((1,)), pltpu.SemaphoreType.DMA((2,))

    def grad_outs(columns):
        if aligned:
            return [((count // 2, rows, columns), LOW)] * 2
        return [((model, columns), LOW)]

    self_stack = layer_stack(self_piece)
    later = after(jnp.concatenate([cross_piece, ffn_piece], axis=1), self_stack)
    self_near = square_list(self_stack)
    later_stack = layer_stack(later)
    self_parts = core_list(self_near)
    cross_columns = cross_piece.shape[1]
    cross_near = square_list(later_stack[:, :, :cross_columns])
    ffn_near = square_list(later_stack[:, :, cross_columns:])

    sources = sources_of(self_parts)
    (
        self_weights, vectors, queries, keys, values, mixed, self_sums,
    ) = call(
        functools.partial(self_forward_kernel, len(sources), depth), "self_forward",
        [spot, row_starts], [after(tokens, later_stack)],
        [((model, self_piece.shape[1]), LOW), ((24, model), FULL), wide, wide, wide, wide, log_sums],
        3 * unit + 2 * attend, sources, [wait_one],
    )
    sources = sources_of(core_list(cross_near))
    (
        cross_weights, unit_one, inverse_one, first_low, cross_queries, cross_keys, cross_values,
        cross_mixed, cross_log,
    ) = call(
        functools.partial(cross_forward_kernel, len(sources), depth), "cross_forward",
        [spot, row_starts, col_starts], [tokens, encoded, mixed, vectors],
        [((model, cross_columns), LOW), tall, thin, wide, wide, wide, wide, wide, log_sums],
        4 * unit + 2 * attend, sources, [wait_one],
    )

    def weight_block(weights, index):
        return (weights, (model, model), (0, index))

    whole_vectors = (vectors, vectors.shape, (0, 0))
    unit_two, inverse_two = blocked(
        cross_finish_kernel, "cross_finish", [unit_one, cross_mixed],
        [weight_block(cross_weights, 4), whole_vectors], [tall, thin], unit,
    )
    sources = ffn_sources_of(core_list(ffn_near))
    hidden = pieces * model
    (
        layer_out, grad_sum, grad_cross_out, grad_cross_mixed, ffn_sums, bias_sums, *ffn_grads
    ) = blocked(
        functools.partial(ffn_kernel, len(sources), depth), "ffn",
        [unit_two, inverse_two, cotangent], [weight_block(cross_weights, 4), whole_vectors],
        [wide, tall, wide, wide], (5 * pieces + 1) * unit, [spot], sources,
        [small, small, *grad_outs(2 * hidden)],
        [
            pltpu.VMEM((model, hidden), LOW), pltpu.VMEM((hidden, model), LOW),
            pltpu.VMEM((total, model), LOW), pltpu.VMEM((total, hidden), LOW),
            pltpu.VMEM((total, model), LOW), pltpu.VMEM((total, hidden), LOW),
            pltpu.VMEM((STEP_ROWS, hidden), FULL), wait_two,
        ],
    )
    if not aligned:
        first, second = ffn_grads[0][:, :hidden], ffn_grads[0][:, hidden:]
        second = second.reshape(model, pieces, model).transpose(1, 0, 2)
        second = second.reshape(count, pieces, rows, model).transpose(0, 2, 1, 3)
        ffn_grads = [jnp.concatenate([first, second.reshape(model, -1)], axis=1)]
    sent, kept = split_core(ffn_grads)
    ffn_moved = exchange(sent, 1)
    cross_dq, cross_dk, cross_dv = call(
        cross_backward_kernel, "cross_backward", [row_starts, col_starts],
        [cross_queries, cross_keys, cross_values, grad_cross_mixed, cross_log],
        [wide, wide, wide], 5 * attend,
    )
    ffn_kept, ffn_moved = sum_square(sum_core(kept, after(ffn_moved, cross_dq)))
    first_sum, self_low, grad_mixed, cross_vector, *cross_grads = call(
        cross_grads_kernel, "cross_grads", [spot],
        [
            cross_dq, cross_dk, cross_dv, cross_weights, vectors, grad_sum, unit_one, inverse_one,
            first_low, encoded, cross_mixed, grad_cross_out,
        ],
        [tall, wide, wide, small, *grad_outs(4 * model)], 6 * unit,
    )
    sent, kept = split_core(cross_grads)
    cross_moved = exchange(sent, 1)
    (encoded_grad,) = blocked(
        encoded_grad_kernel, "encoded_grad", [after(cross_dk, sent), cross_dv],
        [weight_block(cross_weights, 2), weight_block(cross_weights, 3)], [tall], 2 * unit,
    )
    cross_kept, cross_moved = sum_square(sum_core(kept, after(cross_moved, encoded_grad)))
    grad_mixed = after(grad_mixed, encoded_grad, cross_kept)
    self_dq, self_dk, self_dv = call(
        self_backward_kernel, "self_backward", [row_starts],
        [queries, keys, values, grad_mixed, self_sums], [wide, wide, wide], 5 * attend,
    )
    ffn_kept, ffn_moved = sum_layers(add_all(ffn_kept, ffn_moved))
    self_grads = call(
        self_grads_kernel, "self_grads", [spot],
        [tokens, mixed, self_dq, self_dk, self_dv, self_low, cross_vector, ffn_sums, bias_sums],
        grad_outs(4 * model + 128), 4 * unit, (), [pltpu.VMEM((128, model), FULL)],
    )
    sent, kept = split_core(self_grads)
    self_moved = exchange(sent, 1)
    (tokens_grad,) = blocked(
        tokens_grad_kernel, "tokens_grad", [after(self_dq, sent), self_dk, self_dv, first_sum],
        [(self_weights, self_weights.shape, (0, 0))], [tall], 3 * unit,
    )
    self_kept, self_moved = sum_square(sum_core(kept, after(self_moved, tokens_grad)))
    cross_kept, cross_moved = sum_layers(add_all(cross_kept, cross_moved))
    ffn_total = add_all(ffn_kept, ffn_moved)
    cross_total = add_all(cross_kept, cross_moved)
    self_kept, self_moved = sum_layers(add_all(self_kept, self_moved))
    self_total = add_all(self_kept, self_moved)

    def block(values, index):
        return values[:, index * model : (index + 1) * model]

    summed_qkv = jnp.stack(
        [block(self_total, i) for i in range(3)] + [block(cross_total, i) for i in range(3)]
    )
    summed_out = jnp.stack([block(self_total, 3), block(cross_total, 3)])
    summed_ffn_in = ffn_total[:, :hidden]
    summed_ffn_out = (
        ffn_total[:, hidden:].reshape(rows, pieces, model).transpose(1, 0, 2).reshape(-1, model)
    )
    summed_vector = self_total[:, 4 * model : 4 * model + vector_master.shape[0]].T
    grad_scale = 1.0 / math.sqrt(total * count)
    qkv_first_new, qkv_second_new, qkv_master_new, qkv_copy = adamw(
        qkv_master, summed_qkv * grad_scale, qkv_first, qkv_second, 0.04
    )
    out_first_new, out_second_new, out_master_new, out_copy = adamw(
        out_master, summed_out * grad_scale, out_first, out_second, 0.3
    )
    ffn_in_first_new, ffn_in_second_new, ffn_in_master_new, ffn_in_copy = adamw(
        ffn_in_master, summed_ffn_in * grad_scale, ffn_in_first, ffn_in_second, 0.04
    )
    ffn_out_first_new, ffn_out_second_new, ffn_out_master_new, ffn_out_copy = adamw(
        ffn_out_master, summed_ffn_out * grad_scale, ffn_out_first, ffn_out_second, 0.02
    )
    vector_first_new, vector_second_new, vector_master_new, vector_copy = adamw(
        vector_master, summed_vector * grad_scale, vector_first, vector_second, 0.35
    )
    return (
        layer_out,
        tokens_grad,
        encoded_grad,
        qkv_first_new,
        qkv_second_new,
        qkv_master_new,
        qkv_copy,
        out_first_new,
        out_second_new,
        out_master_new,
        out_copy,
        ffn_in_first_new,
        ffn_in_second_new,
        ffn_in_master_new,
        ffn_in_copy,
        ffn_out_first_new,
        ffn_out_second_new,
        ffn_out_master_new,
        ffn_out_copy,
        vector_first_new,
        vector_second_new,
        vector_master_new,
        vector_copy,
    )


def solution(mesh):
    return jax.shard_map(
        body,
        mesh=mesh,
        in_specs=(
            P(("dp", "fsdp"), None),
            P(("dp", "fsdp"), None),
            P(("dp", "fsdp"), None),
            P(("dp", "fsdp"), None),
            P(("dp", "fsdp"), None),
            P(None, ("dp", "fsdp"), None),
            P(None, ("dp", "fsdp"), None),
            P(None, ("dp", "fsdp"), None),
            P(None, ("dp", "fsdp"), None),
            P(None, ("dp", "fsdp"), None),
            P(None, ("dp", "fsdp"), None),
            P(("dp", "fsdp"), None),
            P(("dp", "fsdp"), None),
            P(("dp", "fsdp"), None),
            P(("dp", "fsdp"), None),
            P(("dp", "fsdp"), None),
            P(("dp", "fsdp"), None),
            P(None, ("dp", "fsdp")),
            P(None, ("dp", "fsdp")),
            P(None, ("dp", "fsdp")),
        ),
        out_specs=(
            P(("dp", "fsdp"), None),
            P(("dp", "fsdp"), None),
            P(("dp", "fsdp"), None),
            P(None, ("dp", "fsdp"), None),
            P(None, ("dp", "fsdp"), None),
            P(None, ("dp", "fsdp"), None),
            P(None, ("dp", "fsdp"), None),
            P(None, ("dp", "fsdp"), None),
            P(None, ("dp", "fsdp"), None),
            P(None, ("dp", "fsdp"), None),
            P(None, ("dp", "fsdp"), None),
            P(("dp", "fsdp"), None),
            P(("dp", "fsdp"), None),
            P(("dp", "fsdp"), None),
            P(("dp", "fsdp"), None),
            P(("dp", "fsdp"), None),
            P(("dp", "fsdp"), None),
            P(("dp", "fsdp"), None),
            P(("dp", "fsdp"), None),
            P(None, ("dp", "fsdp")),
            P(None, ("dp", "fsdp")),
            P(None, ("dp", "fsdp")),
            P(None, ("dp", "fsdp")),
        ),
        check_vma=False,
    )
```

```python
import functools
import math

import jax
import jax.numpy as jnp
from jax import lax
from jax.experimental import pallas as pl
from jax.experimental.pallas import tpu as pltpu
from jax.sharding import PartitionSpec as P

HEADS = 8
STEP = 5
SEGMENTS = 10
norm_eps = 1e-05
beta_first = 0.5
beta_second = 0.5
adam_eps = 1e-08
weight_decay = 0.01
mask_fill = -1000000000.0
LOW = jnp.bfloat16
FULL = jnp.float32


def dot_nn(left, right):
    return lax.dot_general(left, right, (((1,), (0,)), ((), ())), preferred_element_type=FULL)


def dot_nt(left, right):
    return lax.dot_general(left, right, (((1,), (1,)), ((), ())), preferred_element_type=FULL)


def dot_tn(left, right):
    return lax.dot_general(left, right, (((0,), (0,)), ((), ())), preferred_element_type=FULL)


def head_masks(width, group, factor):
    lane = lax.broadcasted_iota(jnp.int32, (1, group * width), 1) // width
    return [jnp.where(lane == h, factor, 0.0).astype(LOW) for h in range(group)]


def window(start, size, total):
    return pl.multiple_of(jnp.minimum(start // 16 * 16, total - size), 16)


def inside(base, size, begin, end):
    place = lax.broadcasted_iota(jnp.int32, (size, 1), 0) + base
    return (place >= begin) & (place < end)


def each_span(row_starts, col_starts, total, same, work):
    def segment(s, carry):
        row_begin, row_end = row_starts[s], row_starts[s + 1]
        col_begin, col_end = col_starts[s], col_starts[s + 1]
        row_short = row_end - window(row_begin, 128, total) <= 128
        col_short = col_end - window(col_begin, 128, total) <= 128
        for row_span in (128, 256):
            for col_span in (128, 256):
                if same and row_span != col_span:
                    continue
                wanted = row_short if row_span == 128 else jnp.logical_not(row_short)
                if not same:
                    other = col_short if col_span == 128 else jnp.logical_not(col_short)
                    wanted = jnp.logical_and(wanted, other)

                @pl.when(wanted)
                def _(row_span=row_span, col_span=col_span):
                    row_base = window(row_begin, row_span, total)
                    col_base = window(col_begin, col_span, total)
                    work(
                        s,
                        pl.ds(row_base, row_span),
                        pl.ds(col_base, col_span),
                        inside(row_base, row_span, row_begin, row_end),
                        inside(col_base, col_span, col_begin, col_end),
                        row_span,
                    )

        return carry

    lax.fori_loop(0, SEGMENTS, segment, 0)


def attend_forward(row_starts, col_starts, q_ref, k_ref, v_ref, out_ref, sums_ref):
    total, model = q_ref.shape
    width = model // HEADS
    group = 256 // width
    scales = head_masks(width, group, 1.0 / math.sqrt(width))
    parts = [slice(g * 256, (g + 1) * 256) for g in range(HEADS // group)]

    def work(s, rows, cols, row_mask, col_mask, span):
        raw = []
        for lanes in parts:
            query, keys = q_ref[rows, lanes], k_ref[cols, lanes]
            stacked = jnp.concatenate([query * scale for scale in scales], axis=0)
            raw.append(dot_nt(keys, stacked))
        turned = [v_ref[cols, lanes].T for lanes in parts]
        probs = []
        for g, item in enumerate(raw):
            scores = jnp.where(col_mask, item, mask_fill)
            largest = jnp.max(scores, axis=0, keepdims=True)
            expo = jnp.exp(scores - largest)
            totals = jnp.sum(expo, axis=0, keepdims=True)
            sums_ref[s, g, :, : group * span] = largest + jnp.log(totals)
            probs.append((expo * (1.0 / totals)).astype(LOW))
        mixed = [
            [
                dot_nn(side[h * width : (h + 1) * width], prob[:, h * span : (h + 1) * span])
                for h in range(group)
            ]
            for side, prob in zip(turned, probs)
        ]
        for lanes, items in zip(parts, mixed):
            value = jnp.concatenate(items, axis=0).T
            old = out_ref[rows, lanes].astype(FULL)
            out_ref[rows, lanes] = jnp.where(row_mask, value, old).astype(LOW)

    each_span(row_starts, col_starts, total, row_starts is col_starts, work)


def attend_backward(
    row_starts, col_starts, q_ref, k_ref, v_ref, grad_ref, sums_ref, dq_ref, dk_ref, dv_ref
):
    total, model = q_ref.shape
    width = model // HEADS
    group = 256 // width
    factor = 1.0 / math.sqrt(width)
    scales = head_masks(width, group, factor)
    picks = head_masks(width, group, 1.0)
    parts = [slice(g * 256, (g + 1) * 256) for g in range(HEADS // group)]

    def work(s, rows, cols, row_mask, col_mask, span):
        stacks, grads, raw, grad_probs = [], [], [], []
        for lanes in parts:
            query, keys, values = q_ref[rows, lanes], k_ref[cols, lanes], v_ref[cols, lanes]
            grad = jnp.where(row_mask, grad_ref[rows, lanes].astype(FULL), 0.0).astype(LOW)
            stacks.append(jnp.concatenate([query * scale for scale in scales], axis=0))
            grads.append(jnp.concatenate([grad * item for item in picks], axis=0))
            raw.append(dot_nt(keys, stacks[-1]))
            grad_probs.append(dot_nt(values, grads[-1]))
        grad_values, grad_scores = [], []
        for g, (item, grad_prob) in enumerate(zip(raw, grad_probs)):
            scores = jnp.where(col_mask, item, mask_fill)
            probs = jnp.exp(scores - sums_ref[s, g, :, : group * span])
            grad_values.append(dot_nn(probs.astype(LOW), grads[g]))
            weighted = probs * grad_prob
            inner = jnp.sum(weighted, axis=0, keepdims=True)
            grad_scores.append((weighted - probs * inner).astype(LOW))
        grad_keys, grad_queries = [], []
        for lanes, item, stacked in zip(parts, grad_scores, stacks):
            grad_keys.append(dot_nn(item, stacked))
            turned = k_ref[cols, lanes].T
            grad_queries.append(
                [
                    dot_nn(turned[h * width : (h + 1) * width], item[:, h * span : (h + 1) * span])
                    for h in range(group)
                ]
            )
        for g, lanes in enumerate(parts):
            grad_query = jnp.concatenate(grad_queries[g], axis=0).T * factor
            for ref, place, mask, value in (
                (dq_ref, rows, row_mask, grad_query),
                (dk_ref, cols, col_mask, grad_keys[g]),
                (dv_ref, cols, col_mask, grad_values[g]),
            ):
                old = ref[place, lanes].astype(FULL)
                ref[place, lanes] = jnp.where(mask, value, old).astype(LOW)

    each_span(row_starts, col_starts, total, row_starts is col_starts, work)


def normalize(values):
    center = values - jnp.mean(values, axis=-1, keepdims=True)
    inverse = lax.rsqrt(jnp.mean(center * center, axis=-1, keepdims=True) + norm_eps)
    return center * inverse, inverse


def normalize_back(grad, gain, unit, inverse):
    scaled = grad * (1.0 + gain)
    mean = jnp.mean(scaled, axis=-1, keepdims=True)
    along = jnp.mean(scaled * unit, axis=-1, keepdims=True)
    return (scaled - mean - unit * along) * inverse


def column_sum(values):
    return jnp.sum(values.astype(FULL), axis=0, keepdims=True)


STEP_ROWS = 256


def row_steps(total, step):
    def run(i, carry):
        step(pl.ds(pl.multiple_of(i * STEP_ROWS, STEP_ROWS), STEP_ROWS))
        return carry

    lax.fori_loop(0, total // STEP_ROWS, run, 0)


def load_weights(place, depth, sources, targets, semaphores):
    if len(sources) == 1:
        offset = 0
        for target, semaphore in zip(targets, semaphores):
            source = sources[0].at[:, offset : offset + target.shape[1]]
            offset += target.shape[1]
            pltpu.make_async_copy(source, target, semaphore).start()
        return
    half = len(sources) // 2
    for k, source in enumerate(sources):
        base = (k % half) * 2 * depth + k // half
        for layer in range(depth):
            other = place ^ (base + 2 * layer)
            offset = 0
            for target, semaphore in zip(targets, semaphores):
                rows = source.shape[1]
                span = target.shape[1]
                to_rows = pl.ds(pl.multiple_of(other * rows, rows), rows)
                pltpu.make_async_copy(
                    source.at[layer, :, offset : offset + span], target.at[to_rows, :], semaphore
                ).start()
                offset += span


def await_weights(target, semaphore):
    pltpu.make_async_copy(target, target, semaphore).wait()


def store_grad(refs, core, lanes, value):
    value = value.astype(LOW)
    if len(refs) == 1:
        refs[0][:, lanes] = value
        return
    sent, kept = refs
    chips, rows = kept.shape[0], kept.shape[1]
    parts = value.reshape(chips, 2, rows, value.shape[1])
    first = core == 0
    kept[:, :, lanes] = jnp.where(first, parts[:, 0], parts[:, 1])
    sent[:, :, lanes] = jnp.where(first, parts[:, 1], parts[:, 0])


def self_forward_kernel(count, depth, place, row_starts, tokens, *rest):
    sources = rest[:count]
    weights, vectors, queries, keys, values, mixed, sums, semaphores = rest[count:]
    model = tokens.shape[1]
    load_weights(place[0], depth, sources, [weights], [semaphores.at[0]])
    await_weights(weights, semaphores.at[0])
    turned = weights[:, 3 * model : 3 * model + 128].astype(FULL).T
    vectors[...] = turned[: vectors.shape[0]]

    def project(rows):
        block = tokens[rows, :]
        queries[rows, :] = (dot_nn(block, weights[:, :model]) + vectors[0:1, :]).astype(LOW)
        keys[rows, :] = dot_nn(block, weights[:, model : 2 * model]).astype(LOW)
        values[rows, :] = (
            dot_nn(block, weights[:, 2 * model : 3 * model]) + vectors[1:2, :]
        ).astype(LOW)

    row_steps(tokens.shape[0], project)
    attend_forward(row_starts, row_starts, queries, keys, values, mixed, sums)


def cross_forward_kernel(
    count, depth, place, row_starts, col_starts, tokens, encoded, mixed, vectors, *rest
):
    sources = rest[:count]
    (
        weights, unit_one, inverse_one, first_low, queries, keys, values, cross_mixed, sums, semaphores,
    ) = rest[count:]
    model = tokens.shape[1]
    load_weights(place[0], depth, sources, [weights], [semaphores.at[0]])
    await_weights(weights, semaphores.at[0])

    def project(rows):
        block = encoded[rows, :]
        keys[rows, :] = dot_nn(block, weights[:, 2 * model : 3 * model]).astype(LOW)
        values[rows, :] = (
            dot_nn(block, weights[:, 3 * model : 4 * model]) + vectors[4:5, :]
        ).astype(LOW)
        summed = tokens[rows, :].astype(FULL) + dot_nn(mixed[rows, :], weights[:, :model])
        unit, inverse = normalize(summed + vectors[2:3, :])
        unit_one[rows, :] = unit
        inverse_one[rows, :] = inverse
        low = (unit * (1.0 + vectors[7:8, :]) + vectors[10:11, :]).astype(LOW)
        first_low[rows, :] = low
        queries[rows, :] = (dot_nn(low, weights[:, model : 2 * model]) + vectors[3:4, :]).astype(LOW)

    row_steps(tokens.shape[0], project)
    attend_forward(row_starts, col_starts, queries, keys, values, cross_mixed, sums)


def cross_finish_kernel(unit_one, cross_mixed, weights, vectors, unit_two, inverse_two):
    first = unit_one[...] * (1.0 + vectors[7:8, :]) + vectors[10:11, :]
    summed = first + dot_nn(cross_mixed[...], weights[...]) + vectors[5:6, :]
    unit, inverse = normalize(summed)
    unit_two[...] = unit
    inverse_two[...] = inverse


gelu_scale = math.sqrt(2.0 / math.pi)
gelu_cubic = 0.044715


def ffn_kernel(count, depth, place, unit_two, inverse_two, cotangent, cross_out, vectors, *rest):
    sources = rest[:count]
    (
        layer_out, grad_sum, grad_out, grad_mixed, sums, bias_sums, *grads,
        first_weights, second_weights, second_low, hidden, grad_ffn, grad_pre, slopes, semaphores,
    ) = rest[count:]
    step = pl.program_id(0)
    model = unit_two.shape[1]
    pieces = first_weights.shape[1] // model
    rows = pl.ds(pl.multiple_of(step * STEP_ROWS, STEP_ROWS), STEP_ROWS)

    @pl.when(step == 0)
    def _():
        sums[...] = jnp.zeros_like(sums)
        bias_sums[...] = jnp.zeros_like(bias_sums)
        load_ffn(place[0], depth, sources, first_weights, second_weights, semaphores)
        await_weights(first_weights, semaphores.at[0])
        await_weights(second_weights, semaphores.at[1])

    unit = unit_two[...]
    second = unit * (1.0 + vectors[8:9, :]) + vectors[11:12, :]
    low = second.astype(LOW)
    second_low[rows, :] = low
    total = second + vectors[6:7, :]
    for j in range(pieces):
        lanes = slice(j * model, (j + 1) * model)
        pre = dot_nn(low, first_weights[:, lanes]) + vectors[13 + j : 14 + j, :]
        square = pre * pre
        bend = jnp.tanh(gelu_scale * pre * (1.0 + gelu_cubic * square))
        half = 0.5 * (1.0 + bend)
        value = (pre * half).astype(LOW)
        hidden[rows, lanes] = value
        inner = gelu_scale * (1.0 + 3.0 * gelu_cubic * square)
        slopes[:, lanes] = half + 0.5 * pre * (1.0 - bend * bend) * inner
        total = total + dot_nn(value, second_weights[lanes, :])
    unit_three, inverse_three = normalize(total)
    layer_out[...] = (unit_three * (1.0 + vectors[9:10, :]) + vectors[12:13, :]).astype(LOW)
    upper = cotangent[...].astype(FULL)
    third = normalize_back(upper, vectors[9:10, :], unit_three, inverse_three)
    third_low = third.astype(LOW)
    grad_ffn[rows, :] = third_low
    sums[0:1, :] += column_sum(third_low)
    sums[1:2, :] += column_sum(upper * unit_three)
    sums[2:3, :] += column_sum(upper)
    below = third
    for j in range(pieces):
        lanes = slice(j * model, (j + 1) * model)
        pre = (dot_nt(third_low, second_weights[lanes, :]) * slopes[:, lanes]).astype(LOW)
        grad_pre[rows, lanes] = pre
        bias_sums[j : j + 1, :] += column_sum(pre)
        below = below + dot_nt(pre, first_weights[:, lanes])
    sums[3:4, :] += column_sum(below * unit)
    sums[4:5, :] += column_sum(below)
    second_sum = normalize_back(below, vectors[8:9, :], unit, inverse_two[...])
    grad_sum[...] = second_sum
    out_low = second_sum.astype(LOW)
    grad_out[...] = out_low
    sums[5:6, :] += column_sum(out_low)
    grad_mixed[...] = dot_nt(out_low, cross_out[...]).astype(LOW)

    @pl.when(step == pl.num_programs(0) - 1)
    def _():
        core = place[0] % 2
        for j in range(pieces):
            lanes = slice(j * model, (j + 1) * model)
            store_grad(grads, core, lanes, dot_tn(second_low[...], grad_pre[:, lanes]))
        span = second_weights.shape[0] // pieces
        for j in range(pieces):
            value = dot_tn(hidden[:, j * span : (j + 1) * span], grad_ffn[...])
            store_ffn_out(grads, core, j, pieces, value)


def load_ffn(place, depth, sources, first_weights, second_weights, semaphores):
    first_width = first_weights.shape[1]
    if len(sources) == 1:
        pltpu.make_async_copy(
            sources[0].at[:, :first_width], first_weights, semaphores.at[0]
        ).start()
        pieces = first_width // first_weights.shape[0]
        model = first_weights.shape[0]
        for j in range(pieces):
            pltpu.make_async_copy(
                sources[0].at[:, first_width + j * model : first_width + (j + 1) * model],
                second_weights.at[pl.ds(j * model, model), :],
                semaphores.at[1],
            ).start()
        return
    half = len(sources) // 2
    model = second_weights.shape[1]
    for k, source in enumerate(sources):
        base = (k % half) * 2 * depth + k // half
        rows = source.shape[1]
        for layer in range(depth):
            other = place ^ (base + 2 * layer)
            to_rows = pl.ds(pl.multiple_of(other * rows, rows), rows)
            pltpu.make_async_copy(
                source.at[layer, :, :first_width], first_weights.at[to_rows, :], semaphores.at[0]
            ).start()
            pieces = first_width // model
            for j in range(pieces):
                start = pl.multiple_of((other * pieces + j) * rows, rows)
                pltpu.make_async_copy(
                    source.at[layer, :, first_width + j * model : first_width + (j + 1) * model],
                    second_weights.at[pl.ds(start, rows), :],
                    semaphores.at[1],
                ).start()


def store_ffn_out(refs, core, block, pieces, value):
    value = value.astype(LOW)
    model = value.shape[1]
    if len(refs) == 1:
        offset = (pieces + block) * model
        refs[0][:, offset : offset + model] = value
        return
    sent, kept = refs
    rows = kept.shape[1]
    chips = kept.shape[0] // pieces
    parts = value.reshape(chips, 2, pieces, rows, model)
    first = core == 0
    for j in range(pieces):
        lanes = slice((pieces + j) * model, (pieces + j + 1) * model)
        place = slice(block * chips, (block + 1) * chips)
        kept[place, :, lanes] = jnp.where(first, parts[:, 0, j], parts[:, 1, j])
        sent[place, :, lanes] = jnp.where(first, parts[:, 1, j], parts[:, 0, j])


def cross_backward_kernel(
    row_starts, col_starts, queries, keys, values, grad_mixed, sums_in, dq, dk, dv
):
    attend_backward(row_starts, col_starts, queries, keys, values, grad_mixed, sums_in, dq, dk, dv)


def cross_grads_kernel(
    place, dq, dk, dv, weights, vectors, grad_sum, unit_one, inverse_one,
    first_low, encoded, cross_mixed, grad_out, first_sum, self_low, grad_mixed, sums, *grads,
):
    model = dq.shape[1]
    sums[...] = jnp.zeros_like(sums)

    def finish(rows):
        query, value = dq[rows, :], dv[rows, :]
        sums[0:1, :] += column_sum(query)
        sums[1:2, :] += column_sum(value)
        upper = grad_sum[rows, :] + dot_nt(query, weights[:, model : 2 * model])
        unit = unit_one[rows, :]
        sums[2:3, :] += column_sum(upper * unit)
        sums[3:4, :] += column_sum(upper)
        below = normalize_back(upper, vectors[7:8, :], unit, inverse_one[rows, :])
        first_sum[rows, :] = below
        low = below.astype(LOW)
        self_low[rows, :] = low
        sums[4:5, :] += column_sum(low)
        grad_mixed[rows, :] = dot_nt(low, weights[:, :model]).astype(LOW)

    row_steps(dq.shape[0], finish)
    core = place[0] % 2
    pairs = ((first_low, dq), (encoded, dk), (encoded, dv), (cross_mixed, grad_out))
    for j, (left, right) in enumerate(pairs):
        lanes = slice(j * model, (j + 1) * model)
        store_grad(grads, core, lanes, dot_tn(left[...], right[...]))


def encoded_grad_kernel(dk, dv, key_weights, value_weights, encoded_grad):
    encoded_grad[...] = dot_nt(dk[...], key_weights[...]) + dot_nt(dv[...], value_weights[...])


def self_backward_kernel(row_starts, queries, keys, values, grad_mixed, sums_in, dq, dk, dv):
    attend_backward(row_starts, row_starts, queries, keys, values, grad_mixed, sums_in, dq, dk, dv)


def self_grads_kernel(
    place, tokens, mixed, dq, dk, dv, self_low, cross_sums, ffn_sums, bias_sums, *rest
):
    *grads, stack = rest
    model = dq.shape[1]
    core = place[0] % 2
    pairs = ((tokens, dq), (tokens, dk), (tokens, dv), (mixed, self_low))
    for j, (left, right) in enumerate(pairs):
        lanes = slice(j * model, (j + 1) * model)
        store_grad(grads, core, lanes, dot_tn(left[...], right[...]))
    stack[...] = jnp.zeros_like(stack)
    stack[0:1, :] = column_sum(dq[...])
    stack[1:2, :] = column_sum(dv[...])
    order = (
        (2, cross_sums, 4), (3, cross_sums, 0), (4, cross_sums, 1), (5, ffn_sums, 5),
        (6, ffn_sums, 0), (7, cross_sums, 2), (8, ffn_sums, 3), (9, ffn_sums, 1),
        (10, cross_sums, 3), (11, ffn_sums, 4), (12, ffn_sums, 2),
    )
    for to, ref, at in order:
        stack[to : to + 1, :] = ref[at : at + 1, :]
    extra = bias_sums.shape[0]
    stack[13 : 13 + extra, :] = bias_sums[...]
    start = len(pairs) * model
    store_grad(grads, core, slice(start, start + 128), stack[...].T)


def tokens_grad_kernel(dq, dk, dv, first_sum, weights, tokens_grad):
    model = dq.shape[1]
    below = first_sum[...] + dot_nt(dq[...], weights[:, :model])
    below = below + dot_nt(dk[...], weights[:, model : 2 * model])
    tokens_grad[...] = below + dot_nt(dv[...], weights[:, 2 * model : 3 * model])


def fold_core_kernel(shape, place, kept, received, own, *sends):
    dp_count, depth = shape
    at = place[0] // (2 * depth)
    for k, ref in enumerate((own, *sends)):
        spot = pl.ds((at ^ k) * depth, depth)
        value = kept[spot].astype(FULL) + received[spot].astype(FULL)
        ref[...] = value.astype(ref.dtype)


def fold_square_kernel(shape, place, kept, *rest):
    dp_count, depth = shape
    received, outs = rest[: dp_count - 1], rest[dp_count - 1 :]
    at = place[0] // 2 % depth
    for k, ref in enumerate(outs):
        spot = pl.ds(at ^ k, 1)
        value = kept[spot]
        for item in received:
            value = value + item[spot].astype(FULL)
        ref[...] = value[0].astype(ref.dtype)


LIMITS = {
    "fold_core": 12,
    "fold_square": 10,
    "self_forward": 14,
    "cross_forward": 16,
    "cross_finish": 9,
    "ffn": 27,
    "cross_backward": 11,
    "cross_grads": 16,
    "encoded_grad": 9,
    "self_backward": 11,
    "self_grads": 14,
    "tokens_grad": 11,
}


def out_kind(item):
    if len(item) == 3:
        return pltpu.VMEM(item[0], item[1])
    return jax.ShapeDtypeStruct(*item)


def keep(item):
    return (item[0], item[1], True)


def limit(name):
    return pltpu.CompilerParams(vmem_limit_bytes=LIMITS[name] << 20)


def pinned(sources):
    if len(sources) == 1:
        return sources
    return [pltpu.with_memory_space_constraint(item, pltpu.VMEM) for item in sources]


def source_spec(sources):
    return pl.BlockSpec(memory_space=pltpu.VMEM if len(sources) > 1 else pl.ANY)


def call(kernel, name, scalars, arrays, outs, flops, sources=(), scratch=()):
    specs = [pl.BlockSpec(memory_space=pltpu.SMEM)] * len(scalars)
    specs += [pl.BlockSpec(memory_space=pltpu.VMEM)] * len(arrays)
    specs += [source_spec(sources)] * len(sources)
    shapes = [out_kind(item) for item in outs]
    moved = sum(item.size * item.dtype.itemsize for item in [*arrays, *sources])
    return pl.pallas_call(
        kernel,
        out_shape=shapes,
        in_specs=specs,
        out_specs=[pl.BlockSpec(memory_space=pltpu.VMEM)] * len(outs),
        scratch_shapes=list(scratch),
        compiler_params=limit(name),
        cost_estimate=pl.CostEstimate(flops=flops, transcendentals=0, bytes_accessed=moved),
        name=name,
    )(*scalars, *arrays, *pinned(sources))


def blocked(kernel, name, arrays, fixed, outs, flops, scalars=(), sources=(), fixed_outs=(), scratch=()):
    total = arrays[0].shape[0]
    specs = [pl.BlockSpec(memory_space=pltpu.SMEM)] * len(scalars)
    specs += [pl.BlockSpec((STEP_ROWS, item.shape[1]), lambda i: (i, 0)) for item in arrays]
    for item, shape, index in fixed:
        specs.append(
            pl.BlockSpec(shape, lambda i, index=index: index, pipeline_mode=pl.Buffered(1))
        )
    specs += [source_spec(sources)] * len(sources)
    shapes = [out_kind(item) for item in [*outs, *fixed_outs]]
    out_specs = [pl.BlockSpec((STEP_ROWS, item[0][1]), lambda i: (i, 0)) for item in outs]
    for item in fixed_outs:
        index = (0,) * len(item[0])
        out_specs.append(
            pl.BlockSpec(item[0], lambda i, index=index: index, pipeline_mode=pl.Buffered(1))
        )
    inputs = [*arrays, *[item[0] for item in fixed]]
    moved = sum(item.size * item.dtype.itemsize for item in [*arrays, *sources])
    return pl.pallas_call(
        kernel,
        grid=(total // STEP_ROWS,),
        out_shape=shapes,
        in_specs=specs,
        out_specs=out_specs,
        scratch_shapes=list(scratch),
        compiler_params=limit(name),
        cost_estimate=pl.CostEstimate(flops=flops, transcendentals=0, bytes_accessed=moved),
        name=name,
    )(*scalars, *inputs, *pinned(sources))


def segment_starts(ids):
    marks = jnp.arange(SEGMENTS + 1, dtype=ids.dtype)
    return jnp.sum((ids[None, :] < marks[:, None]).astype(jnp.int32), axis=1)


def adamw(master, grad, first, second, rate):
    first_new = beta_first * first + (1.0 - beta_first) * grad
    second_new = beta_second * second + (1.0 - beta_second) * grad * grad
    first_hat = first_new / (1.0 - beta_first**STEP)
    second_hat = second_new / (1.0 - beta_second**STEP)
    master_new = master - rate * (
        first_hat / (jnp.sqrt(second_hat) + adam_eps) + weight_decay * master
    )
    return (first_new, second_new, master_new, master_new.astype(jnp.bfloat16))


AXES = ("dp", "fsdp")


def exchange(values, offset):
    count = lax.axis_size("dp") * lax.axis_size("fsdp")
    return lax.ppermute(values, AXES, [(i, i ^ offset) for i in range(count)])


def after(value, *others):
    return lax.optimization_barrier((value, *others))[0]


def layer_stack(piece):
    depth = lax.axis_size("fsdp") // 2
    return jnp.stack([piece] + [exchange(piece, 2 * k) for k in range(1, depth)])


def square_list(stack):
    dp_count, fsdp_count = lax.axis_size("dp"), lax.axis_size("fsdp")
    return [stack] + [exchange(stack, fsdp_count * k) for k in range(1, dp_count)]


def core_list(near):
    return near + [exchange(item, 1) for item in near]


def ordered(parts, place):
    half = len(parts) // 2
    both = jnp.stack([jnp.stack(parts[:half]), jnp.stack(parts[half:])], axis=2)
    flat = both.reshape((-1,) + both.shape[3:])
    return flat[jnp.arange(flat.shape[0]) ^ place]


def pick(values, index, axis):
    return lax.dynamic_index_in_dim(values, index, axis, keepdims=False)


def split_core(grads):
    if len(grads) == 2:
        return grads
    count = lax.axis_size("dp") * lax.axis_size("fsdp")
    core = lax.axis_index("fsdp") % 2
    parts = grads[0].reshape((count // 2, 2, -1) + grads[0].shape[1:])
    return pick(parts, 1 - core, 1), pick(parts, core, 1)


def fold_core(spot, kept, received):
    dp_count, depth = lax.axis_size("dp"), lax.axis_size("fsdp") // 2
    shape = (depth,) + kept.shape[1:]
    if kept.shape[1] % 16:
        place = lax.axis_index("dp")
        pair = (kept.astype(FULL) + received.astype(FULL)).reshape((dp_count,) + shape)
        sends = [pick(pair, place ^ k, 0).astype(LOW) for k in range(1, dp_count)]
        return pick(pair, place, 0), sends
    own, *sends = call(
        functools.partial(fold_core_kernel, (dp_count, depth)), "fold_core", [spot],
        [kept, received], [(shape, FULL)] + [(shape, LOW)] * (dp_count - 1), kept.size,
    )
    return own, sends


def fold_square(spot, kept, received):
    dp_count, depth = lax.axis_size("dp"), lax.axis_size("fsdp") // 2
    shape = kept.shape[1:]
    if kept.shape[1] % 16:
        place = lax.axis_index("fsdp") // 2
        square = add_all(kept, received)
        sends = [pick(square, place ^ k, 0).astype(LOW) for k in range(1, depth)]
        return pick(square, place, 0), sends
    own, *sends = call(
        functools.partial(fold_square_kernel, (dp_count, depth)), "fold_square", [spot],
        [kept, *received], [(shape, FULL)] + [(shape, LOW)] * (depth - 1), kept.size,
    )
    return own, sends


def move_square(sends):
    stride = lax.axis_size("fsdp")
    return [exchange(item, stride * (k + 1)) for k, item in enumerate(sends)]


def move_layers(sends):
    return [exchange(item, 2 * (k + 1)) for k, item in enumerate(sends)]


def add_all(kept, moved):
    for item in moved:
        kept = kept + item.astype(FULL)
    return kept


def body(
    tokens,
    encoded,
    cotangent,
    target_ids,
    source_ids,
    qkv_master,
    qkv_first,
    qkv_second,
    out_master,
    out_first,
    out_second,
    ffn_in_master,
    ffn_in_first,
    ffn_in_second,
    ffn_out_master,
    ffn_out_first,
    ffn_out_second,
    vector_master,
    vector_first,
    vector_second,
):
    total, model = tokens.shape
    dp_count, fsdp_count = lax.axis_size("dp"), lax.axis_size("fsdp")
    count, depth = dp_count * fsdp_count, fsdp_count // 2
    rows = model // count
    aligned = rows % 16 == 0
    place = lax.axis_index("dp") * fsdp_count + lax.axis_index("fsdp")
    spot = place.reshape(1).astype(jnp.int32)
    low_qkv = after(qkv_master, spot).astype(LOW)
    low_out = out_master.astype(LOW)
    low_vector = jnp.pad(vector_master.astype(LOW).T, ((0, 0), (0, 128 - vector_master.shape[0])))
    pieces = ffn_in_master.shape[1] // model

    def to_columns(values):
        return values.reshape(-1, rows, model).transpose(1, 0, 2).reshape(rows, -1)

    self_piece = jnp.concatenate([low_qkv[0], low_qkv[1], low_qkv[2], low_vector], axis=1)
    cross_piece = jnp.concatenate([low_out[0], low_qkv[3], low_qkv[4], low_qkv[5], low_out[1]], axis=1)
    ffn_piece = jnp.concatenate(
        [ffn_in_master.astype(LOW), to_columns(ffn_out_master.astype(LOW))], axis=1
    )
    row_starts, col_starts = segment_starts(target_ids[0]), segment_starts(source_ids[0])

    def sources_of(parts):
        if aligned:
            return parts
        flat = ordered(parts, place)
        return [flat.reshape(model, -1)]

    def ffn_sources_of(parts):
        if aligned:
            return parts
        flat = ordered(parts, place)
        width = pieces * model
        second = flat[:, :, width:].reshape(count, rows, pieces, model).transpose(0, 2, 1, 3)
        second = second.reshape(pieces, model, model).transpose(1, 0, 2).reshape(model, -1)
        return [jnp.concatenate([flat[:, :, :width].reshape(model, -1), second], axis=1)]

    wide, tall, thin = ((total, model), LOW), ((total, model), FULL), ((total, 1), FULL)
    log_sums = ((SEGMENTS, model // 256, 1, 1024), FULL)
    small = ((8, model), FULL)
    unit = 2 * total * model * model
    attend = 2 * SEGMENTS * HEADS * 256 * 256 * 256
    wait_one, wait_two = pltpu.SemaphoreType.DMA((1,)), pltpu.SemaphoreType.DMA((2,))

    def grad_outs(columns):
        if aligned:
            return [((count // 2, rows, columns), LOW)] * 2
        return [((model, columns), LOW)]

    self_stack = layer_stack(self_piece)
    later = after(jnp.concatenate([cross_piece, ffn_piece], axis=1), self_stack)
    self_near = square_list(self_stack)
    later_stack = layer_stack(later)
    self_parts = core_list(self_near)
    cross_columns = cross_piece.shape[1]
    cross_near = square_list(later_stack[:, :, :cross_columns])
    ffn_near = square_list(later_stack[:, :, cross_columns:])

    sources = sources_of(self_parts)
    (
        self_weights, vectors, queries, keys, values, mixed, self_sums,
    ) = call(
        functools.partial(self_forward_kernel, len(sources), depth), "self_forward",
        [spot, row_starts], [after(tokens, later_stack)],
        [
            keep(((model, self_piece.shape[1]), LOW)), ((24, model), FULL),
            keep(wide), keep(wide), keep(wide), keep(wide), keep(log_sums),
        ],
        3 * unit + 2 * attend, sources, [wait_one],
    )
    sources = sources_of(core_list(cross_near))
    (
        cross_weights, unit_one, inverse_one, first_low, cross_queries, cross_keys, cross_values,
        cross_mixed, cross_log,
    ) = call(
        functools.partial(cross_forward_kernel, len(sources), depth), "cross_forward",
        [spot, row_starts, col_starts], [tokens, encoded, mixed, vectors],
        [
            keep(((model, cross_columns), LOW)), keep(tall), thin, keep(wide), keep(wide),
            keep(wide), keep(wide), keep(wide), keep(log_sums),
        ],
        4 * unit + 2 * attend, sources, [wait_one],
    )

    def weight_block(weights, index):
        return (weights, (model, model), (0, index))

    whole_vectors = (vectors, vectors.shape, (0, 0))
    unit_two, inverse_two = blocked(
        cross_finish_kernel, "cross_finish", [unit_one, cross_mixed],
        [weight_block(cross_weights, 4), whole_vectors], [tall, thin], unit,
    )
    sources = ffn_sources_of(core_list(ffn_near))
    hidden = pieces * model
    (
        layer_out, grad_sum, grad_cross_out, grad_cross_mixed, ffn_sums, bias_sums, *ffn_grads
    ) = blocked(
        functools.partial(ffn_kernel, len(sources), depth), "ffn",
        [unit_two, inverse_two, cotangent], [weight_block(cross_weights, 4), whole_vectors],
        [wide, tall, wide, wide], (5 * pieces + 1) * unit, [spot], sources,
        [small, small, *grad_outs(2 * hidden)],
        [
            pltpu.VMEM((model, hidden), LOW), pltpu.VMEM((hidden, model), LOW),
            pltpu.VMEM((total, model), LOW), pltpu.VMEM((total, hidden), LOW),
            pltpu.VMEM((total, model), LOW), pltpu.VMEM((total, hidden), LOW),
            pltpu.VMEM((STEP_ROWS, hidden), FULL), wait_two,
        ],
    )
    if not aligned:
        first, second = ffn_grads[0][:, :hidden], ffn_grads[0][:, hidden:]
        second = second.reshape(model, pieces, model).transpose(1, 0, 2)
        second = second.reshape(count, pieces, rows, model).transpose(0, 2, 1, 3)
        ffn_grads = [jnp.concatenate([first, second.reshape(model, -1)], axis=1)]
    sent, kept = split_core(ffn_grads)
    ffn_moved = exchange(sent, 1)
    cross_dq, cross_dk, cross_dv = call(
        cross_backward_kernel, "cross_backward", [row_starts, col_starts],
        [cross_queries, cross_keys, cross_values, after(grad_cross_mixed, sent), cross_log],
        [keep(wide), keep(wide), keep(wide)], 5 * attend,
    )
    ffn_kept, ffn_sends = fold_core(spot, kept, after(ffn_moved, cross_dq))
    ffn_moved = move_square(ffn_sends)
    first_sum, self_low, grad_mixed, cross_vector, *cross_grads = call(
        cross_grads_kernel, "cross_grads", [spot],
        [
            after(cross_dq, *ffn_sends), cross_dk, cross_dv, cross_weights, vectors, grad_sum,
            unit_one, inverse_one, first_low, encoded, cross_mixed, grad_cross_out,
        ],
        [keep(tall), keep(wide), keep(wide), small, *grad_outs(4 * model)], 6 * unit,
    )
    sent, kept = split_core(cross_grads)
    cross_moved = exchange(sent, 1)
    (encoded_grad,) = blocked(
        encoded_grad_kernel, "encoded_grad", [after(cross_dk, sent), cross_dv],
        [weight_block(cross_weights, 2), weight_block(cross_weights, 3)], [tall], 2 * unit,
    )
    cross_kept, cross_sends = fold_core(spot, kept, after(cross_moved, encoded_grad))
    cross_moved = move_square(cross_sends)
    self_dq, self_dk, self_dv = call(
        self_backward_kernel, "self_backward", [row_starts],
        [queries, keys, values, after(grad_mixed, *cross_sends), self_sums],
        [keep(wide), keep(wide), keep(wide)], 5 * attend,
    )
    self_grads = call(
        self_grads_kernel, "self_grads", [spot],
        [tokens, mixed, self_dq, self_dk, self_dv, self_low, cross_vector, ffn_sums, bias_sums],
        grad_outs(4 * model + 128), 4 * unit, (), [pltpu.VMEM((128, model), FULL)],
    )
    sent, kept = split_core(self_grads)
    self_moved = exchange(sent, 1)
    ffn_kept, ffn_sends = fold_square(spot, ffn_kept, [after(item, sent) for item in ffn_moved])
    ffn_moved = move_layers(ffn_sends)
    (tokens_grad,) = blocked(
        tokens_grad_kernel, "tokens_grad",
        [after(self_dq, *ffn_sends), self_dk, self_dv, first_sum],
        [(self_weights, self_weights.shape, (0, 0))], [tall], 3 * unit,
    )
    self_kept, self_sends = fold_core(spot, kept, after(self_moved, tokens_grad))
    self_moved = move_square(self_sends)
    cross_kept, cross_sends = fold_square(
        spot, cross_kept, [after(item, *self_sends) for item in cross_moved]
    )
    cross_moved = move_layers(cross_sends)
    ffn_total = add_all(ffn_kept, ffn_moved)
    cross_total = add_all(cross_kept, cross_moved)
    self_kept, self_sends = fold_square(
        spot, self_kept, [after(item, *cross_sends) for item in self_moved]
    )
    self_moved = move_layers(self_sends)
    self_total = add_all(self_kept, self_moved)

    def block(values, index):
        return values[:, index * model : (index + 1) * model]

    summed_qkv = jnp.stack(
        [block(self_total, i) for i in range(3)] + [block(cross_total, i) for i in range(3)]
    )
    summed_out = jnp.stack([block(self_total, 3), block(cross_total, 3)])
    summed_ffn_in = ffn_total[:, :hidden]
    summed_ffn_out = (
        ffn_total[:, hidden:].reshape(rows, pieces, model).transpose(1, 0, 2).reshape(-1, model)
    )
    summed_vector = self_total[:, 4 * model : 4 * model + vector_master.shape[0]].T
    grad_scale = 1.0 / math.sqrt(total * count)
    qkv_first_new, qkv_second_new, qkv_master_new, qkv_copy = adamw(
        qkv_master, summed_qkv * grad_scale, qkv_first, qkv_second, 0.04
    )
    out_first_new, out_second_new, out_master_new, out_copy = adamw(
        out_master, summed_out * grad_scale, out_first, out_second, 0.3
    )
    ffn_in_first_new, ffn_in_second_new, ffn_in_master_new, ffn_in_copy = adamw(
        ffn_in_master, summed_ffn_in * grad_scale, ffn_in_first, ffn_in_second, 0.04
    )
    ffn_out_first_new, ffn_out_second_new, ffn_out_master_new, ffn_out_copy = adamw(
        ffn_out_master, summed_ffn_out * grad_scale, ffn_out_first, ffn_out_second, 0.02
    )
    vector_first_new, vector_second_new, vector_master_new, vector_copy = adamw(
        vector_master, summed_vector * grad_scale, vector_first, vector_second, 0.35
    )
    return (
        layer_out,
        tokens_grad,
        encoded_grad,
        qkv_first_new,
        qkv_second_new,
        qkv_master_new,
        qkv_copy,
        out_first_new,
        out_second_new,
        out_master_new,
        out_copy,
        ffn_in_first_new,
        ffn_in_second_new,
        ffn_in_master_new,
        ffn_in_copy,
        ffn_out_first_new,
        ffn_out_second_new,
        ffn_out_master_new,
        ffn_out_copy,
        vector_first_new,
        vector_second_new,
        vector_master_new,
        vector_copy,
    )


def solution(mesh):
    return jax.shard_map(
        body,
        mesh=mesh,
        in_specs=(
            P(("dp", "fsdp"), None),
            P(("dp", "fsdp"), None),
            P(("dp", "fsdp"), None),
            P(("dp", "fsdp"), None),
            P(("dp", "fsdp"), None),
            P(None, ("dp", "fsdp"), None),
            P(None, ("dp", "fsdp"), None),
            P(None, ("dp", "fsdp"), None),
            P(None, ("dp", "fsdp"), None),
            P(None, ("dp", "fsdp"), None),
            P(None, ("dp", "fsdp"), None),
            P(("dp", "fsdp"), None),
            P(("dp", "fsdp"), None),
            P(("dp", "fsdp"), None),
            P(("dp", "fsdp"), None),
            P(("dp", "fsdp"), None),
            P(("dp", "fsdp"), None),
            P(None, ("dp", "fsdp")),
            P(None, ("dp", "fsdp")),
            P(None, ("dp", "fsdp")),
        ),
        out_specs=(
            P(("dp", "fsdp"), None),
            P(("dp", "fsdp"), None),
            P(("dp", "fsdp"), None),
            P(None, ("dp", "fsdp"), None),
            P(None, ("dp", "fsdp"), None),
            P(None, ("dp", "fsdp"), None),
            P(None, ("dp", "fsdp"), None),
            P(None, ("dp", "fsdp"), None),
            P(None, ("dp", "fsdp"), None),
            P(None, ("dp", "fsdp"), None),
            P(None, ("dp", "fsdp"), None),
            P(("dp", "fsdp"), None),
            P(("dp", "fsdp"), None),
            P(("dp", "fsdp"), None),
            P(("dp", "fsdp"), None),
            P(("dp", "fsdp"), None),
            P(("dp", "fsdp"), None),
            P(("dp", "fsdp"), None),
            P(("dp", "fsdp"), None),
            P(None, ("dp", "fsdp")),
            P(None, ("dp", "fsdp")),
            P(None, ("dp", "fsdp")),
            P(None, ("dp", "fsdp")),
        ),
        check_vma=False,
    )
```

```python
import functools
import math

import jax
import jax.numpy as jnp
from jax import lax
from jax.experimental import pallas as pl
from jax.experimental.pallas import tpu as pltpu
from jax.sharding import PartitionSpec as P

HEADS = 8
STEP = 5
SEGMENTS = 10
norm_eps = 1e-05
beta_first = 0.5
beta_second = 0.5
adam_eps = 1e-08
weight_decay = 0.01
mask_fill = -1000000000.0
LOW = jnp.bfloat16
FULL = jnp.float32


def dot_nn(left, right):
    return lax.dot_general(left, right, (((1,), (0,)), ((), ())), preferred_element_type=FULL)


def dot_nt(left, right):
    return lax.dot_general(left, right, (((1,), (1,)), ((), ())), preferred_element_type=FULL)


def dot_tn(left, right):
    return lax.dot_general(left, right, (((0,), (0,)), ((), ())), preferred_element_type=FULL)


def head_masks(width, group, factor):
    lane = lax.broadcasted_iota(jnp.int32, (1, group * width), 1) // width
    return [jnp.where(lane == h, factor, 0.0).astype(LOW) for h in range(group)]


def window(start, size, total):
    return pl.multiple_of(jnp.minimum(start // 16 * 16, total - size), 16)


def inside(base, size, begin, end):
    place = lax.broadcasted_iota(jnp.int32, (size, 1), 0) + base
    return (place >= begin) & (place < end)


def each_span(row_starts, col_starts, total, same, work):
    def segment(s, carry):
        row_begin, row_end = row_starts[s], row_starts[s + 1]
        col_begin, col_end = col_starts[s], col_starts[s + 1]
        row_short = row_end - window(row_begin, 128, total) <= 128
        col_short = col_end - window(col_begin, 128, total) <= 128
        for row_span in (128, 256):
            for col_span in (128, 256):
                if same and row_span != col_span:
                    continue
                wanted = row_short if row_span == 128 else jnp.logical_not(row_short)
                if not same:
                    other = col_short if col_span == 128 else jnp.logical_not(col_short)
                    wanted = jnp.logical_and(wanted, other)

                @pl.when(wanted)
                def _(row_span=row_span, col_span=col_span):
                    row_base = window(row_begin, row_span, total)
                    col_base = window(col_begin, col_span, total)
                    work(
                        s,
                        pl.ds(row_base, row_span),
                        pl.ds(col_base, col_span),
                        inside(row_base, row_span, row_begin, row_end),
                        inside(col_base, col_span, col_begin, col_end),
                        row_span,
                    )

        return carry

    lax.fori_loop(0, SEGMENTS, segment, 0)


def attend_forward(row_starts, col_starts, q_ref, k_ref, v_ref, out_ref, sums_ref):
    total, model = q_ref.shape
    width = model // HEADS
    group = 256 // width
    scales = head_masks(width, group, 1.0 / math.sqrt(width))
    parts = [slice(g * 256, (g + 1) * 256) for g in range(HEADS // group)]

    def work(s, rows, cols, row_mask, col_mask, span):
        raw = []
        for lanes in parts:
            query, keys = q_ref[rows, lanes], k_ref[cols, lanes]
            stacked = jnp.concatenate([query * scale for scale in scales], axis=0)
            raw.append(dot_nt(keys, stacked))
        turned = [v_ref[cols, lanes].T for lanes in parts]
        probs = []
        for g, item in enumerate(raw):
            scores = jnp.where(col_mask, item, mask_fill)
            largest = jnp.max(scores, axis=0, keepdims=True)
            expo = jnp.exp(scores - largest)
            totals = jnp.sum(expo, axis=0, keepdims=True)
            sums_ref[s, g, :, : group * span] = largest + jnp.log(totals)
            probs.append((expo * (1.0 / totals)).astype(LOW))
        mixed = [
            [
                dot_nn(side[h * width : (h + 1) * width], prob[:, h * span : (h + 1) * span])
                for h in range(group)
            ]
            for side, prob in zip(turned, probs)
        ]
        for lanes, items in zip(parts, mixed):
            value = jnp.concatenate(items, axis=0).T
            old = out_ref[rows, lanes].astype(FULL)
            out_ref[rows, lanes] = jnp.where(row_mask, value, old).astype(LOW)

    each_span(row_starts, col_starts, total, row_starts is col_starts, work)


def attend_backward(
    row_starts, col_starts, q_ref, k_ref, v_ref, grad_ref, sums_ref, dq_ref, dk_ref, dv_ref
):
    total, model = q_ref.shape
    width = model // HEADS
    group = 256 // width
    factor = 1.0 / math.sqrt(width)
    scales = head_masks(width, group, factor)
    picks = head_masks(width, group, 1.0)
    parts = [slice(g * 256, (g + 1) * 256) for g in range(HEADS // group)]

    def work(s, rows, cols, row_mask, col_mask, span):
        stacks, grads, raw, grad_probs = [], [], [], []
        for lanes in parts:
            query, keys, values = q_ref[rows, lanes], k_ref[cols, lanes], v_ref[cols, lanes]
            grad = jnp.where(row_mask, grad_ref[rows, lanes].astype(FULL), 0.0).astype(LOW)
            stacks.append(jnp.concatenate([query * scale for scale in scales], axis=0))
            grads.append(jnp.concatenate([grad * item for item in picks], axis=0))
            raw.append(dot_nt(keys, stacks[-1]))
            grad_probs.append(dot_nt(values, grads[-1]))
        grad_values, grad_scores = [], []
        for g, (item, grad_prob) in enumerate(zip(raw, grad_probs)):
            scores = jnp.where(col_mask, item, mask_fill)
            probs = jnp.exp(scores - sums_ref[s, g, :, : group * span])
            grad_values.append(dot_nn(probs.astype(LOW), grads[g]))
            weighted = probs * grad_prob
            inner = jnp.sum(weighted, axis=0, keepdims=True)
            grad_scores.append((weighted - probs * inner).astype(LOW))
        grad_keys, grad_queries = [], []
        for lanes, item, stacked in zip(parts, grad_scores, stacks):
            grad_keys.append(dot_nn(item, stacked))
            turned = k_ref[cols, lanes].T
            grad_queries.append(
                [
                    dot_nn(turned[h * width : (h + 1) * width], item[:, h * span : (h + 1) * span])
                    for h in range(group)
                ]
            )
        for g, lanes in enumerate(parts):
            grad_query = jnp.concatenate(grad_queries[g], axis=0).T * factor
            for ref, place, mask, value in (
                (dq_ref, rows, row_mask, grad_query),
                (dk_ref, cols, col_mask, grad_keys[g]),
                (dv_ref, cols, col_mask, grad_values[g]),
            ):
                old = ref[place, lanes].astype(FULL)
                ref[place, lanes] = jnp.where(mask, value, old).astype(LOW)

    each_span(row_starts, col_starts, total, row_starts is col_starts, work)


def normalize(values):
    center = values - jnp.mean(values, axis=-1, keepdims=True)
    inverse = lax.rsqrt(jnp.mean(center * center, axis=-1, keepdims=True) + norm_eps)
    return center * inverse, inverse


def normalize_back(grad, gain, unit, inverse):
    scaled = grad * (1.0 + gain)
    mean = jnp.mean(scaled, axis=-1, keepdims=True)
    along = jnp.mean(scaled * unit, axis=-1, keepdims=True)
    return (scaled - mean - unit * along) * inverse


def column_sum(values):
    return jnp.sum(values.astype(FULL), axis=0, keepdims=True)


STEP_ROWS = 256


def row_steps(total, step):
    def run(i, carry):
        step(pl.ds(pl.multiple_of(i * STEP_ROWS, STEP_ROWS), STEP_ROWS))
        return carry

    lax.fori_loop(0, total // STEP_ROWS, run, 0)


def load_weights(place, depth, sources, targets, semaphores):
    if len(sources) == 1:
        offset = 0
        for target, semaphore in zip(targets, semaphores):
            source = sources[0].at[:, offset : offset + target.shape[1]]
            offset += target.shape[1]
            pltpu.make_async_copy(source, target, semaphore).start()
        return
    half = len(sources) // 2
    for k, source in enumerate(sources):
        base = (k % half) * 2 * depth + k // half
        for layer in range(depth):
            other = place ^ (base + 2 * layer)
            offset = 0
            for target, semaphore in zip(targets, semaphores):
                rows = source.shape[1]
                span = target.shape[1]
                to_rows = pl.ds(pl.multiple_of(other * rows, rows), rows)
                pltpu.make_async_copy(
                    source.at[layer, :, offset : offset + span], target.at[to_rows, :], semaphore
                ).start()
                offset += span


def await_weights(target, semaphore):
    pltpu.make_async_copy(target, target, semaphore).wait()


def store_grad(refs, core, lanes, value):
    value = value.astype(LOW)
    if len(refs) == 1:
        refs[0][:, lanes] = value
        return
    sent, kept = refs
    chips, rows = kept.shape[0], kept.shape[1]
    parts = value.reshape(chips, 2, rows, value.shape[1])
    first = core == 0
    kept[:, :, lanes] = jnp.where(first, parts[:, 0], parts[:, 1])
    sent[:, :, lanes] = jnp.where(first, parts[:, 1], parts[:, 0])


def self_forward_kernel(count, depth, place, row_starts, tokens, *rest):
    sources = rest[:count]
    weights, vectors, queries, keys, values, mixed, sums, semaphores = rest[count:]
    model = tokens.shape[1]
    load_weights(place[0], depth, sources, [weights], [semaphores.at[0]])
    await_weights(weights, semaphores.at[0])
    turned = weights[:, 3 * model : 3 * model + 128].astype(FULL).T
    vectors[...] = turned[: vectors.shape[0]]

    def project(rows):
        block = tokens[rows, :]
        queries[rows, :] = (dot_nn(block, weights[:, :model]) + vectors[0:1, :]).astype(LOW)
        keys[rows, :] = dot_nn(block, weights[:, model : 2 * model]).astype(LOW)
        values[rows, :] = (
            dot_nn(block, weights[:, 2 * model : 3 * model]) + vectors[1:2, :]
        ).astype(LOW)

    row_steps(tokens.shape[0], project)
    attend_forward(row_starts, row_starts, queries, keys, values, mixed, sums)


def cross_forward_kernel(
    count, depth, place, row_starts, col_starts, tokens, encoded, mixed, vectors, *rest
):
    sources = rest[:count]
    (
        weights, unit_one, inverse_one, first_low, queries, keys, values, cross_mixed, sums, semaphores,
    ) = rest[count:]
    model = tokens.shape[1]
    load_weights(place[0], depth, sources, [weights], [semaphores.at[0]])
    await_weights(weights, semaphores.at[0])

    def project(rows):
        block = encoded[rows, :]
        keys[rows, :] = dot_nn(block, weights[:, 2 * model : 3 * model]).astype(LOW)
        values[rows, :] = (
            dot_nn(block, weights[:, 3 * model : 4 * model]) + vectors[4:5, :]
        ).astype(LOW)
        summed = tokens[rows, :].astype(FULL) + dot_nn(mixed[rows, :], weights[:, :model])
        unit, inverse = normalize(summed + vectors[2:3, :])
        unit_one[rows, :] = unit
        inverse_one[rows, :] = inverse
        low = (unit * (1.0 + vectors[7:8, :]) + vectors[10:11, :]).astype(LOW)
        first_low[rows, :] = low
        queries[rows, :] = (dot_nn(low, weights[:, model : 2 * model]) + vectors[3:4, :]).astype(LOW)

    row_steps(tokens.shape[0], project)
    attend_forward(row_starts, col_starts, queries, keys, values, cross_mixed, sums)


def cross_finish_kernel(unit_one, cross_mixed, weights, vectors, unit_two, inverse_two):
    first = unit_one[...] * (1.0 + vectors[7:8, :]) + vectors[10:11, :]
    summed = first + dot_nn(cross_mixed[...], weights[...]) + vectors[5:6, :]
    unit, inverse = normalize(summed)
    unit_two[...] = unit
    inverse_two[...] = inverse


gelu_scale = math.sqrt(2.0 / math.pi)
gelu_cubic = 0.044715


def ffn_kernel(count, depth, place, unit_two, inverse_two, cotangent, cross_out, vectors, *rest):
    sources = rest[:count]
    (
        layer_out, grad_sum, grad_out, grad_mixed, sums, bias_sums, *grads,
        first_weights, second_weights, second_low, hidden, grad_ffn, grad_pre, slopes, semaphores,
    ) = rest[count:]
    step = pl.program_id(0)
    model = unit_two.shape[1]
    pieces = first_weights.shape[1] // model
    rows = pl.ds(pl.multiple_of(step * STEP_ROWS, STEP_ROWS), STEP_ROWS)

    @pl.when(step == 0)
    def _():
        sums[...] = jnp.zeros_like(sums)
        bias_sums[...] = jnp.zeros_like(bias_sums)
        load_ffn(place[0], depth, sources, first_weights, second_weights, semaphores)
        await_weights(first_weights, semaphores.at[0])
        await_weights(second_weights, semaphores.at[1])

    unit = unit_two[...]
    second = unit * (1.0 + vectors[8:9, :]) + vectors[11:12, :]
    low = second.astype(LOW)
    second_low[rows, :] = low
    total = second + vectors[6:7, :]
    for j in range(pieces):
        lanes = slice(j * model, (j + 1) * model)
        pre = dot_nn(low, first_weights[:, lanes]) + vectors[13 + j : 14 + j, :]
        square = pre * pre
        bend = jnp.tanh(gelu_scale * pre * (1.0 + gelu_cubic * square))
        half = 0.5 * (1.0 + bend)
        value = (pre * half).astype(LOW)
        hidden[rows, lanes] = value
        inner = gelu_scale * (1.0 + 3.0 * gelu_cubic * square)
        slopes[:, lanes] = half + 0.5 * pre * (1.0 - bend * bend) * inner
        total = total + dot_nn(value, second_weights[lanes, :])
    unit_three, inverse_three = normalize(total)
    layer_out[...] = (unit_three * (1.0 + vectors[9:10, :]) + vectors[12:13, :]).astype(LOW)
    upper = cotangent[...].astype(FULL)
    third = normalize_back(upper, vectors[9:10, :], unit_three, inverse_three)
    third_low = third.astype(LOW)
    grad_ffn[rows, :] = third_low
    sums[0:1, :] += column_sum(third_low)
    sums[1:2, :] += column_sum(upper * unit_three)
    sums[2:3, :] += column_sum(upper)
    below = third
    for j in range(pieces):
        lanes = slice(j * model, (j + 1) * model)
        pre = (dot_nt(third_low, second_weights[lanes, :]) * slopes[:, lanes]).astype(LOW)
        grad_pre[rows, lanes] = pre
        bias_sums[j : j + 1, :] += column_sum(pre)
        below = below + dot_nt(pre, first_weights[:, lanes])
    sums[3:4, :] += column_sum(below * unit)
    sums[4:5, :] += column_sum(below)
    second_sum = normalize_back(below, vectors[8:9, :], unit, inverse_two[...])
    grad_sum[...] = second_sum
    out_low = second_sum.astype(LOW)
    grad_out[...] = out_low
    sums[5:6, :] += column_sum(out_low)
    grad_mixed[...] = dot_nt(out_low, cross_out[...]).astype(LOW)

    @pl.when(step == pl.num_programs(0) - 1)
    def _():
        core = place[0] % 2
        for j in range(pieces):
            lanes = slice(j * model, (j + 1) * model)
            store_grad(grads, core, lanes, dot_tn(second_low[...], grad_pre[:, lanes]))
        span = second_weights.shape[0] // pieces
        for j in range(pieces):
            value = dot_tn(hidden[:, j * span : (j + 1) * span], grad_ffn[...])
            store_ffn_out(grads, core, j, pieces, value)


def load_ffn(place, depth, sources, first_weights, second_weights, semaphores):
    first_width = first_weights.shape[1]
    if len(sources) == 1:
        pltpu.make_async_copy(
            sources[0].at[:, :first_width], first_weights, semaphores.at[0]
        ).start()
        pieces = first_width // first_weights.shape[0]
        model = first_weights.shape[0]
        for j in range(pieces):
            pltpu.make_async_copy(
                sources[0].at[:, first_width + j * model : first_width + (j + 1) * model],
                second_weights.at[pl.ds(j * model, model), :],
                semaphores.at[1],
            ).start()
        return
    half = len(sources) // 2
    model = second_weights.shape[1]
    for k, source in enumerate(sources):
        base = (k % half) * 2 * depth + k // half
        rows = source.shape[1]
        for layer in range(depth):
            other = place ^ (base + 2 * layer)
            to_rows = pl.ds(pl.multiple_of(other * rows, rows), rows)
            pltpu.make_async_copy(
                source.at[layer, :, :first_width], first_weights.at[to_rows, :], semaphores.at[0]
            ).start()
            pieces = first_width // model
            for j in range(pieces):
                start = pl.multiple_of((other * pieces + j) * rows, rows)
                pltpu.make_async_copy(
                    source.at[layer, :, first_width + j * model : first_width + (j + 1) * model],
                    second_weights.at[pl.ds(start, rows), :],
                    semaphores.at[1],
                ).start()


def store_ffn_out(refs, core, block, pieces, value):
    value = value.astype(LOW)
    model = value.shape[1]
    if len(refs) == 1:
        offset = (pieces + block) * model
        refs[0][:, offset : offset + model] = value
        return
    sent, kept = refs
    rows = kept.shape[1]
    chips = kept.shape[0] // pieces
    parts = value.reshape(chips, 2, pieces, rows, model)
    first = core == 0
    for j in range(pieces):
        lanes = slice((pieces + j) * model, (pieces + j + 1) * model)
        place = slice(block * chips, (block + 1) * chips)
        kept[place, :, lanes] = jnp.where(first, parts[:, 0, j], parts[:, 1, j])
        sent[place, :, lanes] = jnp.where(first, parts[:, 1, j], parts[:, 0, j])


def cross_backward_kernel(
    row_starts, col_starts, queries, keys, values, grad_mixed, sums_in, dq, dk, dv
):
    attend_backward(row_starts, col_starts, queries, keys, values, grad_mixed, sums_in, dq, dk, dv)


def cross_grads_kernel(
    place, dq, dk, dv, weights, vectors, grad_sum, unit_one, inverse_one,
    first_low, encoded, cross_mixed, grad_out,
    first_sum, self_low, grad_mixed, sums, encoded_grad, *grads,
):
    model = dq.shape[1]
    sums[...] = jnp.zeros_like(sums)

    def finish(rows):
        query, key, value = dq[rows, :], dk[rows, :], dv[rows, :]
        sums[0:1, :] += column_sum(query)
        sums[1:2, :] += column_sum(value)
        encoded_grad[rows, :] = dot_nt(key, weights[:, 2 * model : 3 * model]) + dot_nt(
            value, weights[:, 3 * model : 4 * model]
        )
        upper = grad_sum[rows, :] + dot_nt(query, weights[:, model : 2 * model])
        unit = unit_one[rows, :]
        sums[2:3, :] += column_sum(upper * unit)
        sums[3:4, :] += column_sum(upper)
        below = normalize_back(upper, vectors[7:8, :], unit, inverse_one[rows, :])
        first_sum[rows, :] = below
        low = below.astype(LOW)
        self_low[rows, :] = low
        sums[4:5, :] += column_sum(low)
        grad_mixed[rows, :] = dot_nt(low, weights[:, :model]).astype(LOW)

    row_steps(dq.shape[0], finish)
    core = place[0] % 2
    pairs = ((first_low, dq), (encoded, dk), (encoded, dv), (cross_mixed, grad_out))
    for j, (left, right) in enumerate(pairs):
        lanes = slice(j * model, (j + 1) * model)
        store_grad(grads, core, lanes, dot_tn(left[...], right[...]))


def self_backward_kernel(
    place, row_starts, queries, keys, values, grad_mixed, sums_in, tokens, mixed, self_low,
    cross_sums, ffn_sums, bias_sums, dq, dk, dv, *rest,
):
    *grads, stack = rest
    attend_backward(row_starts, row_starts, queries, keys, values, grad_mixed, sums_in, dq, dk, dv)
    model = dq.shape[1]
    core = place[0] % 2
    pairs = ((tokens, dq), (tokens, dk), (tokens, dv), (mixed, self_low))
    for j, (left, right) in enumerate(pairs):
        lanes = slice(j * model, (j + 1) * model)
        store_grad(grads, core, lanes, dot_tn(left[...], right[...]))
    stack[...] = jnp.zeros_like(stack)
    stack[0:1, :] = column_sum(dq[...])
    stack[1:2, :] = column_sum(dv[...])
    order = (
        (2, cross_sums, 4), (3, cross_sums, 0), (4, cross_sums, 1), (5, ffn_sums, 5),
        (6, ffn_sums, 0), (7, cross_sums, 2), (8, ffn_sums, 3), (9, ffn_sums, 1),
        (10, cross_sums, 3), (11, ffn_sums, 4), (12, ffn_sums, 2),
    )
    for to, ref, at in order:
        stack[to : to + 1, :] = ref[at : at + 1, :]
    extra = bias_sums.shape[0]
    stack[13 : 13 + extra, :] = bias_sums[...]
    start = len(pairs) * model
    store_grad(grads, core, slice(start, start + 128), stack[...].T)


def tokens_grad_kernel(dq, dk, dv, first_sum, weights, tokens_grad):
    model = dq.shape[1]
    below = first_sum[...] + dot_nt(dq[...], weights[:, :model])
    below = below + dot_nt(dk[...], weights[:, model : 2 * model])
    tokens_grad[...] = below + dot_nt(dv[...], weights[:, 2 * model : 3 * model])


def fold_core_kernel(shape, place, kept, received, own, *sends):
    dp_count, depth = shape
    at = place[0] // (2 * depth)
    for k, ref in enumerate((own, *sends)):
        spot = pl.ds((at ^ k) * depth, depth)
        value = kept[spot].astype(FULL) + received[spot].astype(FULL)
        ref[...] = value.astype(ref.dtype)


def fold_square_kernel(shape, place, kept, *rest):
    dp_count, depth = shape
    received, outs = rest[: dp_count - 1], rest[dp_count - 1 :]
    at = place[0] // 2 % depth
    for k, ref in enumerate(outs):
        spot = pl.ds(at ^ k, 1)
        value = kept[spot]
        for item in received:
            value = value + item[spot].astype(FULL)
        ref[...] = value[0].astype(ref.dtype)


def fold_halves_kernel(depth, place, kept, received, keep_first, send_first, keep_second, send_second):
    at = place[0] // (2 * depth)
    half = kept.shape[2] // 2
    low, high = slice(0, half), slice(half, 2 * half)
    for ref, lanes, offsets in (
        (keep_first, low, (0, 1)),
        (send_first, low, (2, 3)),
        (keep_second, high, (0, 2)),
        (send_second, high, (1, 3)),
    ):
        for slot, k in enumerate(offsets):
            spot = pl.ds((at ^ k) * depth, depth)
            value = kept[spot, :, lanes].astype(FULL) + received[spot, :, lanes].astype(FULL)
            ref[slot] = value.astype(ref.dtype)


def fold_pairs_kernel(keep_first, got_first, keep_second, got_second, *outs):
    own_first, send_first, own_second, send_second = outs
    own_first[...] = keep_first[0] + got_first[0].astype(FULL)
    send_first[...] = (keep_first[1] + got_first[1].astype(FULL)).astype(LOW)
    own_second[...] = keep_second[0] + got_second[0].astype(FULL)
    send_second[...] = (keep_second[1] + got_second[1].astype(FULL)).astype(LOW)


def fold_layers_kernel(depth, place, first, got_first, second, got_second, cross, *rest):
    *got_cross, keep, send = rest
    at = place[0] // 2 % depth
    half = first.shape[2]
    for ref, offsets in ((keep, (0, 1)), (send, (2, 3))):
        for slot, k in enumerate(offsets):
            spot = pl.ds(at ^ k, 1)
            value = first[spot] + got_first[spot].astype(FULL)
            ref[slot, :, :half] = value[0].astype(ref.dtype)
            value = second[spot] + got_second[spot].astype(FULL)
            ref[slot, :, half : 2 * half] = value[0].astype(ref.dtype)
            value = cross[spot]
            for item in got_cross:
                value = value + item[spot].astype(FULL)
            ref[slot, :, 2 * half :] = value[0].astype(ref.dtype)


def fold_last_kernel(keep, got, own, send):
    own[...] = keep[0] + got[0].astype(FULL)
    send[...] = (keep[1] + got[1].astype(FULL)).astype(LOW)


def update_into(outs, index, state, grad, rate):
    for ref, value in zip(outs, adamw(state[0][index], grad, state[1][index], state[2][index], rate)):
        ref[index] = value


def ffn_update_kernel(grad_scale, own, got, *rest):
    first_state, second_state, outs = rest[:3], rest[3:6], rest[6:]
    rows, width = first_state[0].shape
    model = second_state[0].shape[1]
    grad = (own[:, :width] + got[:, :width].astype(FULL)) * grad_scale
    update_into(outs[:4], (slice(None), slice(None)), first_state, grad, 0.04)
    for j in range(second_state[0].shape[0] // rows):
        lanes = slice(width + j * model, width + (j + 1) * model)
        grad = (own[:, lanes] + got[:, lanes].astype(FULL)) * grad_scale
        index = (slice(j * rows, (j + 1) * rows), slice(None))
        update_into(outs[4:], index, second_state, grad, 0.02)


def final_update_kernel(grad_scale, start, own, got, kept, *rest):
    moved, states, outs = rest[:-21], rest[-21:-12], rest[-12:]
    qkv_state, out_state, vector_state = states[:3], states[3:6], states[6:]
    model = qkv_state[0].shape[2]

    def self_grad(lanes):
        value = kept[:, lanes]
        for item in moved:
            value = value + item[:, lanes].astype(FULL)
        return value * grad_scale

    def cross_grad(index):
        lanes = slice(start + index * model, start + (index + 1) * model)
        return (own[:, lanes] + got[:, lanes].astype(FULL)) * grad_scale

    for j in range(4):
        grad = self_grad(slice(j * model, (j + 1) * model))
        if j < 3:
            update_into(outs[:4], j, qkv_state, grad, 0.04)
            update_into(outs[:4], 3 + j, qkv_state, cross_grad(j), 0.04)
        else:
            update_into(outs[4:8], 0, out_state, grad, 0.3)
            update_into(outs[4:8], 1, out_state, cross_grad(j), 0.3)
    grad = self_grad(slice(4 * model, 4 * model + vector_state[0].shape[1]))
    update_into(outs[8:], (slice(None), slice(None)), vector_state, grad, 0.35)


LIMITS = {
    "fold_halves": 16,
    "fold_pairs": 14,
    "fold_layers": 12,
    "fold_last": 8,
    "ffn_update": 8,
    "final_update": 10,
    "fold_core": 12,
    "fold_square": 10,
    "self_forward": 14,
    "cross_forward": 16,
    "cross_finish": 9,
    "ffn": 27,
    "cross_backward": 11,
    "cross_grads": 20,
    "self_backward": 16,
    "tokens_grad": 11,
}


def out_kind(item):
    if len(item) == 3:
        return pltpu.VMEM(item[0], item[1])
    return jax.ShapeDtypeStruct(*item)


def keep(item):
    return (item[0], item[1], True)


def limit(name):
    return pltpu.CompilerParams(vmem_limit_bytes=LIMITS[name] << 20)


def pinned(sources):
    if len(sources) == 1:
        return sources
    return [pltpu.with_memory_space_constraint(item, pltpu.VMEM) for item in sources]


def source_spec(sources):
    return pl.BlockSpec(memory_space=pltpu.VMEM if len(sources) > 1 else pl.ANY)


def call(kernel, name, scalars, arrays, outs, flops, sources=(), scratch=()):
    specs = [pl.BlockSpec(memory_space=pltpu.SMEM)] * len(scalars)
    specs += [pl.BlockSpec(memory_space=pltpu.VMEM)] * len(arrays)
    specs += [source_spec(sources)] * len(sources)
    shapes = [out_kind(item) for item in outs]
    moved = sum(item.size * item.dtype.itemsize for item in [*arrays, *sources])
    return pl.pallas_call(
        kernel,
        out_shape=shapes,
        in_specs=specs,
        out_specs=[pl.BlockSpec(memory_space=pltpu.VMEM)] * len(outs),
        scratch_shapes=list(scratch),
        compiler_params=limit(name),
        cost_estimate=pl.CostEstimate(flops=flops, transcendentals=0, bytes_accessed=moved),
        name=name,
    )(*scalars, *arrays, *pinned(sources))


def blocked(kernel, name, arrays, fixed, outs, flops, scalars=(), sources=(), fixed_outs=(), scratch=()):
    total = arrays[0].shape[0]
    specs = [pl.BlockSpec(memory_space=pltpu.SMEM)] * len(scalars)
    specs += [pl.BlockSpec((STEP_ROWS, item.shape[1]), lambda i: (i, 0)) for item in arrays]
    for item, shape, index in fixed:
        specs.append(
            pl.BlockSpec(shape, lambda i, index=index: index, pipeline_mode=pl.Buffered(1))
        )
    specs += [source_spec(sources)] * len(sources)
    shapes = [out_kind(item) for item in [*outs, *fixed_outs]]
    out_specs = [pl.BlockSpec((STEP_ROWS, item[0][1]), lambda i: (i, 0)) for item in outs]
    for item in fixed_outs:
        index = (0,) * len(item[0])
        out_specs.append(
            pl.BlockSpec(item[0], lambda i, index=index: index, pipeline_mode=pl.Buffered(1))
        )
    inputs = [*arrays, *[item[0] for item in fixed]]
    moved = sum(item.size * item.dtype.itemsize for item in [*arrays, *sources])
    return pl.pallas_call(
        kernel,
        grid=(total // STEP_ROWS,),
        out_shape=shapes,
        in_specs=specs,
        out_specs=out_specs,
        scratch_shapes=list(scratch),
        compiler_params=limit(name),
        cost_estimate=pl.CostEstimate(flops=flops, transcendentals=0, bytes_accessed=moved),
        name=name,
    )(*scalars, *inputs, *pinned(sources))


def segment_starts(ids):
    marks = jnp.arange(SEGMENTS + 1, dtype=ids.dtype)
    return jnp.sum((ids[None, :] < marks[:, None]).astype(jnp.int32), axis=1)


def adamw(master, grad, first, second, rate):
    first_new = beta_first * first + (1.0 - beta_first) * grad
    second_new = beta_second * second + (1.0 - beta_second) * grad * grad
    first_hat = first_new / (1.0 - beta_first**STEP)
    second_hat = second_new / (1.0 - beta_second**STEP)
    master_new = master - rate * (
        first_hat / (jnp.sqrt(second_hat) + adam_eps) + weight_decay * master
    )
    return (first_new, second_new, master_new, master_new.astype(jnp.bfloat16))


AXES = ("dp", "fsdp")


def exchange(values, offset):
    count = lax.axis_size("dp") * lax.axis_size("fsdp")
    return lax.ppermute(values, AXES, [(i, i ^ offset) for i in range(count)])


def after(value, *others):
    return lax.optimization_barrier((value, *others))[0]


def layer_stack(piece):
    depth = lax.axis_size("fsdp") // 2
    return jnp.stack([piece] + [exchange(piece, 2 * k) for k in range(1, depth)])


def square_list(stack):
    dp_count, fsdp_count = lax.axis_size("dp"), lax.axis_size("fsdp")
    return [stack] + [exchange(stack, fsdp_count * k) for k in range(1, dp_count)]


def forward_list(stack):
    stride, near = lax.axis_size("fsdp"), [stack]
    for k in range(1, lax.axis_size("dp")):
        near.append(None if k & (k - 1) else exchange(stack, stride * k))
    return near


def forward_rest(near, gate):
    stride = lax.axis_size("fsdp")
    for k, item in enumerate(near):
        if item is None:
            high = 1 << (k.bit_length() - 1)
            near[k] = exchange(after(near[k - high], gate), stride * high)
    return near


def core_list(near):
    return near + [exchange(item, 1) for item in near]


def ordered(parts, place):
    half = len(parts) // 2
    both = jnp.stack([jnp.stack(parts[:half]), jnp.stack(parts[half:])], axis=2)
    flat = both.reshape((-1,) + both.shape[3:])
    return flat[jnp.arange(flat.shape[0]) ^ place]


def pick(values, index, axis):
    return lax.dynamic_index_in_dim(values, index, axis, keepdims=False)


def split_core(grads):
    if len(grads) == 2:
        return grads
    count = lax.axis_size("dp") * lax.axis_size("fsdp")
    core = lax.axis_index("fsdp") % 2
    parts = grads[0].reshape((count // 2, 2, -1) + grads[0].shape[1:])
    return pick(parts, 1 - core, 1), pick(parts, core, 1)


def fold_core(spot, kept, received):
    dp_count, depth = lax.axis_size("dp"), lax.axis_size("fsdp") // 2
    shape = (depth,) + kept.shape[1:]
    if kept.shape[1] % 16:
        place = lax.axis_index("dp")
        pair = (kept.astype(FULL) + received.astype(FULL)).reshape((dp_count,) + shape)
        sends = [pick(pair, place ^ k, 0).astype(LOW) for k in range(1, dp_count)]
        return pick(pair, place, 0), sends
    own, *sends = call(
        functools.partial(fold_core_kernel, (dp_count, depth)), "fold_core", [spot],
        [kept, received], [(shape, FULL)] + [(shape, LOW)] * (dp_count - 1), kept.size,
    )
    return own, sends


def fold_square(spot, kept, received):
    dp_count, depth = lax.axis_size("dp"), lax.axis_size("fsdp") // 2
    shape = kept.shape[1:]
    if kept.shape[1] % 16:
        place = lax.axis_index("fsdp") // 2
        square = add_all(kept, received)
        sends = [pick(square, place ^ k, 0).astype(LOW) for k in range(1, depth)]
        return pick(square, place, 0), sends
    own, *sends = call(
        functools.partial(fold_square_kernel, (dp_count, depth)), "fold_square", [spot],
        [kept, *received], [(shape, FULL)] + [(shape, LOW)] * (depth - 1), kept.size,
    )
    return own, sends


def move_square(sends):
    stride = lax.axis_size("fsdp")
    return [exchange(item, stride * (k + 1)) for k, item in enumerate(sends)]


def move_layers(sends):
    return [exchange(item, 2 * (k + 1)) for k, item in enumerate(sends)]


def add_all(kept, moved):
    for item in moved:
        kept = kept + item.astype(FULL)
    return kept


def body(
    tokens,
    encoded,
    cotangent,
    target_ids,
    source_ids,
    qkv_master,
    qkv_first,
    qkv_second,
    out_master,
    out_first,
    out_second,
    ffn_in_master,
    ffn_in_first,
    ffn_in_second,
    ffn_out_master,
    ffn_out_first,
    ffn_out_second,
    vector_master,
    vector_first,
    vector_second,
):
    total, model = tokens.shape
    dp_count, fsdp_count = lax.axis_size("dp"), lax.axis_size("fsdp")
    count, depth = dp_count * fsdp_count, fsdp_count // 2
    rows = model // count
    aligned = rows % 16 == 0
    place = lax.axis_index("dp") * fsdp_count + lax.axis_index("fsdp")
    spot = place.reshape(1).astype(jnp.int32)
    low_qkv = after(qkv_master, spot).astype(LOW)
    low_out = out_master.astype(LOW)
    low_vector = jnp.pad(vector_master.astype(LOW).T, ((0, 0), (0, 128 - vector_master.shape[0])))
    pieces = ffn_in_master.shape[1] // model

    def to_columns(values):
        return values.reshape(-1, rows, model).transpose(1, 0, 2).reshape(rows, -1)

    self_piece = jnp.concatenate([low_qkv[0], low_qkv[1], low_qkv[2], low_vector], axis=1)
    cross_piece = jnp.concatenate([low_out[0], low_qkv[3], low_qkv[4], low_qkv[5], low_out[1]], axis=1)
    ffn_piece = jnp.concatenate(
        [ffn_in_master.astype(LOW), to_columns(ffn_out_master.astype(LOW))], axis=1
    )
    row_starts, col_starts = segment_starts(target_ids[0]), segment_starts(source_ids[0])

    def sources_of(parts):
        if aligned:
            return parts
        flat = ordered(parts, place)
        return [flat.reshape(model, -1)]

    def ffn_sources_of(parts):
        if aligned:
            return parts
        flat = ordered(parts, place)
        width = pieces * model
        second = flat[:, :, width:].reshape(count, rows, pieces, model).transpose(0, 2, 1, 3)
        second = second.reshape(pieces, model, model).transpose(1, 0, 2).reshape(model, -1)
        return [jnp.concatenate([flat[:, :, :width].reshape(model, -1), second], axis=1)]

    wide, tall, thin = ((total, model), LOW), ((total, model), FULL), ((total, 1), FULL)
    log_sums = ((SEGMENTS, model // 256, 1, 1024), FULL)
    small = ((8, model), FULL)
    unit = 2 * total * model * model
    attend = 2 * SEGMENTS * HEADS * 256 * 256 * 256
    wait_one, wait_two = pltpu.SemaphoreType.DMA((1,)), pltpu.SemaphoreType.DMA((2,))

    def grad_outs(columns):
        if aligned:
            return [((count // 2, rows, columns), LOW)] * 2
        return [((model, columns), LOW)]

    self_stack = layer_stack(self_piece)
    later = after(jnp.concatenate([cross_piece, ffn_piece], axis=1), self_stack)
    self_near = square_list(self_stack)
    later_stack = layer_stack(later)
    self_parts = core_list(self_near)
    cross_columns = cross_piece.shape[1]
    cross_own, ffn_own = later_stack[:, :, :cross_columns], later_stack[:, :, cross_columns:]
    cross_near = square_list(cross_own)
    ffn_near = forward_list(ffn_own)

    sources = sources_of(self_parts)
    (
        self_weights, vectors, queries, keys, values, mixed, self_sums,
    ) = call(
        functools.partial(self_forward_kernel, len(sources), depth), "self_forward",
        [spot, row_starts], [after(tokens, cross_own, ffn_own)],
        [
            keep(((model, self_piece.shape[1]), LOW)), ((24, model), FULL),
            keep(wide), keep(wide), keep(wide), keep(wide), keep(log_sums),
        ],
        3 * unit + 2 * attend, sources, [wait_one],
    )
    ffn_near = forward_rest(ffn_near, mixed)
    sources = sources_of(core_list([after(item, mixed) for item in cross_near]))
    (
        cross_weights, unit_one, inverse_one, first_low, cross_queries, cross_keys, cross_values,
        cross_mixed, cross_log,
    ) = call(
        functools.partial(cross_forward_kernel, len(sources), depth), "cross_forward",
        [spot, row_starts, col_starts], [tokens, encoded, mixed, vectors],
        [
            keep(((model, cross_columns), LOW)), keep(tall), thin, keep(wide), keep(wide),
            keep(wide), keep(wide), keep(wide), keep(log_sums),
        ],
        4 * unit + 2 * attend, sources, [wait_one],
    )

    def weight_block(weights, index):
        return (weights, (model, model), (0, index))

    whole_vectors = (vectors, vectors.shape, (0, 0))
    unit_two, inverse_two = blocked(
        cross_finish_kernel, "cross_finish", [unit_one, cross_mixed],
        [weight_block(cross_weights, 4), whole_vectors], [tall, thin], unit,
    )
    gates = [mixed] * (dp_count // 2) + [cross_mixed] * (dp_count // 2)
    sources = ffn_sources_of(core_list([after(*pair) for pair in zip(ffn_near, gates)]))
    hidden = pieces * model
    (
        layer_out, grad_sum, grad_cross_out, grad_cross_mixed, ffn_sums, bias_sums, *ffn_grads
    ) = blocked(
        functools.partial(ffn_kernel, len(sources), depth), "ffn",
        [unit_two, inverse_two, cotangent], [weight_block(cross_weights, 4), whole_vectors],
        [wide, tall, wide, wide], (5 * pieces + 1) * unit, [spot], sources,
        [small, small, *grad_outs(2 * hidden)],
        [
            pltpu.VMEM((model, hidden), LOW), pltpu.VMEM((hidden, model), LOW),
            pltpu.VMEM((total, model), LOW), pltpu.VMEM((total, hidden), LOW),
            pltpu.VMEM((total, model), LOW), pltpu.VMEM((total, hidden), LOW),
            pltpu.VMEM((STEP_ROWS, hidden), FULL), wait_two,
        ],
    )
    if not aligned:
        first, second = ffn_grads[0][:, :hidden], ffn_grads[0][:, hidden:]
        second = second.reshape(model, pieces, model).transpose(1, 0, 2)
        second = second.reshape(count, pieces, rows, model).transpose(0, 2, 1, 3)
        ffn_grads = [jnp.concatenate([first, second.reshape(model, -1)], axis=1)]
    sent, kept = split_core(ffn_grads)
    ffn_moved = exchange(sent, 1)
    cross_dq, cross_dk, cross_dv = call(
        cross_backward_kernel, "cross_backward", [row_starts, col_starts],
        [cross_queries, cross_keys, cross_values, after(grad_cross_mixed, sent), cross_log],
        [keep(wide), keep(wide), keep(wide)], 5 * attend,
    )
    fast = aligned and dp_count == 4 and depth == 4
    ffn_moved = after(ffn_moved, cross_dq)
    if fast:
        pair = (2, depth, rows, hidden)
        keep_first, send_first, keep_second, send_second = call(
            functools.partial(fold_halves_kernel, depth), "fold_halves", [spot], [kept, ffn_moved],
            [(pair, FULL), (pair, LOW), (pair, FULL), (pair, LOW)], 1,
        )
        ffn_sends = [send_first, send_second]
        got_first = exchange(send_first, 2 * fsdp_count)
        got_second = exchange(send_second, fsdp_count)
    else:
        ffn_kept, ffn_sends = fold_core(spot, kept, ffn_moved)
        ffn_moved = move_square(ffn_sends)
    first_sum, self_low, grad_mixed, cross_vector, encoded_grad, *cross_grads = call(
        cross_grads_kernel, "cross_grads", [spot],
        [
            after(cross_dq, *ffn_sends), cross_dk, cross_dv, cross_weights, vectors, grad_sum,
            unit_one, inverse_one, first_low, encoded, cross_mixed, grad_cross_out,
        ],
        [keep(tall), keep(wide), keep(wide), small, tall, *grad_outs(4 * model)], 8 * unit,
    )
    sent, kept = split_core(cross_grads)
    ffn_sends = [sent]
    if fast:
        half = (depth, rows, hidden)
        own_first, send_first, own_second, send_second = call(
            fold_pairs_kernel, "fold_pairs", [],
            [keep_first, after(got_first, sent), keep_second, got_second],
            [(half, FULL), (half, LOW), (half, FULL), (half, LOW)], 1,
        )
        ffn_sends = [send_first, send_second]
        got_first = exchange(send_first, fsdp_count)
        got_second = exchange(send_second, 2 * fsdp_count)
    cross_moved = exchange(after(sent, *ffn_sends), 1)
    cross_kept, cross_sends = fold_core(spot, kept, cross_moved)
    cross_moved = move_square(cross_sends)
    self_dq, self_dk, self_dv, *self_grads = call(
        self_backward_kernel, "self_backward", [spot, row_starts],
        [
            queries, keys, values, after(grad_mixed, *cross_sends, *ffn_sends), self_sums,
            tokens, mixed, self_low, cross_vector, ffn_sums, bias_sums,
        ],
        [keep(wide), keep(wide), keep(wide), *grad_outs(4 * model + 128)],
        5 * attend + 4 * unit, (), [pltpu.VMEM((128, model), FULL)],
    )
    sent, kept = split_core(self_grads)
    if fast:
        wide_pair = (2, rows, 2 * hidden + 4 * model)
        layer_keep, layer_send = call(
            functools.partial(fold_layers_kernel, depth), "fold_layers", [spot],
            [own_first, after(got_first, sent), own_second, got_second, cross_kept, *cross_moved],
            [(wide_pair, FULL), (wide_pair, LOW)], 1,
        )
        ffn_sends = [layer_send]
        layer_got = exchange(layer_send, 4)
        self_moved = exchange(after(sent, layer_send), 1)
    else:
        self_moved = exchange(sent, 1)
        ffn_kept, ffn_sends = fold_square(spot, ffn_kept, [after(item, sent) for item in ffn_moved])
        ffn_moved = move_layers(ffn_sends)
    (tokens_grad,) = blocked(
        tokens_grad_kernel, "tokens_grad",
        [after(self_dq, *ffn_sends), self_dk, self_dv, first_sum],
        [(self_weights, self_weights.shape, (0, 0))], [tall], 3 * unit,
    )
    self_kept, self_sends = fold_core(spot, kept, after(self_moved, tokens_grad))
    self_moved = move_square(self_sends)
    grad_scale = 1.0 / math.sqrt(total * count)
    if fast:
        wide_row = wide_pair[1:]
        layer_own, layer_send = call(
            fold_last_kernel, "fold_last", [], [layer_keep, after(layer_got, *self_sends)],
            [(wide_row, FULL), (wide_row, LOW)], 1,
        )
        layer_got = exchange(layer_send, 2)
        kinds = [FULL, FULL, FULL, LOW]
        ffn_out_state = (ffn_out_master, ffn_out_first, ffn_out_second)
        ffn_in_state = (ffn_in_master, ffn_in_first, ffn_in_second)
        ffn_new = call(
            functools.partial(ffn_update_kernel, grad_scale), "ffn_update", [],
            [layer_own, layer_got, *ffn_in_state, *ffn_out_state],
            [(ffn_in_master.shape, kind) for kind in kinds]
            + [(ffn_out_master.shape, kind) for kind in kinds], 1,
        )
        self_kept, self_sends = fold_square(
            spot, self_kept, [after(item, layer_send) for item in self_moved]
        )
        self_moved = move_layers(self_sends)
        states = [
            qkv_master, qkv_first, qkv_second, out_master, out_first, out_second,
            vector_master.T, vector_first.T, vector_second.T,
        ]
        final_new = call(
            functools.partial(final_update_kernel, grad_scale, 2 * hidden), "final_update", [],
            [layer_own, layer_got, self_kept, *self_moved, *states],
            [(item.shape, kind) for item in states[::3] for kind in kinds], 1,
        )
        return (
            layer_out, tokens_grad, encoded_grad, *final_new[:8], *ffn_new,
            *[item.T for item in final_new[8:]],
        )
    cross_kept, cross_sends = fold_square(
        spot, cross_kept, [after(item, *self_sends) for item in cross_moved]
    )
    cross_moved = move_layers(cross_sends)
    ffn_total = add_all(ffn_kept, ffn_moved)
    cross_total = add_all(cross_kept, cross_moved)
    self_kept, self_sends = fold_square(
        spot, self_kept, [after(item, *cross_sends) for item in self_moved]
    )
    self_moved = move_layers(self_sends)
    self_total = add_all(self_kept, self_moved)

    def block(values, index):
        return values[:, index * model : (index + 1) * model]

    summed_qkv = jnp.stack(
        [block(self_total, i) for i in range(3)] + [block(cross_total, i) for i in range(3)]
    )
    summed_out = jnp.stack([block(self_total, 3), block(cross_total, 3)])
    summed_ffn_in = ffn_total[:, :hidden]
    summed_ffn_out = (
        ffn_total[:, hidden:].reshape(rows, pieces, model).transpose(1, 0, 2).reshape(-1, model)
    )
    summed_vector = self_total[:, 4 * model : 4 * model + vector_master.shape[0]].T
    qkv_first_new, qkv_second_new, qkv_master_new, qkv_copy = adamw(
        qkv_master, summed_qkv * grad_scale, qkv_first, qkv_second, 0.04
    )
    out_first_new, out_second_new, out_master_new, out_copy = adamw(
        out_master, summed_out * grad_scale, out_first, out_second, 0.3
    )
    ffn_in_first_new, ffn_in_second_new, ffn_in_master_new, ffn_in_copy = adamw(
        ffn_in_master, summed_ffn_in * grad_scale, ffn_in_first, ffn_in_second, 0.04
    )
    ffn_out_first_new, ffn_out_second_new, ffn_out_master_new, ffn_out_copy = adamw(
        ffn_out_master, summed_ffn_out * grad_scale, ffn_out_first, ffn_out_second, 0.02
    )
    vector_first_new, vector_second_new, vector_master_new, vector_copy = adamw(
        vector_master, summed_vector * grad_scale, vector_first, vector_second, 0.35
    )
    return (
        layer_out,
        tokens_grad,
        encoded_grad,
        qkv_first_new,
        qkv_second_new,
        qkv_master_new,
        qkv_copy,
        out_first_new,
        out_second_new,
        out_master_new,
        out_copy,
        ffn_in_first_new,
        ffn_in_second_new,
        ffn_in_master_new,
        ffn_in_copy,
        ffn_out_first_new,
        ffn_out_second_new,
        ffn_out_master_new,
        ffn_out_copy,
        vector_first_new,
        vector_second_new,
        vector_master_new,
        vector_copy,
    )


def solution(mesh):
    return jax.shard_map(
        body,
        mesh=mesh,
        in_specs=(
            P(("dp", "fsdp"), None),
            P(("dp", "fsdp"), None),
            P(("dp", "fsdp"), None),
            P(("dp", "fsdp"), None),
            P(("dp", "fsdp"), None),
            P(None, ("dp", "fsdp"), None),
            P(None, ("dp", "fsdp"), None),
            P(None, ("dp", "fsdp"), None),
            P(None, ("dp", "fsdp"), None),
            P(None, ("dp", "fsdp"), None),
            P(None, ("dp", "fsdp"), None),
            P(("dp", "fsdp"), None),
            P(("dp", "fsdp"), None),
            P(("dp", "fsdp"), None),
            P(("dp", "fsdp"), None),
            P(("dp", "fsdp"), None),
            P(("dp", "fsdp"), None),
            P(None, ("dp", "fsdp")),
            P(None, ("dp", "fsdp")),
            P(None, ("dp", "fsdp")),
        ),
        out_specs=(
            P(("dp", "fsdp"), None),
            P(("dp", "fsdp"), None),
            P(("dp", "fsdp"), None),
            P(None, ("dp", "fsdp"), None),
            P(None, ("dp", "fsdp"), None),
            P(None, ("dp", "fsdp"), None),
            P(None, ("dp", "fsdp"), None),
            P(None, ("dp", "fsdp"), None),
            P(None, ("dp", "fsdp"), None),
            P(None, ("dp", "fsdp"), None),
            P(None, ("dp", "fsdp"), None),
            P(("dp", "fsdp"), None),
            P(("dp", "fsdp"), None),
            P(("dp", "fsdp"), None),
            P(("dp", "fsdp"), None),
            P(("dp", "fsdp"), None),
            P(("dp", "fsdp"), None),
            P(("dp", "fsdp"), None),
            P(("dp", "fsdp"), None),
            P(None, ("dp", "fsdp")),
            P(None, ("dp", "fsdp")),
            P(None, ("dp", "fsdp")),
            P(None, ("dp", "fsdp")),
        ),
        check_vma=False,
    )
```

```python
import functools
import math

import jax
import jax.numpy as jnp
from jax import lax
from jax.experimental import pallas as pl
from jax.experimental.pallas import tpu as pltpu
from jax.sharding import PartitionSpec as P

HEADS = 8
STEP = 5
SEGMENTS = 10
norm_eps = 1e-05
beta_first = 0.5
beta_second = 0.5
adam_eps = 1e-08
weight_decay = 0.01
mask_fill = -1000000000.0
LOW = jnp.bfloat16
FULL = jnp.float32


def dot_nn(left, right):
    return lax.dot_general(left, right, (((1,), (0,)), ((), ())), preferred_element_type=FULL)


def dot_nt(left, right):
    return lax.dot_general(left, right, (((1,), (1,)), ((), ())), preferred_element_type=FULL)


def dot_tn(left, right):
    return lax.dot_general(left, right, (((0,), (0,)), ((), ())), preferred_element_type=FULL)


def head_masks(width, group, factor):
    lane = lax.broadcasted_iota(jnp.int32, (1, group * width), 1) // width
    return [jnp.where(lane == h, factor, 0.0).astype(LOW) for h in range(group)]


def window(start, size, total):
    return pl.multiple_of(jnp.minimum(start // 16 * 16, total - size), 16)


def inside(base, size, begin, end):
    place = lax.broadcasted_iota(jnp.int32, (size, 1), 0) + base
    return (place >= begin) & (place < end)


def each_span(row_starts, col_starts, total, same, work):
    def segment(s, carry):
        row_begin, row_end = row_starts[s], row_starts[s + 1]
        col_begin, col_end = col_starts[s], col_starts[s + 1]
        row_short = row_end - window(row_begin, 128, total) <= 128
        col_short = col_end - window(col_begin, 128, total) <= 128
        for row_span in (128, 256):
            for col_span in (128, 256):
                if same and row_span != col_span:
                    continue
                wanted = row_short if row_span == 128 else jnp.logical_not(row_short)
                if not same:
                    other = col_short if col_span == 128 else jnp.logical_not(col_short)
                    wanted = jnp.logical_and(wanted, other)

                @pl.when(wanted)
                def _(row_span=row_span, col_span=col_span):
                    row_base = window(row_begin, row_span, total)
                    col_base = window(col_begin, col_span, total)
                    work(
                        s,
                        pl.ds(row_base, row_span),
                        pl.ds(col_base, col_span),
                        inside(row_base, row_span, row_begin, row_end),
                        inside(col_base, col_span, col_begin, col_end),
                        row_span,
                    )

        return carry

    lax.fori_loop(0, SEGMENTS, segment, 0)


def attend_forward(row_starts, col_starts, q_ref, k_ref, v_ref, out_ref, sums_ref):
    total, model = q_ref.shape
    width = model // HEADS
    group = 256 // width
    scales = head_masks(width, group, 1.0 / math.sqrt(width))
    parts = [slice(g * 256, (g + 1) * 256) for g in range(HEADS // group)]

    def work(s, rows, cols, row_mask, col_mask, span):
        raw = []
        for lanes in parts:
            query, keys = q_ref[rows, lanes], k_ref[cols, lanes]
            stacked = jnp.concatenate([query * scale for scale in scales], axis=0)
            raw.append(dot_nt(keys, stacked))
        turned = [v_ref[cols, lanes].T for lanes in parts]
        probs = []
        for g, item in enumerate(raw):
            scores = jnp.where(col_mask, item, mask_fill)
            largest = jnp.max(scores, axis=0, keepdims=True)
            expo = jnp.exp(scores - largest)
            totals = jnp.sum(expo, axis=0, keepdims=True)
            sums_ref[s, g, :, : group * span] = largest + jnp.log(totals)
            probs.append((expo * (1.0 / totals)).astype(LOW))
        mixed = [
            [
                dot_nn(side[h * width : (h + 1) * width], prob[:, h * span : (h + 1) * span])
                for h in range(group)
            ]
            for side, prob in zip(turned, probs)
        ]
        for lanes, items in zip(parts, mixed):
            value = jnp.concatenate(items, axis=0).T
            old = out_ref[rows, lanes].astype(FULL)
            out_ref[rows, lanes] = jnp.where(row_mask, value, old).astype(LOW)

    each_span(row_starts, col_starts, total, row_starts is col_starts, work)


def attend_backward(
    row_starts, col_starts, q_ref, k_ref, v_ref, grad_ref, sums_ref, dq_ref, dk_ref, dv_ref
):
    total, model = q_ref.shape
    width = model // HEADS
    group = 256 // width
    factor = 1.0 / math.sqrt(width)
    scales = head_masks(width, group, factor)
    picks = head_masks(width, group, 1.0)
    parts = [slice(g * 256, (g + 1) * 256) for g in range(HEADS // group)]

    def work(s, rows, cols, row_mask, col_mask, span):
        stacks, grads, raw, grad_probs = [], [], [], []
        for lanes in parts:
            query, keys, values = q_ref[rows, lanes], k_ref[cols, lanes], v_ref[cols, lanes]
            grad = jnp.where(row_mask, grad_ref[rows, lanes].astype(FULL), 0.0).astype(LOW)
            stacks.append(jnp.concatenate([query * scale for scale in scales], axis=0))
            grads.append(jnp.concatenate([grad * item for item in picks], axis=0))
            raw.append(dot_nt(keys, stacks[-1]))
            grad_probs.append(dot_nt(values, grads[-1]))
        grad_values, grad_scores = [], []
        for g, (item, grad_prob) in enumerate(zip(raw, grad_probs)):
            scores = jnp.where(col_mask, item, mask_fill)
            probs = jnp.exp(scores - sums_ref[s, g, :, : group * span])
            grad_values.append(dot_nn(probs.astype(LOW), grads[g]))
            weighted = probs * grad_prob
            inner = jnp.sum(weighted, axis=0, keepdims=True)
            grad_scores.append((weighted - probs * inner).astype(LOW))
        grad_keys, grad_queries = [], []
        for lanes, item, stacked in zip(parts, grad_scores, stacks):
            grad_keys.append(dot_nn(item, stacked))
            turned = k_ref[cols, lanes].T
            grad_queries.append(
                [
                    dot_nn(turned[h * width : (h + 1) * width], item[:, h * span : (h + 1) * span])
                    for h in range(group)
                ]
            )
        for g, lanes in enumerate(parts):
            grad_query = jnp.concatenate(grad_queries[g], axis=0).T * factor
            for ref, place, mask, value in (
                (dq_ref, rows, row_mask, grad_query),
                (dk_ref, cols, col_mask, grad_keys[g]),
                (dv_ref, cols, col_mask, grad_values[g]),
            ):
                old = ref[place, lanes].astype(FULL)
                ref[place, lanes] = jnp.where(mask, value, old).astype(LOW)

    each_span(row_starts, col_starts, total, row_starts is col_starts, work)


def normalize(values):
    center = values - jnp.mean(values, axis=-1, keepdims=True)
    inverse = lax.rsqrt(jnp.mean(center * center, axis=-1, keepdims=True) + norm_eps)
    return center * inverse, inverse


def normalize_back(grad, gain, unit, inverse):
    scaled = grad * (1.0 + gain)
    mean = jnp.mean(scaled, axis=-1, keepdims=True)
    along = jnp.mean(scaled * unit, axis=-1, keepdims=True)
    return (scaled - mean - unit * along) * inverse


def column_sum(values):
    return jnp.sum(values.astype(FULL), axis=0, keepdims=True)


STEP_ROWS = 512


def row_steps(total, step):
    def run(i, carry):
        step(pl.ds(pl.multiple_of(i * STEP_ROWS, STEP_ROWS), STEP_ROWS))
        return carry

    lax.fori_loop(0, total // STEP_ROWS, run, 0)


def load_weights(place, depth, sources, targets, semaphores):
    if len(sources) == 1:
        offset = 0
        for target, semaphore in zip(targets, semaphores):
            source = sources[0].at[:, offset : offset + target.shape[1]]
            offset += target.shape[1]
            pltpu.make_async_copy(source, target, semaphore).start()
        return
    half = len(sources) // 2
    for k, source in enumerate(sources):
        base = (k % half) * 2 * depth + k // half
        for layer in range(depth):
            other = place ^ (base + 2 * layer)
            offset = 0
            for target, semaphore in zip(targets, semaphores):
                rows = source.shape[1]
                span = target.shape[1]
                to_rows = pl.ds(pl.multiple_of(other * rows, rows), rows)
                pltpu.make_async_copy(
                    source.at[layer, :, offset : offset + span], target.at[to_rows, :], semaphore
                ).start()
                offset += span


def await_weights(target, semaphore):
    pltpu.make_async_copy(target, target, semaphore).wait()


def store_grad(refs, core, lanes, value):
    value = value.astype(LOW)
    if len(refs) == 1:
        refs[0][:, lanes] = value
        return
    sent, kept = refs
    chips, rows = kept.shape[0], kept.shape[1]
    parts = value.reshape(chips, 2, rows, value.shape[1])
    first = core == 0
    kept[:, :, lanes] = jnp.where(first, parts[:, 0], parts[:, 1])
    sent[:, :, lanes] = jnp.where(first, parts[:, 1], parts[:, 0])


def self_forward_kernel(count, depth, place, row_starts, tokens, *rest):
    sources = rest[:count]
    weights, vectors, queries, keys, values, mixed, sums, semaphores = rest[count:]
    model = tokens.shape[1]
    load_weights(place[0], depth, sources, [weights], [semaphores.at[0]])
    await_weights(weights, semaphores.at[0])
    turned = weights[:, 3 * model : 3 * model + 128].astype(FULL).T
    vectors[...] = turned[: vectors.shape[0]]

    def project(rows):
        block = tokens[rows, :]
        queries[rows, :] = (dot_nn(block, weights[:, :model]) + vectors[0:1, :]).astype(LOW)
        keys[rows, :] = dot_nn(block, weights[:, model : 2 * model]).astype(LOW)
        values[rows, :] = (
            dot_nn(block, weights[:, 2 * model : 3 * model]) + vectors[1:2, :]
        ).astype(LOW)

    row_steps(tokens.shape[0], project)
    attend_forward(row_starts, row_starts, queries, keys, values, mixed, sums)


def cross_project_kernel(count, depth, place, tokens, encoded, mixed, vectors, *rest):
    sources = rest[:count]
    weights, unit_one, inverse_one, queries, keys, values, semaphores = rest[count:]
    model = tokens.shape[1]
    load_weights(place[0], depth, sources, [weights], [semaphores.at[0]])
    await_weights(weights, semaphores.at[0])

    def project(rows):
        block = encoded[rows, :]
        keys[rows, :] = dot_nn(block, weights[:, 2 * model : 3 * model]).astype(LOW)
        values[rows, :] = (
            dot_nn(block, weights[:, 3 * model : 4 * model]) + vectors[4:5, :]
        ).astype(LOW)
        summed = tokens[rows, :].astype(FULL) + dot_nn(mixed[rows, :], weights[:, :model])
        unit, inverse = normalize(summed + vectors[2:3, :])
        unit_one[rows, :] = unit
        inverse_one[rows, :] = inverse
        low = (unit * (1.0 + vectors[7:8, :]) + vectors[10:11, :]).astype(LOW)
        queries[rows, :] = (dot_nn(low, weights[:, model : 2 * model]) + vectors[3:4, :]).astype(LOW)

    row_steps(tokens.shape[0], project)


def cross_attend_kernel(row_starts, col_starts, queries, keys, values, cross_mixed, sums):
    attend_forward(row_starts, col_starts, queries, keys, values, cross_mixed, sums)


def cross_finish_kernel(unit_one, cross_mixed, weights, vectors, unit_two, inverse_two):
    first = unit_one[...] * (1.0 + vectors[7:8, :]) + vectors[10:11, :]
    model = cross_mixed.shape[1]
    summed = first + dot_nn(cross_mixed[...], weights[:, 4 * model : 5 * model]) + vectors[5:6, :]
    unit, inverse = normalize(summed)
    unit_two[...] = unit
    inverse_two[...] = inverse


gelu_scale = math.sqrt(2.0 / math.pi)
gelu_cubic = 0.044715


def ffn_kernel(count, depth, place, unit_two, inverse_two, cotangent, weights, vectors, *rest):
    sources = rest[:count]
    (
        layer_out, grad_sum, grad_out, grad_mixed, sums, bias_sums, *grads,
        first_weights, second_weights, hidden, grad_ffn, grad_pre, slopes, semaphores,
    ) = rest[count:]
    model = unit_two.shape[1]
    pieces = first_weights.shape[1] // model
    load_ffn(place[0], depth, sources, first_weights, second_weights, semaphores)
    sums[...] = jnp.zeros_like(sums)
    bias_sums[...] = jnp.zeros_like(bias_sums)
    await_weights(first_weights, semaphores.at[0])
    await_weights(second_weights, semaphores.at[1])

    def step(rows):
        unit = unit_two[rows, :]
        second = unit * (1.0 + vectors[8:9, :]) + vectors[11:12, :]
        low = second.astype(LOW)
        total = second + vectors[6:7, :]
        for j in range(pieces):
            lanes = slice(j * model, (j + 1) * model)
            pre = dot_nn(low, first_weights[:, lanes]) + vectors[13 + j : 14 + j, :]
            square = pre * pre
            bend = jnp.tanh(gelu_scale * pre * (1.0 + gelu_cubic * square))
            half = 0.5 * (1.0 + bend)
            value = (pre * half).astype(LOW)
            hidden[rows, lanes] = value
            inner = gelu_scale * (1.0 + 3.0 * gelu_cubic * square)
            slopes[:, lanes] = half + 0.5 * pre * (1.0 - bend * bend) * inner
            total = total + dot_nn(value, second_weights[lanes, :])
        unit_three, inverse_three = normalize(total)
        layer_out[rows, :] = (unit_three * (1.0 + vectors[9:10, :]) + vectors[12:13, :]).astype(LOW)
        upper = cotangent[rows, :].astype(FULL)
        third = normalize_back(upper, vectors[9:10, :], unit_three, inverse_three)
        third_low = third.astype(LOW)
        grad_ffn[rows, :] = third_low
        sums[0:1, :] += column_sum(third_low)
        sums[1:2, :] += column_sum(upper * unit_three)
        sums[2:3, :] += column_sum(upper)
        below = third
        for j in range(pieces):
            lanes = slice(j * model, (j + 1) * model)
            pre = (dot_nt(third_low, second_weights[lanes, :]) * slopes[:, lanes]).astype(LOW)
            grad_pre[rows, lanes] = pre
            bias_sums[j : j + 1, :] += column_sum(pre)
            below = below + dot_nt(pre, first_weights[:, lanes])
        sums[3:4, :] += column_sum(below * unit)
        sums[4:5, :] += column_sum(below)
        second_sum = normalize_back(below, vectors[8:9, :], unit, inverse_two[rows, :])
        grad_sum[rows, :] = second_sum
        out_low = second_sum.astype(LOW)
        grad_out[rows, :] = out_low
        sums[5:6, :] += column_sum(out_low)
        grad_mixed[rows, :] = dot_nt(out_low, weights[:, 4 * model : 5 * model]).astype(LOW)

    row_steps(unit_two.shape[0], step)
    core = place[0] % 2
    second_low = (unit_two[...] * (1.0 + vectors[8:9, :]) + vectors[11:12, :]).astype(LOW)
    for j in range(pieces):
        lanes = slice(j * model, (j + 1) * model)
        store_grad(grads, core, lanes, dot_tn(second_low, grad_pre[:, lanes]))
    span = second_weights.shape[0] // pieces
    for j in range(pieces):
        value = dot_tn(hidden[:, j * span : (j + 1) * span], grad_ffn[...])
        store_ffn_out(grads, core, j, pieces, value)


def load_ffn(place, depth, sources, first_weights, second_weights, semaphores):
    first_width = first_weights.shape[1]
    if len(sources) == 1:
        pltpu.make_async_copy(
            sources[0].at[:, :first_width], first_weights, semaphores.at[0]
        ).start()
        pieces = first_width // first_weights.shape[0]
        model = first_weights.shape[0]
        for j in range(pieces):
            pltpu.make_async_copy(
                sources[0].at[:, first_width + j * model : first_width + (j + 1) * model],
                second_weights.at[pl.ds(j * model, model), :],
                semaphores.at[1],
            ).start()
        return
    half = len(sources) // 2
    model = second_weights.shape[1]
    for k, source in enumerate(sources):
        base = (k % half) * 2 * depth + k // half
        rows = source.shape[1]
        for layer in range(depth):
            other = place ^ (base + 2 * layer)
            to_rows = pl.ds(pl.multiple_of(other * rows, rows), rows)
            pltpu.make_async_copy(
                source.at[layer, :, :first_width], first_weights.at[to_rows, :], semaphores.at[0]
            ).start()
            pieces = first_width // model
            for j in range(pieces):
                start = pl.multiple_of((other * pieces + j) * rows, rows)
                pltpu.make_async_copy(
                    source.at[layer, :, first_width + j * model : first_width + (j + 1) * model],
                    second_weights.at[pl.ds(start, rows), :],
                    semaphores.at[1],
                ).start()


def store_ffn_out(refs, core, block, pieces, value):
    value = value.astype(LOW)
    model = value.shape[1]
    if len(refs) == 1:
        offset = (pieces + block) * model
        refs[0][:, offset : offset + model] = value
        return
    sent, kept = refs
    rows = kept.shape[1]
    chips = kept.shape[0] // pieces
    parts = value.reshape(chips, 2, pieces, rows, model)
    first = core == 0
    for j in range(pieces):
        lanes = slice((pieces + j) * model, (pieces + j + 1) * model)
        place = slice(block * chips, (block + 1) * chips)
        kept[place, :, lanes] = jnp.where(first, parts[:, 0, j], parts[:, 1, j])
        sent[place, :, lanes] = jnp.where(first, parts[:, 1, j], parts[:, 0, j])


def cross_backward_kernel(
    row_starts, col_starts, queries, keys, values, grad_mixed, sums_in, dq, dk, dv
):
    attend_backward(row_starts, col_starts, queries, keys, values, grad_mixed, sums_in, dq, dk, dv)


def cross_grads_kernel(
    place, dq, dk, dv, weights, vectors, grad_sum, unit_one, inverse_one,
    encoded, cross_mixed, grad_out,
    first_sum, self_low, grad_mixed, sums, encoded_grad, *grads,
):
    model = dq.shape[1]
    sums[...] = jnp.zeros_like(sums)

    def finish(rows):
        query, key, value = dq[rows, :], dk[rows, :], dv[rows, :]
        sums[0:1, :] += column_sum(query)
        sums[1:2, :] += column_sum(value)
        encoded_grad[rows, :] = dot_nt(key, weights[:, 2 * model : 3 * model]) + dot_nt(
            value, weights[:, 3 * model : 4 * model]
        )
        upper = grad_sum[rows, :] + dot_nt(query, weights[:, model : 2 * model])
        unit = unit_one[rows, :]
        sums[2:3, :] += column_sum(upper * unit)
        sums[3:4, :] += column_sum(upper)
        below = normalize_back(upper, vectors[7:8, :], unit, inverse_one[rows, :])
        first_sum[rows, :] = below
        low = below.astype(LOW)
        self_low[rows, :] = low
        sums[4:5, :] += column_sum(low)
        grad_mixed[rows, :] = dot_nt(low, weights[:, :model]).astype(LOW)

    row_steps(dq.shape[0], finish)
    core = place[0] % 2
    first_low = (unit_one[...] * (1.0 + vectors[7:8, :]) + vectors[10:11, :]).astype(LOW)
    pairs = ((first_low, dq), (encoded, dk), (encoded, dv), (cross_mixed, grad_out))
    for j, (left, right) in enumerate(pairs):
        lanes = slice(j * model, (j + 1) * model)
        store_grad(grads, core, lanes, dot_tn(left[...], right[...]))


def self_backward_kernel(
    place, row_starts, queries, keys, values, grad_mixed, sums_in, tokens, mixed, self_low,
    cross_sums, ffn_sums, bias_sums, dq, dk, dv, *rest,
):
    *grads, stack = rest
    attend_backward(row_starts, row_starts, queries, keys, values, grad_mixed, sums_in, dq, dk, dv)
    model = dq.shape[1]
    core = place[0] % 2
    pairs = ((tokens, dq), (tokens, dk), (tokens, dv), (mixed, self_low))
    for j, (left, right) in enumerate(pairs):
        lanes = slice(j * model, (j + 1) * model)
        store_grad(grads, core, lanes, dot_tn(left[...], right[...]))
    stack[...] = jnp.zeros_like(stack)
    stack[0:1, :] = column_sum(dq[...])
    stack[1:2, :] = column_sum(dv[...])
    order = (
        (2, cross_sums, 4), (3, cross_sums, 0), (4, cross_sums, 1), (5, ffn_sums, 5),
        (6, ffn_sums, 0), (7, cross_sums, 2), (8, ffn_sums, 3), (9, ffn_sums, 1),
        (10, cross_sums, 3), (11, ffn_sums, 4), (12, ffn_sums, 2),
    )
    for to, ref, at in order:
        stack[to : to + 1, :] = ref[at : at + 1, :]
    extra = bias_sums.shape[0]
    stack[13 : 13 + extra, :] = bias_sums[...]
    start = len(pairs) * model
    store_grad(grads, core, slice(start, start + 128), stack[...].T)


def tokens_grad_kernel(dq, dk, dv, first_sum, weights, tokens_grad):
    model = dq.shape[1]
    below = first_sum[...] + dot_nt(dq[...], weights[:, :model])
    below = below + dot_nt(dk[...], weights[:, model : 2 * model])
    tokens_grad[...] = below + dot_nt(dv[...], weights[:, 2 * model : 3 * model])


def fold_core_kernel(shape, place, kept, received, own, *sends):
    dp_count, depth = shape
    at = place[0] // (2 * depth)
    for k, ref in enumerate((own, *sends)):
        spot = pl.ds((at ^ k) * depth, depth)
        value = kept[spot].astype(FULL) + received[spot].astype(FULL)
        ref[...] = value.astype(ref.dtype)


def fold_square_kernel(shape, place, kept, *rest):
    dp_count, depth = shape
    received, outs = rest[: dp_count - 1], rest[dp_count - 1 :]
    at = place[0] // 2 % depth
    for k, ref in enumerate(outs):
        spot = pl.ds(at ^ k, 1)
        value = kept[spot]
        for item in received:
            value = value + item[spot].astype(FULL)
        ref[...] = value[0].astype(ref.dtype)


def fold_halves_kernel(depth, place, kept, received, keep_first, send_first, keep_second, send_second):
    at = place[0] // (2 * depth)
    half = kept.shape[2] // 2
    low, high = slice(0, half), slice(half, 2 * half)
    for ref, lanes, offsets in (
        (keep_first, low, (0, 1)),
        (send_first, low, (2, 3)),
        (keep_second, high, (0, 2)),
        (send_second, high, (1, 3)),
    ):
        for slot, k in enumerate(offsets):
            spot = pl.ds((at ^ k) * depth, depth)
            value = kept[spot, :, lanes].astype(FULL) + received[spot, :, lanes].astype(FULL)
            ref[slot] = value.astype(ref.dtype)


def fold_pairs_kernel(keep_first, got_first, keep_second, got_second, *outs):
    own_first, send_first, own_second, send_second = outs
    own_first[...] = keep_first[0] + got_first[0].astype(FULL)
    send_first[...] = (keep_first[1] + got_first[1].astype(FULL)).astype(LOW)
    own_second[...] = keep_second[0] + got_second[0].astype(FULL)
    send_second[...] = (keep_second[1] + got_second[1].astype(FULL)).astype(LOW)


def fold_layers_kernel(depth, place, first, got_first, second, got_second, cross, *rest):
    *got_cross, keep, send = rest
    at = place[0] // 2 % depth
    half = first.shape[2]
    for ref, offsets in ((keep, (0, 1)), (send, (2, 3))):
        for slot, k in enumerate(offsets):
            spot = pl.ds(at ^ k, 1)
            value = first[spot] + got_first[spot].astype(FULL)
            ref[slot, :, :half] = value[0].astype(ref.dtype)
            value = second[spot] + got_second[spot].astype(FULL)
            ref[slot, :, half : 2 * half] = value[0].astype(ref.dtype)
            value = cross[spot]
            for item in got_cross:
                value = value + item[spot].astype(FULL)
            ref[slot, :, 2 * half :] = value[0].astype(ref.dtype)


def fold_last_kernel(keep, got, own, send):
    own[...] = keep[0] + got[0].astype(FULL)
    send[...] = (keep[1] + got[1].astype(FULL)).astype(LOW)


def update_into(outs, index, state, grad, rate):
    for ref, value in zip(outs, adamw(state[0][index], grad, state[1][index], state[2][index], rate)):
        ref[index] = value


def ffn_update_kernel(grad_scale, own, got, *rest):
    first_state, second_state, outs = rest[:3], rest[3:6], rest[6:]
    rows, width = first_state[0].shape
    model = second_state[0].shape[1]
    grad = (own[:, :width] + got[:, :width].astype(FULL)) * grad_scale
    update_into(outs[:4], (slice(None), slice(None)), first_state, grad, 0.04)
    for j in range(second_state[0].shape[0] // rows):
        lanes = slice(width + j * model, width + (j + 1) * model)
        grad = (own[:, lanes] + got[:, lanes].astype(FULL)) * grad_scale
        index = (slice(j * rows, (j + 1) * rows), slice(None))
        update_into(outs[4:], index, second_state, grad, 0.02)


def final_update_kernel(grad_scale, start, own, got, kept, *rest):
    moved, states, outs = rest[:-21], rest[-21:-12], rest[-12:]
    qkv_state, out_state, vector_state = states[:3], states[3:6], states[6:]
    model = qkv_state[0].shape[2]

    def self_grad(lanes):
        value = kept[:, lanes]
        for item in moved:
            value = value + item[:, lanes].astype(FULL)
        return value * grad_scale

    def cross_grad(index):
        lanes = slice(start + index * model, start + (index + 1) * model)
        return (own[:, lanes] + got[:, lanes].astype(FULL)) * grad_scale

    for j in range(4):
        grad = self_grad(slice(j * model, (j + 1) * model))
        if j < 3:
            update_into(outs[:4], j, qkv_state, grad, 0.04)
            update_into(outs[:4], 3 + j, qkv_state, cross_grad(j), 0.04)
        else:
            update_into(outs[4:8], 0, out_state, grad, 0.3)
            update_into(outs[4:8], 1, out_state, cross_grad(j), 0.3)
    grad = self_grad(slice(4 * model, 4 * model + vector_state[0].shape[1]))
    update_into(outs[8:], (slice(None), slice(None)), vector_state, grad, 0.35)


LIMITS = {
    "fold_halves": 16,
    "fold_pairs": 14,
    "fold_layers": 12,
    "fold_last": 8,
    "ffn_update": 8,
    "final_update": 10,
    "fold_core": 12,
    "fold_square": 10,
    "self_forward": 14,
    "cross_project": 14,
    "cross_attend": 10,
    "cross_finish": 9,
    "ffn": 32,
    "cross_backward": 11,
    "cross_grads": 20,
    "self_backward": 16,
    "tokens_grad": 11,
}


def out_kind(item):
    if len(item) == 3:
        return pltpu.VMEM(item[0], item[1])
    return jax.ShapeDtypeStruct(*item)


def keep(item):
    return (item[0], item[1], True)


def limit(name):
    return pltpu.CompilerParams(vmem_limit_bytes=LIMITS[name] << 20)


def pinned(sources):
    if len(sources) == 1:
        return sources
    return [pltpu.with_memory_space_constraint(item, pltpu.VMEM) for item in sources]


def source_spec(sources):
    return pl.BlockSpec(memory_space=pltpu.VMEM if len(sources) > 1 else pl.ANY)


def call(kernel, name, scalars, arrays, outs, flops, sources=(), scratch=()):
    specs = [pl.BlockSpec(memory_space=pltpu.SMEM)] * len(scalars)
    specs += [pl.BlockSpec(memory_space=pltpu.VMEM)] * len(arrays)
    specs += [source_spec(sources)] * len(sources)
    shapes = [out_kind(item) for item in outs]
    moved = sum(item.size * item.dtype.itemsize for item in [*arrays, *sources])
    return pl.pallas_call(
        kernel,
        out_shape=shapes,
        in_specs=specs,
        out_specs=[pl.BlockSpec(memory_space=pltpu.VMEM)] * len(outs),
        scratch_shapes=list(scratch),
        compiler_params=limit(name),
        cost_estimate=pl.CostEstimate(flops=flops, transcendentals=0, bytes_accessed=moved),
        name=name,
    )(*scalars, *arrays, *pinned(sources))


def segment_starts(ids):
    marks = jnp.arange(SEGMENTS + 1, dtype=ids.dtype)
    return jnp.sum((ids[None, :] < marks[:, None]).astype(jnp.int32), axis=1)


def adamw(master, grad, first, second, rate):
    first_new = beta_first * first + (1.0 - beta_first) * grad
    second_new = beta_second * second + (1.0 - beta_second) * grad * grad
    first_hat = first_new / (1.0 - beta_first**STEP)
    second_hat = second_new / (1.0 - beta_second**STEP)
    master_new = master - rate * (
        first_hat / (jnp.sqrt(second_hat) + adam_eps) + weight_decay * master
    )
    return (first_new, second_new, master_new, master_new.astype(jnp.bfloat16))


AXES = ("dp", "fsdp")


def exchange(values, offset):
    count = lax.axis_size("dp") * lax.axis_size("fsdp")
    return lax.ppermute(values, AXES, [(i, i ^ offset) for i in range(count)])


def after(value, *others):
    return lax.optimization_barrier((value, *others))[0]


def layer_stack(piece):
    depth = lax.axis_size("fsdp") // 2
    return jnp.stack([piece] + [exchange(piece, 2 * k) for k in range(1, depth)])


def layer_double(piece, gate=None):
    stack, step = piece[None], 1
    while step < lax.axis_size("fsdp") // 2:
        if gate is not None and step > 1:
            stack = after(stack, gate)
        stack = jnp.concatenate([stack, exchange(stack, 2 * step)])
        step *= 2
    return stack


def square_list(stack):
    dp_count, fsdp_count = lax.axis_size("dp"), lax.axis_size("fsdp")
    return [stack] + [exchange(stack, fsdp_count * k) for k in range(1, dp_count)]


def forward_list(stack):
    stride, near = lax.axis_size("fsdp"), [stack]
    for k in range(1, lax.axis_size("dp")):
        near.append(None if k & (k - 1) else exchange(stack, stride * k))
    return near


def forward_rest(near, gate):
    stride = lax.axis_size("fsdp")
    for k, item in enumerate(near):
        if item is None:
            high = 1 << (k.bit_length() - 1)
            near[k] = exchange(after(near[k - high], gate), stride * high)
    return near


def core_list(near):
    return near + [exchange(item, 1) for item in near]


def ordered(parts, place):
    half = len(parts) // 2
    both = jnp.stack([jnp.stack(parts[:half]), jnp.stack(parts[half:])], axis=2)
    flat = both.reshape((-1,) + both.shape[3:])
    return flat[jnp.arange(flat.shape[0]) ^ place]


def pick(values, index, axis):
    return lax.dynamic_index_in_dim(values, index, axis, keepdims=False)


def split_core(grads):
    if len(grads) == 2:
        return grads
    count = lax.axis_size("dp") * lax.axis_size("fsdp")
    core = lax.axis_index("fsdp") % 2
    parts = grads[0].reshape((count // 2, 2, -1) + grads[0].shape[1:])
    return pick(parts, 1 - core, 1), pick(parts, core, 1)


def fold_core(spot, kept, received):
    dp_count, depth = lax.axis_size("dp"), lax.axis_size("fsdp") // 2
    shape = (depth,) + kept.shape[1:]
    if kept.shape[1] % 16:
        place = lax.axis_index("dp")
        pair = (kept.astype(FULL) + received.astype(FULL)).reshape((dp_count,) + shape)
        sends = [pick(pair, place ^ k, 0).astype(LOW) for k in range(1, dp_count)]
        return pick(pair, place, 0), sends
    own, *sends = call(
        functools.partial(fold_core_kernel, (dp_count, depth)), "fold_core", [spot],
        [kept, received], [(shape, FULL)] + [(shape, LOW)] * (dp_count - 1), kept.size,
    )
    return own, sends


def fold_square(spot, kept, received):
    dp_count, depth = lax.axis_size("dp"), lax.axis_size("fsdp") // 2
    shape = kept.shape[1:]
    if kept.shape[1] % 16:
        place = lax.axis_index("fsdp") // 2
        square = add_all(kept, received)
        sends = [pick(square, place ^ k, 0).astype(LOW) for k in range(1, depth)]
        return pick(square, place, 0), sends
    own, *sends = call(
        functools.partial(fold_square_kernel, (dp_count, depth)), "fold_square", [spot],
        [kept, *received], [(shape, FULL)] + [(shape, LOW)] * (depth - 1), kept.size,
    )
    return own, sends


def move_square(sends):
    stride = lax.axis_size("fsdp")
    return [exchange(item, stride * (k + 1)) for k, item in enumerate(sends)]


def move_layers(sends):
    return [exchange(item, 2 * (k + 1)) for k, item in enumerate(sends)]


def add_all(kept, moved):
    for item in moved:
        kept = kept + item.astype(FULL)
    return kept


def body(
    tokens,
    encoded,
    cotangent,
    target_ids,
    source_ids,
    qkv_master,
    qkv_first,
    qkv_second,
    out_master,
    out_first,
    out_second,
    ffn_in_master,
    ffn_in_first,
    ffn_in_second,
    ffn_out_master,
    ffn_out_first,
    ffn_out_second,
    vector_master,
    vector_first,
    vector_second,
):
    total, model = tokens.shape
    dp_count, fsdp_count = lax.axis_size("dp"), lax.axis_size("fsdp")
    count, depth = dp_count * fsdp_count, fsdp_count // 2
    rows = model // count
    aligned = rows % 16 == 0
    place = lax.axis_index("dp") * fsdp_count + lax.axis_index("fsdp")
    spot = place.reshape(1).astype(jnp.int32)
    low_qkv = after(qkv_master, spot).astype(LOW)
    low_out = out_master.astype(LOW)
    low_vector = jnp.pad(vector_master.astype(LOW).T, ((0, 0), (0, 128 - vector_master.shape[0])))
    pieces = ffn_in_master.shape[1] // model

    def to_columns(values):
        return values.reshape(-1, rows, model).transpose(1, 0, 2).reshape(rows, -1)

    self_piece = jnp.concatenate([low_qkv[0], low_qkv[1], low_qkv[2], low_vector], axis=1)
    cross_piece = jnp.concatenate([low_out[0], low_qkv[3], low_qkv[4], low_qkv[5], low_out[1]], axis=1)
    ffn_piece = jnp.concatenate(
        [ffn_in_master.astype(LOW), to_columns(ffn_out_master.astype(LOW))], axis=1
    )
    row_starts, col_starts = segment_starts(target_ids[0]), segment_starts(source_ids[0])

    def sources_of(parts):
        if aligned:
            return parts
        flat = ordered(parts, place)
        return [flat.reshape(model, -1)]

    def ffn_sources_of(parts):
        if aligned:
            return parts
        flat = ordered(parts, place)
        width = pieces * model
        second = flat[:, :, width:].reshape(count, rows, pieces, model).transpose(0, 2, 1, 3)
        second = second.reshape(pieces, model, model).transpose(1, 0, 2).reshape(model, -1)
        return [jnp.concatenate([flat[:, :, :width].reshape(model, -1), second], axis=1)]

    wide, tall, thin = ((total, model), LOW), ((total, model), FULL), ((total, 1), FULL)
    log_sums = ((SEGMENTS, model // 256, 1, 1024), FULL)
    small = ((8, model), FULL)
    unit = 2 * total * model * model
    attend = 2 * SEGMENTS * HEADS * 256 * 256 * 256
    wait_one, wait_two = pltpu.SemaphoreType.DMA((1,)), pltpu.SemaphoreType.DMA((2,))

    def grad_outs(columns):
        if aligned:
            return [((count // 2, rows, columns), LOW)] * 2
        return [((model, columns), LOW)]

    self_stack = layer_stack(self_piece)
    self_near = square_list(self_stack)
    cross_own = layer_double(after(cross_piece, self_stack))
    ffn_own = layer_double(after(ffn_piece, self_stack), cross_own)
    self_parts = core_list(self_near)
    cross_columns = cross_piece.shape[1]
    cross_near = square_list(cross_own)
    ffn_near = forward_list(ffn_own)

    sources = sources_of(self_parts)
    (
        self_weights, vectors, queries, keys, values, mixed, self_sums,
    ) = call(
        functools.partial(self_forward_kernel, len(sources), depth), "self_forward",
        [spot, row_starts], [after(tokens, cross_own)],
        [
            keep(((model, self_piece.shape[1]), LOW)), ((24, model), FULL),
            keep(wide), keep(wide), keep(wide), keep(wide), keep(log_sums),
        ],
        3 * unit + 2 * attend, sources, [wait_one],
    )
    sources = sources_of(core_list([after(item, mixed) for item in cross_near]))
    cross_weights, unit_one, inverse_one, cross_queries, cross_keys, cross_values = call(
        functools.partial(cross_project_kernel, len(sources), depth), "cross_project", [spot],
        [tokens, encoded, mixed, vectors],
        [
            keep(((model, cross_columns), LOW)), keep(tall), thin, keep(wide), keep(wide),
            keep(wide),
        ],
        4 * unit, sources, [wait_one],
    )
    ffn_near = forward_rest(ffn_near, cross_queries)
    cross_mixed, cross_log = call(
        cross_attend_kernel, "cross_attend", [row_starts, col_starts],
        [cross_queries, cross_keys, cross_values], [keep(wide), keep(log_sums)], 2 * attend,
    )
    unit_two, inverse_two = call(
        cross_finish_kernel, "cross_finish", [], [unit_one, cross_mixed, cross_weights, vectors],
        [keep(tall), thin], unit,
    )
    gates = [mixed] * (dp_count // 2) + [cross_mixed] * (dp_count // 2)
    sources = ffn_sources_of(core_list([after(*pair) for pair in zip(ffn_near, gates)]))
    hidden = pieces * model
    (
        layer_out, grad_sum, grad_cross_out, grad_cross_mixed, ffn_sums, bias_sums, *ffn_grads
    ) = call(
        functools.partial(ffn_kernel, len(sources), depth), "ffn", [spot],
        [unit_two, inverse_two, cotangent, cross_weights, vectors],
        [wide, keep(tall), keep(wide), keep(wide), small, small, *grad_outs(2 * hidden)],
        (5 * pieces + 1) * unit, sources,
        [
            pltpu.VMEM((model, hidden), LOW), pltpu.VMEM((hidden, model), LOW),
            pltpu.VMEM((total, hidden), LOW), pltpu.VMEM((total, model), LOW),
            pltpu.VMEM((total, hidden), LOW),
            pltpu.VMEM((STEP_ROWS, hidden), FULL), wait_two,
        ],
    )
    if not aligned:
        first, second = ffn_grads[0][:, :hidden], ffn_grads[0][:, hidden:]
        second = second.reshape(model, pieces, model).transpose(1, 0, 2)
        second = second.reshape(count, pieces, rows, model).transpose(0, 2, 1, 3)
        ffn_grads = [jnp.concatenate([first, second.reshape(model, -1)], axis=1)]
    sent, kept = split_core(ffn_grads)
    ffn_moved = exchange(sent, 1)
    cross_dq, cross_dk, cross_dv = call(
        cross_backward_kernel, "cross_backward", [row_starts, col_starts],
        [cross_queries, cross_keys, cross_values, after(grad_cross_mixed, sent), cross_log],
        [keep(wide), keep(wide), keep(wide)], 5 * attend,
    )
    fast = aligned and dp_count == 4 and depth == 4
    ffn_moved = after(ffn_moved, cross_dq)
    if fast:
        pair = (2, depth, rows, hidden)
        keep_first, send_first, keep_second, send_second = call(
            functools.partial(fold_halves_kernel, depth), "fold_halves", [spot], [kept, ffn_moved],
            [(pair, FULL), (pair, LOW), (pair, FULL), (pair, LOW)], 1,
        )
        ffn_sends = [send_first, send_second]
        got_first = exchange(send_first, 2 * fsdp_count)
        got_second = exchange(send_second, fsdp_count)
    else:
        ffn_kept, ffn_sends = fold_core(spot, kept, ffn_moved)
        ffn_moved = move_square(ffn_sends)
    first_sum, self_low, grad_mixed, cross_vector, encoded_grad, *cross_grads = call(
        cross_grads_kernel, "cross_grads", [spot],
        [
            after(cross_dq, *ffn_sends), cross_dk, cross_dv, cross_weights, vectors, grad_sum,
            unit_one, inverse_one, encoded, cross_mixed, grad_cross_out,
        ],
        [keep(tall), keep(wide), keep(wide), small, tall, *grad_outs(4 * model)], 8 * unit,
    )
    sent, kept = split_core(cross_grads)
    ffn_sends = [sent]
    if fast:
        half = (depth, rows, hidden)
        own_first, send_first, own_second, send_second = call(
            fold_pairs_kernel, "fold_pairs", [],
            [keep_first, after(got_first, sent), keep_second, got_second],
            [(half, FULL), (half, LOW), (half, FULL), (half, LOW)], 1,
        )
        ffn_sends = [send_first, send_second]
        got_first = exchange(send_first, fsdp_count)
        got_second = exchange(send_second, 2 * fsdp_count)
    cross_moved = exchange(after(sent, *ffn_sends), 1)
    cross_kept, cross_sends = fold_core(spot, kept, cross_moved)
    cross_moved = move_square(cross_sends)
    self_dq, self_dk, self_dv, *self_grads = call(
        self_backward_kernel, "self_backward", [spot, row_starts],
        [
            queries, keys, values, after(grad_mixed, *cross_sends, *ffn_sends), self_sums,
            tokens, mixed, self_low, cross_vector, ffn_sums, bias_sums,
        ],
        [keep(wide), keep(wide), keep(wide), *grad_outs(4 * model + 128)],
        5 * attend + 4 * unit, (), [pltpu.VMEM((128, model), FULL)],
    )
    sent, kept = split_core(self_grads)
    if fast:
        wide_pair = (2, rows, 2 * hidden + 4 * model)
        layer_keep, layer_send = call(
            functools.partial(fold_layers_kernel, depth), "fold_layers", [spot],
            [own_first, after(got_first, sent), own_second, got_second, cross_kept, *cross_moved],
            [(wide_pair, FULL), (wide_pair, LOW)], 1,
        )
        ffn_sends = [layer_send]
        layer_got = exchange(layer_send, 4)
        self_moved = exchange(after(sent, layer_send), 1)
    else:
        self_moved = exchange(sent, 1)
        ffn_kept, ffn_sends = fold_square(spot, ffn_kept, [after(item, sent) for item in ffn_moved])
        ffn_moved = move_layers(ffn_sends)
    (tokens_grad,) = call(
        tokens_grad_kernel, "tokens_grad", [],
        [after(self_dq, *ffn_sends), self_dk, self_dv, first_sum, self_weights], [tall], 3 * unit,
    )
    self_kept, self_sends = fold_core(spot, kept, after(self_moved, tokens_grad))
    self_moved = move_square(self_sends)
    grad_scale = 1.0 / math.sqrt(total * count)
    if fast:
        wide_row = wide_pair[1:]
        layer_own, layer_send = call(
            fold_last_kernel, "fold_last", [], [layer_keep, after(layer_got, *self_sends)],
            [(wide_row, FULL), (wide_row, LOW)], 1,
        )
        layer_got = exchange(layer_send, 2)
        kinds = [FULL, FULL, FULL, LOW]
        ffn_out_state = (ffn_out_master, ffn_out_first, ffn_out_second)
        ffn_in_state = (ffn_in_master, ffn_in_first, ffn_in_second)
        ffn_new = call(
            functools.partial(ffn_update_kernel, grad_scale), "ffn_update", [],
            [layer_own, layer_got, *ffn_in_state, *ffn_out_state],
            [(ffn_in_master.shape, kind) for kind in kinds]
            + [(ffn_out_master.shape, kind) for kind in kinds], 1,
        )
        self_kept, self_sends = fold_square(
            spot, self_kept, [after(item, layer_send) for item in self_moved]
        )
        self_moved = move_layers(self_sends)
        states = [
            qkv_master, qkv_first, qkv_second, out_master, out_first, out_second,
            vector_master.T, vector_first.T, vector_second.T,
        ]
        final_new = call(
            functools.partial(final_update_kernel, grad_scale, 2 * hidden), "final_update", [],
            [layer_own, layer_got, self_kept, *self_moved, *states],
            [(item.shape, kind) for item in states[::3] for kind in kinds], 1,
        )
        return (
            layer_out, tokens_grad, encoded_grad, *final_new[:8], *ffn_new,
            *[item.T for item in final_new[8:]],
        )
    cross_kept, cross_sends = fold_square(
        spot, cross_kept, [after(item, *self_sends) for item in cross_moved]
    )
    cross_moved = move_layers(cross_sends)
    ffn_total = add_all(ffn_kept, ffn_moved)
    cross_total = add_all(cross_kept, cross_moved)
    self_kept, self_sends = fold_square(
        spot, self_kept, [after(item, *cross_sends) for item in self_moved]
    )
    self_moved = move_layers(self_sends)
    self_total = add_all(self_kept, self_moved)

    def block(values, index):
        return values[:, index * model : (index + 1) * model]

    summed_qkv = jnp.stack(
        [block(self_total, i) for i in range(3)] + [block(cross_total, i) for i in range(3)]
    )
    summed_out = jnp.stack([block(self_total, 3), block(cross_total, 3)])
    summed_ffn_in = ffn_total[:, :hidden]
    summed_ffn_out = (
        ffn_total[:, hidden:].reshape(rows, pieces, model).transpose(1, 0, 2).reshape(-1, model)
    )
    summed_vector = self_total[:, 4 * model : 4 * model + vector_master.shape[0]].T
    qkv_first_new, qkv_second_new, qkv_master_new, qkv_copy = adamw(
        qkv_master, summed_qkv * grad_scale, qkv_first, qkv_second, 0.04
    )
    out_first_new, out_second_new, out_master_new, out_copy = adamw(
        out_master, summed_out * grad_scale, out_first, out_second, 0.3
    )
    ffn_in_first_new, ffn_in_second_new, ffn_in_master_new, ffn_in_copy = adamw(
        ffn_in_master, summed_ffn_in * grad_scale, ffn_in_first, ffn_in_second, 0.04
    )
    ffn_out_first_new, ffn_out_second_new, ffn_out_master_new, ffn_out_copy = adamw(
        ffn_out_master, summed_ffn_out * grad_scale, ffn_out_first, ffn_out_second, 0.02
    )
    vector_first_new, vector_second_new, vector_master_new, vector_copy = adamw(
        vector_master, summed_vector * grad_scale, vector_first, vector_second, 0.35
    )
    return (
        layer_out,
        tokens_grad,
        encoded_grad,
        qkv_first_new,
        qkv_second_new,
        qkv_master_new,
        qkv_copy,
        out_first_new,
        out_second_new,
        out_master_new,
        out_copy,
        ffn_in_first_new,
        ffn_in_second_new,
        ffn_in_master_new,
        ffn_in_copy,
        ffn_out_first_new,
        ffn_out_second_new,
        ffn_out_master_new,
        ffn_out_copy,
        vector_first_new,
        vector_second_new,
        vector_master_new,
        vector_copy,
    )


def solution(mesh):
    return jax.shard_map(
        body,
        mesh=mesh,
        in_specs=(
            P(("dp", "fsdp"), None),
            P(("dp", "fsdp"), None),
            P(("dp", "fsdp"), None),
            P(("dp", "fsdp"), None),
            P(("dp", "fsdp"), None),
            P(None, ("dp", "fsdp"), None),
            P(None, ("dp", "fsdp"), None),
            P(None, ("dp", "fsdp"), None),
            P(None, ("dp", "fsdp"), None),
            P(None, ("dp", "fsdp"), None),
            P(None, ("dp", "fsdp"), None),
            P(("dp", "fsdp"), None),
            P(("dp", "fsdp"), None),
            P(("dp", "fsdp"), None),
            P(("dp", "fsdp"), None),
            P(("dp", "fsdp"), None),
            P(("dp", "fsdp"), None),
            P(None, ("dp", "fsdp")),
            P(None, ("dp", "fsdp")),
            P(None, ("dp", "fsdp")),
        ),
        out_specs=(
            P(("dp", "fsdp"), None),
            P(("dp", "fsdp"), None),
            P(("dp", "fsdp"), None),
            P(None, ("dp", "fsdp"), None),
            P(None, ("dp", "fsdp"), None),
            P(None, ("dp", "fsdp"), None),
            P(None, ("dp", "fsdp"), None),
            P(None, ("dp", "fsdp"), None),
            P(None, ("dp", "fsdp"), None),
            P(None, ("dp", "fsdp"), None),
            P(None, ("dp", "fsdp"), None),
            P(("dp", "fsdp"), None),
            P(("dp", "fsdp"), None),
            P(("dp", "fsdp"), None),
            P(("dp", "fsdp"), None),
            P(("dp", "fsdp"), None),
            P(("dp", "fsdp"), None),
            P(("dp", "fsdp"), None),
            P(("dp", "fsdp"), None),
            P(None, ("dp", "fsdp")),
            P(None, ("dp", "fsdp")),
            P(None, ("dp", "fsdp")),
            P(None, ("dp", "fsdp")),
        ),
        check_vma=False,
    )
```

```python
import functools
import math

import jax
import jax.numpy as jnp
from jax import lax
from jax.experimental import pallas as pl
from jax.experimental.pallas import tpu as pltpu
from jax.sharding import PartitionSpec as P

HEADS = 8
STEP = 5
SEGMENTS = 10
norm_eps = 1e-05
beta_first = 0.5
beta_second = 0.5
adam_eps = 1e-08
weight_decay = 0.01
mask_fill = -1000000000.0
LOW = jnp.bfloat16
FULL = jnp.float32


def dot_nn(left, right):
    return lax.dot_general(left, right, (((1,), (0,)), ((), ())), preferred_element_type=FULL)


def dot_nt(left, right):
    return lax.dot_general(left, right, (((1,), (1,)), ((), ())), preferred_element_type=FULL)


def dot_tn(left, right):
    return lax.dot_general(left, right, (((0,), (0,)), ((), ())), preferred_element_type=FULL)


def head_masks(width, group, factor):
    lane = lax.broadcasted_iota(jnp.int32, (1, group * width), 1) // width
    return [jnp.where(lane == h, factor, 0.0).astype(LOW) for h in range(group)]


def window(start, size, total):
    return pl.multiple_of(jnp.minimum(start // 16 * 16, total - size), 16)


def inside(base, size, begin, end):
    place = lax.broadcasted_iota(jnp.int32, (size, 1), 0) + base
    return (place >= begin) & (place < end)


def each_span(row_starts, col_starts, total, same, work):
    def segment(s, carry):
        row_begin, row_end = row_starts[s], row_starts[s + 1]
        col_begin, col_end = col_starts[s], col_starts[s + 1]
        row_short = row_end - window(row_begin, 128, total) <= 128
        col_short = col_end - window(col_begin, 128, total) <= 128
        for row_span in (128, 256):
            for col_span in (128, 256):
                if same and row_span != col_span:
                    continue
                wanted = row_short if row_span == 128 else jnp.logical_not(row_short)
                if not same:
                    other = col_short if col_span == 128 else jnp.logical_not(col_short)
                    wanted = jnp.logical_and(wanted, other)

                @pl.when(wanted)
                def _(row_span=row_span, col_span=col_span):
                    row_base = window(row_begin, row_span, total)
                    col_base = window(col_begin, col_span, total)
                    work(
                        s,
                        pl.ds(row_base, row_span),
                        pl.ds(col_base, col_span),
                        inside(row_base, row_span, row_begin, row_end),
                        inside(col_base, col_span, col_begin, col_end),
                        row_span,
                    )

        return carry

    lax.fori_loop(0, SEGMENTS, segment, 0)


def attend_forward(row_starts, col_starts, q_ref, k_ref, v_ref, out_ref, sums_ref):
    total, model = q_ref.shape
    width = model // HEADS
    group = 256 // width
    scales = head_masks(width, group, 1.0 / math.sqrt(width))
    parts = [slice(g * 256, (g + 1) * 256) for g in range(HEADS // group)]

    def work(s, rows, cols, row_mask, col_mask, span):
        raw = []
        for lanes in parts:
            query, keys = q_ref[rows, lanes], k_ref[cols, lanes]
            stacked = jnp.concatenate([query * scale for scale in scales], axis=0)
            raw.append(dot_nt(keys, stacked))
        turned = [v_ref[cols, lanes].T for lanes in parts]
        probs = []
        for g, item in enumerate(raw):
            scores = jnp.where(col_mask, item, mask_fill)
            largest = jnp.max(scores, axis=0, keepdims=True)
            expo = jnp.exp(scores - largest)
            totals = jnp.sum(expo, axis=0, keepdims=True)
            sums_ref[s, g, :, : group * span] = largest + jnp.log(totals)
            probs.append((expo * (1.0 / totals)).astype(LOW))
        mixed = [
            [
                dot_nn(side[h * width : (h + 1) * width], prob[:, h * span : (h + 1) * span])
                for h in range(group)
            ]
            for side, prob in zip(turned, probs)
        ]
        for lanes, items in zip(parts, mixed):
            value = jnp.concatenate(items, axis=0).T
            old = out_ref[rows, lanes].astype(FULL)
            out_ref[rows, lanes] = jnp.where(row_mask, value, old).astype(LOW)

    each_span(row_starts, col_starts, total, row_starts is col_starts, work)


def attend_backward(
    row_starts, col_starts, q_ref, k_ref, v_ref, grad_ref, sums_ref, dq_ref, dk_ref, dv_ref
):
    total, model = q_ref.shape
    width = model // HEADS
    group = 256 // width
    factor = 1.0 / math.sqrt(width)
    scales = head_masks(width, group, factor)
    picks = head_masks(width, group, 1.0)
    parts = [slice(g * 256, (g + 1) * 256) for g in range(HEADS // group)]

    def work(s, rows, cols, row_mask, col_mask, span):
        stacks, grads, raw, grad_probs = [], [], [], []
        for lanes in parts:
            query, keys, values = q_ref[rows, lanes], k_ref[cols, lanes], v_ref[cols, lanes]
            grad = jnp.where(row_mask, grad_ref[rows, lanes].astype(FULL), 0.0).astype(LOW)
            stacks.append(jnp.concatenate([query * scale for scale in scales], axis=0))
            grads.append(jnp.concatenate([grad * item for item in picks], axis=0))
            raw.append(dot_nt(keys, stacks[-1]))
            grad_probs.append(dot_nt(values, grads[-1]))
        grad_values, grad_scores = [], []
        for g, (item, grad_prob) in enumerate(zip(raw, grad_probs)):
            scores = jnp.where(col_mask, item, mask_fill)
            probs = jnp.exp(scores - sums_ref[s, g, :, : group * span])
            grad_values.append(dot_nn(probs.astype(LOW), grads[g]))
            weighted = probs * grad_prob
            inner = jnp.sum(weighted, axis=0, keepdims=True)
            grad_scores.append((weighted - probs * inner).astype(LOW))
        grad_keys, grad_queries = [], []
        for lanes, item, stacked in zip(parts, grad_scores, stacks):
            grad_keys.append(dot_nn(item, stacked))
            turned = k_ref[cols, lanes].T
            grad_queries.append(
                [
                    dot_nn(turned[h * width : (h + 1) * width], item[:, h * span : (h + 1) * span])
                    for h in range(group)
                ]
            )
        for g, lanes in enumerate(parts):
            grad_query = jnp.concatenate(grad_queries[g], axis=0).T * factor
            for ref, place, mask, value in (
                (dq_ref, rows, row_mask, grad_query),
                (dk_ref, cols, col_mask, grad_keys[g]),
                (dv_ref, cols, col_mask, grad_values[g]),
            ):
                old = ref[place, lanes].astype(FULL)
                ref[place, lanes] = jnp.where(mask, value, old).astype(LOW)

    each_span(row_starts, col_starts, total, row_starts is col_starts, work)


def normalize(values):
    center = values - jnp.mean(values, axis=-1, keepdims=True)
    inverse = lax.rsqrt(jnp.mean(center * center, axis=-1, keepdims=True) + norm_eps)
    return center * inverse, inverse


def normalize_back(grad, gain, unit, inverse):
    scaled = grad * (1.0 + gain)
    mean = jnp.mean(scaled, axis=-1, keepdims=True)
    along = jnp.mean(scaled * unit, axis=-1, keepdims=True)
    return (scaled - mean - unit * along) * inverse


def column_sum(values):
    return jnp.sum(values.astype(FULL), axis=0, keepdims=True)


STEP_ROWS = 512


def row_steps(total, step, size=256):
    def run(i, carry):
        step(pl.ds(pl.multiple_of(i * size, size), size))
        return carry

    lax.fori_loop(0, total // size, run, 0)


def load_weights(place, depth, sources, targets, semaphores):
    if len(sources) == 1:
        offset = 0
        for target, semaphore in zip(targets, semaphores):
            source = sources[0].at[:, offset : offset + target.shape[1]]
            offset += target.shape[1]
            pltpu.make_async_copy(source, target, semaphore).start()
        return
    half = len(sources) // 2
    for k, source in enumerate(sources):
        base = (k % half) * 2 * depth + k // half
        for layer in range(depth):
            other = place ^ (base + 2 * layer)
            offset = 0
            for target, semaphore in zip(targets, semaphores):
                rows = source.shape[1]
                span = target.shape[1]
                to_rows = pl.ds(pl.multiple_of(other * rows, rows), rows)
                pltpu.make_async_copy(
                    source.at[layer, :, offset : offset + span], target.at[to_rows, :], semaphore
                ).start()
                offset += span


def await_weights(target, semaphore):
    pltpu.make_async_copy(target, target, semaphore).wait()


def store_grad(refs, core, lanes, value):
    value = value.astype(LOW)
    if len(refs) == 1:
        refs[0][:, lanes] = value
        return
    sent, kept = refs
    chips, rows = kept.shape[0], kept.shape[1]
    parts = value.reshape(chips, 2, rows, value.shape[1])
    first = core == 0
    kept[:, :, lanes] = jnp.where(first, parts[:, 0], parts[:, 1])
    sent[:, :, lanes] = jnp.where(first, parts[:, 1], parts[:, 0])


def self_forward_kernel(count, depth, place, row_starts, tokens, *rest):
    sources = rest[:count]
    weights, vectors, queries, keys, values, mixed, sums, semaphores = rest[count:]
    model = tokens.shape[1]
    load_weights(place[0], depth, sources, [weights], [semaphores.at[0]])
    await_weights(weights, semaphores.at[0])
    turned = weights[:, 3 * model : 3 * model + 128].astype(FULL).T
    vectors[...] = turned[: vectors.shape[0]]

    def project(rows):
        block = tokens[rows, :]
        queries[rows, :] = (dot_nn(block, weights[:, :model]) + vectors[0:1, :]).astype(LOW)
        keys[rows, :] = dot_nn(block, weights[:, model : 2 * model]).astype(LOW)
        values[rows, :] = (
            dot_nn(block, weights[:, 2 * model : 3 * model]) + vectors[1:2, :]
        ).astype(LOW)

    row_steps(tokens.shape[0], project)
    attend_forward(row_starts, row_starts, queries, keys, values, mixed, sums)


def cross_project_kernel(count, depth, place, tokens, encoded, mixed, vectors, *rest):
    sources = rest[:count]
    weights, unit_one, inverse_one, queries, keys, values, semaphores = rest[count:]
    model = tokens.shape[1]
    load_weights(place[0], depth, sources, [weights], [semaphores.at[0]])
    await_weights(weights, semaphores.at[0])

    def project(rows):
        block = encoded[rows, :]
        keys[rows, :] = dot_nn(block, weights[:, 2 * model : 3 * model]).astype(LOW)
        values[rows, :] = (
            dot_nn(block, weights[:, 3 * model : 4 * model]) + vectors[4:5, :]
        ).astype(LOW)
        summed = tokens[rows, :].astype(FULL) + dot_nn(mixed[rows, :], weights[:, :model])
        unit, inverse = normalize(summed + vectors[2:3, :])
        unit_one[rows, :] = unit
        inverse_one[rows, :] = inverse
        low = (unit * (1.0 + vectors[7:8, :]) + vectors[10:11, :]).astype(LOW)
        queries[rows, :] = (dot_nn(low, weights[:, model : 2 * model]) + vectors[3:4, :]).astype(LOW)

    row_steps(tokens.shape[0], project, 512)


def cross_attend_kernel(row_starts, col_starts, queries, keys, values, cross_mixed, sums):
    attend_forward(row_starts, col_starts, queries, keys, values, cross_mixed, sums)


def cross_finish_kernel(unit_one, cross_mixed, weights, vectors, unit_two, inverse_two):
    model = cross_mixed.shape[1]

    def finish(rows):
        first = unit_one[rows, :] * (1.0 + vectors[7:8, :]) + vectors[10:11, :]
        summed = first + dot_nn(cross_mixed[rows, :], weights[:, 4 * model : 5 * model])
        unit, inverse = normalize(summed + vectors[5:6, :])
        unit_two[rows, :] = unit
        inverse_two[rows, :] = inverse

    row_steps(unit_one.shape[0], finish, 512)


gelu_scale = math.sqrt(2.0 / math.pi)
gelu_cubic = 0.044715


def ffn_kernel(count, depth, place, unit_two, inverse_two, cotangent, weights, vectors, *rest):
    sources = rest[:count]
    (
        layer_out, grad_sum, grad_out, grad_mixed, sums, bias_sums, *grads,
        first_weights, second_weights, hidden, grad_ffn, grad_pre, slopes, semaphores,
    ) = rest[count:]
    model = unit_two.shape[1]
    pieces = first_weights.shape[1] // model
    load_ffn(place[0], depth, sources, first_weights, second_weights, semaphores)
    sums[...] = jnp.zeros_like(sums)
    bias_sums[...] = jnp.zeros_like(bias_sums)
    await_weights(first_weights, semaphores.at[0])
    await_weights(second_weights, semaphores.at[1])

    def step(rows):
        unit = unit_two[rows, :]
        second = unit * (1.0 + vectors[8:9, :]) + vectors[11:12, :]
        low = second.astype(LOW)
        total = second + vectors[6:7, :]
        for j in range(pieces):
            lanes = slice(j * model, (j + 1) * model)
            pre = dot_nn(low, first_weights[:, lanes]) + vectors[13 + j : 14 + j, :]
            square = pre * pre
            bend = jnp.tanh(gelu_scale * pre * (1.0 + gelu_cubic * square))
            half = 0.5 * (1.0 + bend)
            value = (pre * half).astype(LOW)
            hidden[rows, lanes] = value
            inner = gelu_scale * (1.0 + 3.0 * gelu_cubic * square)
            slopes[:, lanes] = half + 0.5 * pre * (1.0 - bend * bend) * inner
            total = total + dot_nn(value, second_weights[lanes, :])
        unit_three, inverse_three = normalize(total)
        layer_out[rows, :] = (unit_three * (1.0 + vectors[9:10, :]) + vectors[12:13, :]).astype(LOW)
        upper = cotangent[rows, :].astype(FULL)
        third = normalize_back(upper, vectors[9:10, :], unit_three, inverse_three)
        third_low = third.astype(LOW)
        grad_ffn[rows, :] = third_low
        sums[0:1, :] += column_sum(third_low)
        sums[1:2, :] += column_sum(upper * unit_three)
        sums[2:3, :] += column_sum(upper)
        below = third
        for j in range(pieces):
            lanes = slice(j * model, (j + 1) * model)
            pre = (dot_nt(third_low, second_weights[lanes, :]) * slopes[:, lanes]).astype(LOW)
            grad_pre[rows, lanes] = pre
            bias_sums[j : j + 1, :] += column_sum(pre)
            below = below + dot_nt(pre, first_weights[:, lanes])
        sums[3:4, :] += column_sum(below * unit)
        sums[4:5, :] += column_sum(below)
        second_sum = normalize_back(below, vectors[8:9, :], unit, inverse_two[rows, :])
        grad_sum[rows, :] = second_sum
        out_low = second_sum.astype(LOW)
        grad_out[rows, :] = out_low
        sums[5:6, :] += column_sum(out_low)
        grad_mixed[rows, :] = dot_nt(out_low, weights[:, 4 * model : 5 * model]).astype(LOW)

    row_steps(unit_two.shape[0], step, STEP_ROWS)
    core = place[0] % 2
    second_low = (unit_two[...] * (1.0 + vectors[8:9, :]) + vectors[11:12, :]).astype(LOW)

    def block_grads(j, carry):
        lanes = pl.ds(pl.multiple_of(j * model, model), model)
        store_grad(grads, core, lanes, dot_tn(second_low, grad_pre[:, lanes]))
        store_ffn_out(grads, core, j, pieces, dot_tn(hidden[:, lanes], grad_ffn[...]))
        return carry

    lax.fori_loop(0, pieces, block_grads, 0)


def load_ffn(place, depth, sources, first_weights, second_weights, semaphores):
    first_width = first_weights.shape[1]
    if len(sources) == 1:
        pltpu.make_async_copy(
            sources[0].at[:, :first_width], first_weights, semaphores.at[0]
        ).start()
        pieces = first_width // first_weights.shape[0]
        model = first_weights.shape[0]
        for j in range(pieces):
            pltpu.make_async_copy(
                sources[0].at[:, first_width + j * model : first_width + (j + 1) * model],
                second_weights.at[pl.ds(j * model, model), :],
                semaphores.at[1],
            ).start()
        return
    half = len(sources) // 2
    model = second_weights.shape[1]
    for k, source in enumerate(sources):
        base = (k % half) * 2 * depth + k // half
        rows = source.shape[1]
        for layer in range(depth):
            other = place ^ (base + 2 * layer)
            to_rows = pl.ds(pl.multiple_of(other * rows, rows), rows)
            pltpu.make_async_copy(
                source.at[layer, :, :first_width], first_weights.at[to_rows, :], semaphores.at[0]
            ).start()
            pieces = first_width // model
            for j in range(pieces):
                start = pl.multiple_of((other * pieces + j) * rows, rows)
                pltpu.make_async_copy(
                    source.at[layer, :, first_width + j * model : first_width + (j + 1) * model],
                    second_weights.at[pl.ds(start, rows), :],
                    semaphores.at[1],
                ).start()


def store_ffn_out(refs, core, block, pieces, value):
    value = value.astype(LOW)
    model = value.shape[1]
    if len(refs) == 1:
        offset = pl.multiple_of((pieces + block) * model, model)
        refs[0][:, pl.ds(offset, model)] = value
        return
    sent, kept = refs
    rows = kept.shape[1]
    chips = kept.shape[0] // pieces
    parts = value.reshape(chips, 2, pieces, rows, model)
    first = core == 0
    place = pl.ds(block * chips, chips)
    for j in range(pieces):
        lanes = slice((pieces + j) * model, (pieces + j + 1) * model)
        kept[place, :, lanes] = jnp.where(first, parts[:, 0, j], parts[:, 1, j])
        sent[place, :, lanes] = jnp.where(first, parts[:, 1, j], parts[:, 0, j])


def cross_backward_kernel(
    row_starts, col_starts, queries, keys, values, grad_mixed, sums_in, dq, dk, dv
):
    attend_backward(row_starts, col_starts, queries, keys, values, grad_mixed, sums_in, dq, dk, dv)


def cross_grads_kernel(
    place, dq, dk, dv, weights, vectors, grad_sum, unit_one, inverse_one,
    encoded, cross_mixed, grad_out,
    first_sum, self_low, grad_mixed, sums, encoded_grad, *grads,
):
    model = dq.shape[1]
    sums[...] = jnp.zeros_like(sums)

    def finish(rows):
        query, key, value = dq[rows, :], dk[rows, :], dv[rows, :]
        sums[0:1, :] += column_sum(query)
        sums[1:2, :] += column_sum(value)
        encoded_grad[rows, :] = dot_nt(key, weights[:, 2 * model : 3 * model]) + dot_nt(
            value, weights[:, 3 * model : 4 * model]
        )
        upper = grad_sum[rows, :] + dot_nt(query, weights[:, model : 2 * model])
        unit = unit_one[rows, :]
        sums[2:3, :] += column_sum(upper * unit)
        sums[3:4, :] += column_sum(upper)
        below = normalize_back(upper, vectors[7:8, :], unit, inverse_one[rows, :])
        first_sum[rows, :] = below
        low = below.astype(LOW)
        self_low[rows, :] = low
        sums[4:5, :] += column_sum(low)
        grad_mixed[rows, :] = dot_nt(low, weights[:, :model]).astype(LOW)

    row_steps(dq.shape[0], finish)
    core = place[0] % 2
    first_low = (unit_one[...] * (1.0 + vectors[7:8, :]) + vectors[10:11, :]).astype(LOW)
    pairs = ((first_low, dq), (encoded, dk), (encoded, dv), (cross_mixed, grad_out))
    for j, (left, right) in enumerate(pairs):
        lanes = slice(j * model, (j + 1) * model)
        store_grad(grads, core, lanes, dot_tn(left[...], right[...]))


def self_backward_kernel(
    place, row_starts, queries, keys, values, grad_mixed, sums_in, tokens, mixed, self_low,
    cross_sums, ffn_sums, bias_sums, dq, dk, dv, *rest,
):
    *grads, stack = rest
    attend_backward(row_starts, row_starts, queries, keys, values, grad_mixed, sums_in, dq, dk, dv)
    model = dq.shape[1]
    core = place[0] % 2
    pairs = ((tokens, dq), (tokens, dk), (tokens, dv), (mixed, self_low))
    for j, (left, right) in enumerate(pairs):
        lanes = slice(j * model, (j + 1) * model)
        store_grad(grads, core, lanes, dot_tn(left[...], right[...]))
    stack[...] = jnp.zeros_like(stack)
    stack[0:1, :] = column_sum(dq[...])
    stack[1:2, :] = column_sum(dv[...])
    order = (
        (2, cross_sums, 4), (3, cross_sums, 0), (4, cross_sums, 1), (5, ffn_sums, 5),
        (6, ffn_sums, 0), (7, cross_sums, 2), (8, ffn_sums, 3), (9, ffn_sums, 1),
        (10, cross_sums, 3), (11, ffn_sums, 4), (12, ffn_sums, 2),
    )
    for to, ref, at in order:
        stack[to : to + 1, :] = ref[at : at + 1, :]
    extra = bias_sums.shape[0]
    stack[13 : 13 + extra, :] = bias_sums[...]
    start = len(pairs) * model
    store_grad(grads, core, slice(start, start + 128), stack[...].T)


def tokens_grad_kernel(dq, dk, dv, first_sum, weights, tokens_grad):
    model = dq.shape[1]

    def finish(rows):
        below = first_sum[rows, :] + dot_nt(dq[rows, :], weights[:, :model])
        below = below + dot_nt(dk[rows, :], weights[:, model : 2 * model])
        tokens_grad[rows, :] = below + dot_nt(dv[rows, :], weights[:, 2 * model : 3 * model])

    row_steps(dq.shape[0], finish, 512)


def fold_core_kernel(shape, place, kept, received, own, *sends):
    dp_count, depth = shape
    at = place[0] // (2 * depth)
    for k, ref in enumerate((own, *sends)):
        spot = pl.ds((at ^ k) * depth, depth)
        value = kept[spot].astype(FULL) + received[spot].astype(FULL)
        ref[...] = value.astype(ref.dtype)


def fold_square_kernel(shape, place, kept, *rest):
    dp_count, depth = shape
    received, outs = rest[: dp_count - 1], rest[dp_count - 1 :]
    at = place[0] // 2 % depth
    for k, ref in enumerate(outs):
        spot = pl.ds(at ^ k, 1)
        value = kept[spot]
        for item in received:
            value = value + item[spot].astype(FULL)
        ref[...] = value[0].astype(ref.dtype)


def fold_halves_kernel(depth, place, kept, received, keep_first, send_first, keep_second, send_second):
    at = place[0] // (2 * depth)
    half = kept.shape[2] // 2
    low, high = slice(0, half), slice(half, 2 * half)
    for ref, lanes, offsets in (
        (keep_first, low, (0, 1)),
        (send_first, low, (2, 3)),
        (keep_second, high, (0, 2)),
        (send_second, high, (1, 3)),
    ):
        for slot, k in enumerate(offsets):
            spot = pl.ds((at ^ k) * depth, depth)
            value = kept[spot, :, lanes].astype(FULL) + received[spot, :, lanes].astype(FULL)
            ref[slot] = value.astype(ref.dtype)


def fold_pairs_kernel(keep_first, got_first, keep_second, got_second, *outs):
    own_first, send_first, own_second, send_second = outs
    own_first[...] = keep_first[0] + got_first[0].astype(FULL)
    send_first[...] = (keep_first[1] + got_first[1].astype(FULL)).astype(LOW)
    own_second[...] = keep_second[0] + got_second[0].astype(FULL)
    send_second[...] = (keep_second[1] + got_second[1].astype(FULL)).astype(LOW)


def fold_layers_kernel(depth, place, first, got_first, second, got_second, cross, *rest):
    *got_cross, keep, send = rest
    at = place[0] // 2 % depth
    half = first.shape[2]
    for ref, offsets in ((keep, (0, 1)), (send, (2, 3))):
        for slot, k in enumerate(offsets):
            spot = pl.ds(at ^ k, 1)
            value = first[spot] + got_first[spot].astype(FULL)
            ref[slot, :, :half] = value[0].astype(ref.dtype)
            value = second[spot] + got_second[spot].astype(FULL)
            ref[slot, :, half : 2 * half] = value[0].astype(ref.dtype)
            value = cross[spot]
            for item in got_cross:
                value = value + item[spot].astype(FULL)
            ref[slot, :, 2 * half :] = value[0].astype(ref.dtype)


def fold_last_kernel(keep, got, own, send):
    own[...] = keep[0] + got[0].astype(FULL)
    send[...] = (keep[1] + got[1].astype(FULL)).astype(LOW)


def update_into(outs, index, state, grad, rate):
    for ref, value in zip(outs, adamw(state[0][index], grad, state[1][index], state[2][index], rate)):
        ref[index] = value


def ffn_update_kernel(grad_scale, own, got, *rest):
    first_state, second_state, outs = rest[:3], rest[3:6], rest[6:]
    rows, width = first_state[0].shape
    model = second_state[0].shape[1]
    grad = (own[:, :width] + got[:, :width].astype(FULL)) * grad_scale
    update_into(outs[:4], (slice(None), slice(None)), first_state, grad, 0.04)
    for j in range(second_state[0].shape[0] // rows):
        lanes = slice(width + j * model, width + (j + 1) * model)
        grad = (own[:, lanes] + got[:, lanes].astype(FULL)) * grad_scale
        index = (slice(j * rows, (j + 1) * rows), slice(None))
        update_into(outs[4:], index, second_state, grad, 0.02)


def final_update_kernel(grad_scale, start, own, got, kept, *rest):
    moved, states, outs = rest[:-21], rest[-21:-12], rest[-12:]
    qkv_state, out_state, vector_state = states[:3], states[3:6], states[6:]
    model = qkv_state[0].shape[2]

    def self_grad(lanes):
        value = kept[:, lanes]
        for item in moved:
            value = value + item[:, lanes].astype(FULL)
        return value * grad_scale

    def cross_grad(index):
        lanes = slice(start + index * model, start + (index + 1) * model)
        return (own[:, lanes] + got[:, lanes].astype(FULL)) * grad_scale

    for j in range(4):
        grad = self_grad(slice(j * model, (j + 1) * model))
        if j < 3:
            update_into(outs[:4], j, qkv_state, grad, 0.04)
            update_into(outs[:4], 3 + j, qkv_state, cross_grad(j), 0.04)
        else:
            update_into(outs[4:8], 0, out_state, grad, 0.3)
            update_into(outs[4:8], 1, out_state, cross_grad(j), 0.3)
    grad = self_grad(slice(4 * model, 4 * model + vector_state[0].shape[1]))
    update_into(outs[8:], (slice(None), slice(None)), vector_state, grad, 0.35)


LIMITS = {
    "fold_halves": 16,
    "fold_pairs": 14,
    "fold_layers": 12,
    "fold_last": 8,
    "ffn_update": 8,
    "final_update": 10,
    "fold_core": 12,
    "fold_square": 10,
    "self_forward": 14,
    "cross_project": 14,
    "cross_attend": 10,
    "cross_finish": 9,
    "ffn": 33,
    "cross_backward": 11,
    "cross_grads": 20,
    "self_backward": 16,
    "tokens_grad": 11,
}


def out_kind(item):
    if len(item) == 3:
        return pltpu.VMEM(item[0], item[1])
    return jax.ShapeDtypeStruct(*item)


def keep(item):
    return (item[0], item[1], True)


def limit(name):
    return pltpu.CompilerParams(vmem_limit_bytes=LIMITS[name] << 20)


def pinned(sources):
    if len(sources) == 1:
        return sources
    return [pltpu.with_memory_space_constraint(item, pltpu.VMEM) for item in sources]


def source_spec(sources):
    return pl.BlockSpec(memory_space=pltpu.VMEM if len(sources) > 1 else pl.ANY)


def call(kernel, name, scalars, arrays, outs, flops, sources=(), scratch=()):
    specs = [pl.BlockSpec(memory_space=pltpu.SMEM)] * len(scalars)
    specs += [pl.BlockSpec(memory_space=pltpu.VMEM)] * len(arrays)
    specs += [source_spec(sources)] * len(sources)
    shapes = [out_kind(item) for item in outs]
    moved = sum(item.size * item.dtype.itemsize for item in [*arrays, *sources])
    return pl.pallas_call(
        kernel,
        out_shape=shapes,
        in_specs=specs,
        out_specs=[pl.BlockSpec(memory_space=pltpu.VMEM)] * len(outs),
        scratch_shapes=list(scratch),
        compiler_params=limit(name),
        cost_estimate=pl.CostEstimate(flops=flops, transcendentals=0, bytes_accessed=moved),
        name=name,
    )(*scalars, *arrays, *pinned(sources))


def segment_starts(ids):
    marks = jnp.arange(SEGMENTS + 1, dtype=ids.dtype)
    return jnp.sum((ids[None, :] < marks[:, None]).astype(jnp.int32), axis=1)


def adamw(master, grad, first, second, rate):
    first_new = beta_first * first + (1.0 - beta_first) * grad
    second_new = beta_second * second + (1.0 - beta_second) * grad * grad
    first_hat = first_new / (1.0 - beta_first**STEP)
    second_hat = second_new / (1.0 - beta_second**STEP)
    master_new = master - rate * (
        first_hat / (jnp.sqrt(second_hat) + adam_eps) + weight_decay * master
    )
    return (first_new, second_new, master_new, master_new.astype(jnp.bfloat16))


AXES = ("dp", "fsdp")


def exchange(values, offset):
    count = lax.axis_size("dp") * lax.axis_size("fsdp")
    return lax.ppermute(values, AXES, [(i, i ^ offset) for i in range(count)])


def after(value, *others):
    return lax.optimization_barrier((value, *others))[0]


def layer_stack(piece):
    depth = lax.axis_size("fsdp") // 2
    return jnp.stack([piece] + [exchange(piece, 2 * k) for k in range(1, depth)])


def layer_double(piece, gate=None):
    stack, step = piece[None], 1
    while step < lax.axis_size("fsdp") // 2:
        if gate is not None and step > 1:
            stack = after(stack, gate)
        stack = jnp.concatenate([stack, exchange(stack, 2 * step)])
        step *= 2
    return stack


def square_list(stack):
    dp_count, fsdp_count = lax.axis_size("dp"), lax.axis_size("fsdp")
    return [stack] + [exchange(stack, fsdp_count * k) for k in range(1, dp_count)]


def forward_list(stack):
    stride, near = lax.axis_size("fsdp"), [stack]
    for k in range(1, lax.axis_size("dp")):
        near.append(None if k & (k - 1) else exchange(stack, stride * k))
    return near


def forward_rest(near, gate):
    stride = lax.axis_size("fsdp")
    for k, item in enumerate(near):
        if item is None:
            high = 1 << (k.bit_length() - 1)
            near[k] = exchange(after(near[k - high], gate), stride * high)
    return near


def core_list(near):
    return near + [exchange(item, 1) for item in near]


def ordered(parts, place):
    half = len(parts) // 2
    both = jnp.stack([jnp.stack(parts[:half]), jnp.stack(parts[half:])], axis=2)
    flat = both.reshape((-1,) + both.shape[3:])
    return flat[jnp.arange(flat.shape[0]) ^ place]


def pick(values, index, axis):
    return lax.dynamic_index_in_dim(values, index, axis, keepdims=False)


def split_core(grads):
    if len(grads) == 2:
        return grads
    count = lax.axis_size("dp") * lax.axis_size("fsdp")
    core = lax.axis_index("fsdp") % 2
    parts = grads[0].reshape((count // 2, 2, -1) + grads[0].shape[1:])
    return pick(parts, 1 - core, 1), pick(parts, core, 1)


def fold_core(spot, kept, received):
    dp_count, depth = lax.axis_size("dp"), lax.axis_size("fsdp") // 2
    shape = (depth,) + kept.shape[1:]
    if kept.shape[1] % 16:
        place = lax.axis_index("dp")
        pair = (kept.astype(FULL) + received.astype(FULL)).reshape((dp_count,) + shape)
        sends = [pick(pair, place ^ k, 0).astype(LOW) for k in range(1, dp_count)]
        return pick(pair, place, 0), sends
    own, *sends = call(
        functools.partial(fold_core_kernel, (dp_count, depth)), "fold_core", [spot],
        [kept, received], [(shape, FULL)] + [(shape, LOW)] * (dp_count - 1), kept.size,
    )
    return own, sends


def fold_square(spot, kept, received):
    dp_count, depth = lax.axis_size("dp"), lax.axis_size("fsdp") // 2
    shape = kept.shape[1:]
    if kept.shape[1] % 16:
        place = lax.axis_index("fsdp") // 2
        square = add_all(kept, received)
        sends = [pick(square, place ^ k, 0).astype(LOW) for k in range(1, depth)]
        return pick(square, place, 0), sends
    own, *sends = call(
        functools.partial(fold_square_kernel, (dp_count, depth)), "fold_square", [spot],
        [kept, *received], [(shape, FULL)] + [(shape, LOW)] * (depth - 1), kept.size,
    )
    return own, sends


def move_square(sends):
    stride = lax.axis_size("fsdp")
    return [exchange(item, stride * (k + 1)) for k, item in enumerate(sends)]


def move_layers(sends):
    return [exchange(item, 2 * (k + 1)) for k, item in enumerate(sends)]


def add_all(kept, moved):
    for item in moved:
        kept = kept + item.astype(FULL)
    return kept


def body(
    tokens,
    encoded,
    cotangent,
    target_ids,
    source_ids,
    qkv_master,
    qkv_first,
    qkv_second,
    out_master,
    out_first,
    out_second,
    ffn_in_master,
    ffn_in_first,
    ffn_in_second,
    ffn_out_master,
    ffn_out_first,
    ffn_out_second,
    vector_master,
    vector_first,
    vector_second,
):
    total, model = tokens.shape
    dp_count, fsdp_count = lax.axis_size("dp"), lax.axis_size("fsdp")
    count, depth = dp_count * fsdp_count, fsdp_count // 2
    rows = model // count
    aligned = rows % 16 == 0
    place = lax.axis_index("dp") * fsdp_count + lax.axis_index("fsdp")
    spot = place.reshape(1).astype(jnp.int32)
    low_qkv = after(qkv_master, spot).astype(LOW)
    low_out = out_master.astype(LOW)
    low_vector = jnp.pad(vector_master.astype(LOW).T, ((0, 0), (0, 128 - vector_master.shape[0])))
    pieces = ffn_in_master.shape[1] // model

    def to_columns(values):
        return values.reshape(-1, rows, model).transpose(1, 0, 2).reshape(rows, -1)

    self_piece = jnp.concatenate([low_qkv[0], low_qkv[1], low_qkv[2], low_vector], axis=1)
    cross_piece = jnp.concatenate([low_out[0], low_qkv[3], low_qkv[4], low_qkv[5], low_out[1]], axis=1)
    ffn_piece = jnp.concatenate(
        [ffn_in_master.astype(LOW), to_columns(ffn_out_master.astype(LOW))], axis=1
    )
    row_starts, col_starts = segment_starts(target_ids[0]), segment_starts(source_ids[0])

    def sources_of(parts):
        if aligned:
            return parts
        flat = ordered(parts, place)
        return [flat.reshape(model, -1)]

    def ffn_sources_of(parts):
        if aligned:
            return parts
        flat = ordered(parts, place)
        width = pieces * model
        second = flat[:, :, width:].reshape(count, rows, pieces, model).transpose(0, 2, 1, 3)
        second = second.reshape(pieces, model, model).transpose(1, 0, 2).reshape(model, -1)
        return [jnp.concatenate([flat[:, :, :width].reshape(model, -1), second], axis=1)]

    wide, tall, thin = ((total, model), LOW), ((total, model), FULL), ((total, 1), FULL)
    log_sums = ((SEGMENTS, model // 256, 1, 1024), FULL)
    small = ((8, model), FULL)
    unit = 2 * total * model * model
    attend = 2 * SEGMENTS * HEADS * 256 * 256 * 256
    wait_one, wait_two = pltpu.SemaphoreType.DMA((1,)), pltpu.SemaphoreType.DMA((2,))

    def grad_outs(columns):
        if aligned:
            return [((count // 2, rows, columns), LOW)] * 2
        return [((model, columns), LOW)]

    self_stack = layer_stack(self_piece)
    self_near = square_list(self_stack)
    cross_own = layer_double(after(cross_piece, self_stack))
    ffn_own = layer_double(after(ffn_piece, self_stack), cross_own)
    self_parts = core_list(self_near)
    cross_columns = cross_piece.shape[1]
    cross_near = square_list(cross_own)
    ffn_near = forward_list(ffn_own)

    sources = sources_of(self_parts)
    (
        self_weights, vectors, queries, keys, values, mixed, self_sums,
    ) = call(
        functools.partial(self_forward_kernel, len(sources), depth), "self_forward",
        [spot, row_starts], [after(tokens, cross_own)],
        [
            keep(((model, self_piece.shape[1]), LOW)), ((24, model), FULL),
            keep(wide), keep(wide), keep(wide), keep(wide), keep(log_sums),
        ],
        3 * unit + 2 * attend, sources, [wait_one],
    )
    sources = sources_of(core_list([after(item, mixed) for item in cross_near]))
    cross_weights, unit_one, inverse_one, cross_queries, cross_keys, cross_values = call(
        functools.partial(cross_project_kernel, len(sources), depth), "cross_project", [spot],
        [tokens, encoded, mixed, vectors],
        [
            keep(((model, cross_columns), LOW)), keep(tall), thin, keep(wide), keep(wide),
            keep(wide),
        ],
        4 * unit, sources, [wait_one],
    )
    ffn_near = forward_rest(ffn_near, cross_queries)
    cross_mixed, cross_log = call(
        cross_attend_kernel, "cross_attend", [row_starts, col_starts],
        [cross_queries, cross_keys, cross_values], [keep(wide), keep(log_sums)], 2 * attend,
    )
    unit_two, inverse_two = call(
        cross_finish_kernel, "cross_finish", [], [unit_one, cross_mixed, cross_weights, vectors],
        [keep(tall), thin], unit,
    )
    gates = [mixed] * (dp_count // 2) + [cross_mixed] * (dp_count // 2)
    sources = ffn_sources_of(core_list([after(*pair) for pair in zip(ffn_near, gates)]))
    hidden = pieces * model
    (
        layer_out, grad_sum, grad_cross_out, grad_cross_mixed, ffn_sums, bias_sums, *ffn_grads
    ) = call(
        functools.partial(ffn_kernel, len(sources), depth), "ffn", [spot],
        [unit_two, inverse_two, cotangent, cross_weights, vectors],
        [wide, keep(tall), keep(wide), keep(wide), small, small, *grad_outs(2 * hidden)],
        (5 * pieces + 1) * unit, sources,
        [
            pltpu.VMEM((model, hidden), LOW), pltpu.VMEM((hidden, model), LOW),
            pltpu.VMEM((total, hidden), LOW), pltpu.VMEM((total, model), LOW),
            pltpu.VMEM((total, hidden), LOW),
            pltpu.VMEM((STEP_ROWS, hidden), FULL), wait_two,
        ],
    )
    if not aligned:
        first, second = ffn_grads[0][:, :hidden], ffn_grads[0][:, hidden:]
        second = second.reshape(model, pieces, model).transpose(1, 0, 2)
        second = second.reshape(count, pieces, rows, model).transpose(0, 2, 1, 3)
        ffn_grads = [jnp.concatenate([first, second.reshape(model, -1)], axis=1)]
    sent, kept = split_core(ffn_grads)
    ffn_moved = exchange(sent, 1)
    cross_dq, cross_dk, cross_dv = call(
        cross_backward_kernel, "cross_backward", [row_starts, col_starts],
        [cross_queries, cross_keys, cross_values, after(grad_cross_mixed, sent), cross_log],
        [keep(wide), keep(wide), keep(wide)], 5 * attend,
    )
    fast = aligned and dp_count == 4 and depth == 4
    ffn_moved = after(ffn_moved, cross_dq)
    if fast:
        pair = (2, depth, rows, hidden)
        keep_first, send_first, keep_second, send_second = call(
            functools.partial(fold_halves_kernel, depth), "fold_halves", [spot], [kept, ffn_moved],
            [(pair, FULL), (pair, LOW), (pair, FULL), (pair, LOW)], 1,
        )
        ffn_sends = [send_first, send_second]
        got_first = exchange(send_first, 2 * fsdp_count)
        got_second = exchange(send_second, fsdp_count)
    else:
        ffn_kept, ffn_sends = fold_core(spot, kept, ffn_moved)
        ffn_moved = move_square(ffn_sends)
    first_sum, self_low, grad_mixed, cross_vector, encoded_grad, *cross_grads = call(
        cross_grads_kernel, "cross_grads", [spot],
        [
            after(cross_dq, *ffn_sends), cross_dk, cross_dv, cross_weights, vectors, grad_sum,
            unit_one, inverse_one, encoded, cross_mixed, grad_cross_out,
        ],
        [keep(tall), keep(wide), keep(wide), small, tall, *grad_outs(4 * model)], 8 * unit,
    )
    sent, kept = split_core(cross_grads)
    ffn_sends = [sent]
    if fast:
        half = (depth, rows, hidden)
        own_first, send_first, own_second, send_second = call(
            fold_pairs_kernel, "fold_pairs", [],
            [keep_first, after(got_first, sent), keep_second, got_second],
            [(half, FULL), (half, LOW), (half, FULL), (half, LOW)], 1,
        )
        ffn_sends = [send_first, send_second]
        got_first = exchange(send_first, fsdp_count)
        got_second = exchange(send_second, 2 * fsdp_count)
    cross_moved = exchange(after(sent, *ffn_sends), 1)
    cross_kept, cross_sends = fold_core(spot, kept, cross_moved)
    cross_moved = move_square(cross_sends)
    self_dq, self_dk, self_dv, *self_grads = call(
        self_backward_kernel, "self_backward", [spot, row_starts],
        [
            queries, keys, values, after(grad_mixed, *cross_sends, *ffn_sends), self_sums,
            tokens, mixed, self_low, cross_vector, ffn_sums, bias_sums,
        ],
        [keep(wide), keep(wide), keep(wide), *grad_outs(4 * model + 128)],
        5 * attend + 4 * unit, (), [pltpu.VMEM((128, model), FULL)],
    )
    sent, kept = split_core(self_grads)
    if fast:
        wide_pair = (2, rows, 2 * hidden + 4 * model)
        layer_keep, layer_send = call(
            functools.partial(fold_layers_kernel, depth), "fold_layers", [spot],
            [own_first, after(got_first, sent), own_second, got_second, cross_kept, *cross_moved],
            [(wide_pair, FULL), (wide_pair, LOW)], 1,
        )
        ffn_sends = [layer_send]
        layer_got = exchange(layer_send, 4)
        self_moved = exchange(after(sent, layer_send), 1)
    else:
        self_moved = exchange(sent, 1)
        ffn_kept, ffn_sends = fold_square(spot, ffn_kept, [after(item, sent) for item in ffn_moved])
        ffn_moved = move_layers(ffn_sends)
    (tokens_grad,) = call(
        tokens_grad_kernel, "tokens_grad", [],
        [after(self_dq, *ffn_sends), self_dk, self_dv, first_sum, self_weights], [tall], 3 * unit,
    )
    self_kept, self_sends = fold_core(spot, kept, after(self_moved, tokens_grad))
    self_moved = move_square(self_sends)
    grad_scale = 1.0 / math.sqrt(total * count)
    if fast:
        wide_row = wide_pair[1:]
        layer_own, layer_send = call(
            fold_last_kernel, "fold_last", [], [layer_keep, after(layer_got, *self_sends)],
            [(wide_row, FULL), (wide_row, LOW)], 1,
        )
        layer_got = exchange(layer_send, 2)
        kinds = [FULL, FULL, FULL, LOW]
        ffn_out_state = (ffn_out_master, ffn_out_first, ffn_out_second)
        ffn_in_state = (ffn_in_master, ffn_in_first, ffn_in_second)
        ffn_new = call(
            functools.partial(ffn_update_kernel, grad_scale), "ffn_update", [],
            [layer_own, layer_got, *ffn_in_state, *ffn_out_state],
            [(ffn_in_master.shape, kind) for kind in kinds]
            + [(ffn_out_master.shape, kind) for kind in kinds], 1,
        )
        self_kept, self_sends = fold_square(
            spot, self_kept, [after(item, layer_send) for item in self_moved]
        )
        self_moved = move_layers(self_sends)
        states = [
            qkv_master, qkv_first, qkv_second, out_master, out_first, out_second,
            vector_master.T, vector_first.T, vector_second.T,
        ]
        final_new = call(
            functools.partial(final_update_kernel, grad_scale, 2 * hidden), "final_update", [],
            [layer_own, layer_got, self_kept, *self_moved, *states],
            [(item.shape, kind) for item in states[::3] for kind in kinds], 1,
        )
        return (
            layer_out, tokens_grad, encoded_grad, *final_new[:8], *ffn_new,
            *[item.T for item in final_new[8:]],
        )
    cross_kept, cross_sends = fold_square(
        spot, cross_kept, [after(item, *self_sends) for item in cross_moved]
    )
    cross_moved = move_layers(cross_sends)
    ffn_total = add_all(ffn_kept, ffn_moved)
    cross_total = add_all(cross_kept, cross_moved)
    self_kept, self_sends = fold_square(
        spot, self_kept, [after(item, *cross_sends) for item in self_moved]
    )
    self_moved = move_layers(self_sends)
    self_total = add_all(self_kept, self_moved)

    def block(values, index):
        return values[:, index * model : (index + 1) * model]

    summed_qkv = jnp.stack(
        [block(self_total, i) for i in range(3)] + [block(cross_total, i) for i in range(3)]
    )
    summed_out = jnp.stack([block(self_total, 3), block(cross_total, 3)])
    summed_ffn_in = ffn_total[:, :hidden]
    summed_ffn_out = (
        ffn_total[:, hidden:].reshape(rows, pieces, model).transpose(1, 0, 2).reshape(-1, model)
    )
    summed_vector = self_total[:, 4 * model : 4 * model + vector_master.shape[0]].T
    qkv_first_new, qkv_second_new, qkv_master_new, qkv_copy = adamw(
        qkv_master, summed_qkv * grad_scale, qkv_first, qkv_second, 0.04
    )
    out_first_new, out_second_new, out_master_new, out_copy = adamw(
        out_master, summed_out * grad_scale, out_first, out_second, 0.3
    )
    ffn_in_first_new, ffn_in_second_new, ffn_in_master_new, ffn_in_copy = adamw(
        ffn_in_master, summed_ffn_in * grad_scale, ffn_in_first, ffn_in_second, 0.04
    )
    ffn_out_first_new, ffn_out_second_new, ffn_out_master_new, ffn_out_copy = adamw(
        ffn_out_master, summed_ffn_out * grad_scale, ffn_out_first, ffn_out_second, 0.02
    )
    vector_first_new, vector_second_new, vector_master_new, vector_copy = adamw(
        vector_master, summed_vector * grad_scale, vector_first, vector_second, 0.35
    )
    return (
        layer_out,
        tokens_grad,
        encoded_grad,
        qkv_first_new,
        qkv_second_new,
        qkv_master_new,
        qkv_copy,
        out_first_new,
        out_second_new,
        out_master_new,
        out_copy,
        ffn_in_first_new,
        ffn_in_second_new,
        ffn_in_master_new,
        ffn_in_copy,
        ffn_out_first_new,
        ffn_out_second_new,
        ffn_out_master_new,
        ffn_out_copy,
        vector_first_new,
        vector_second_new,
        vector_master_new,
        vector_copy,
    )


def solution(mesh):
    return jax.shard_map(
        body,
        mesh=mesh,
        in_specs=(
            P(("dp", "fsdp"), None),
            P(("dp", "fsdp"), None),
            P(("dp", "fsdp"), None),
            P(("dp", "fsdp"), None),
            P(("dp", "fsdp"), None),
            P(None, ("dp", "fsdp"), None),
            P(None, ("dp", "fsdp"), None),
            P(None, ("dp", "fsdp"), None),
            P(None, ("dp", "fsdp"), None),
            P(None, ("dp", "fsdp"), None),
            P(None, ("dp", "fsdp"), None),
            P(("dp", "fsdp"), None),
            P(("dp", "fsdp"), None),
            P(("dp", "fsdp"), None),
            P(("dp", "fsdp"), None),
            P(("dp", "fsdp"), None),
            P(("dp", "fsdp"), None),
            P(None, ("dp", "fsdp")),
            P(None, ("dp", "fsdp")),
            P(None, ("dp", "fsdp")),
        ),
        out_specs=(
            P(("dp", "fsdp"), None),
            P(("dp", "fsdp"), None),
            P(("dp", "fsdp"), None),
            P(None, ("dp", "fsdp"), None),
            P(None, ("dp", "fsdp"), None),
            P(None, ("dp", "fsdp"), None),
            P(None, ("dp", "fsdp"), None),
            P(None, ("dp", "fsdp"), None),
            P(None, ("dp", "fsdp"), None),
            P(None, ("dp", "fsdp"), None),
            P(None, ("dp", "fsdp"), None),
            P(("dp", "fsdp"), None),
            P(("dp", "fsdp"), None),
            P(("dp", "fsdp"), None),
            P(("dp", "fsdp"), None),
            P(("dp", "fsdp"), None),
            P(("dp", "fsdp"), None),
            P(("dp", "fsdp"), None),
            P(("dp", "fsdp"), None),
            P(None, ("dp", "fsdp")),
            P(None, ("dp", "fsdp")),
            P(None, ("dp", "fsdp")),
            P(None, ("dp", "fsdp")),
        ),
        check_vma=False,
    )
```

```python
import functools
import math

import jax
import jax.numpy as jnp
from jax import lax
from jax.experimental import pallas as pl
from jax.experimental.pallas import tpu as pltpu
from jax.sharding import PartitionSpec as P

HEADS = 8
STEP = 5
SEGMENTS = 10
norm_eps = 1e-05
beta_first = 0.5
beta_second = 0.5
adam_eps = 1e-08
weight_decay = 0.01
mask_fill = -1000000000.0
LOW = jnp.bfloat16
FULL = jnp.float32


def dot_nn(left, right):
    return lax.dot_general(left, right, (((1,), (0,)), ((), ())), preferred_element_type=FULL)


def dot_nt(left, right):
    return lax.dot_general(left, right, (((1,), (1,)), ((), ())), preferred_element_type=FULL)


def dot_tn(left, right):
    return lax.dot_general(left, right, (((0,), (0,)), ((), ())), preferred_element_type=FULL)


def head_masks(width, group, factor):
    lane = lax.broadcasted_iota(jnp.int32, (1, group * width), 1) // width
    return [jnp.where(lane == h, factor, 0.0).astype(LOW) for h in range(group)]


def window(start, size, total):
    return pl.multiple_of(jnp.minimum(start // 16 * 16, total - size), 16)


def inside(base, size, begin, end):
    place = lax.broadcasted_iota(jnp.int32, (size, 1), 0) + base
    return (place >= begin) & (place < end)


def each_span(row_starts, col_starts, total, same, work):
    def segment(s, carry):
        row_begin, row_end = row_starts[s], row_starts[s + 1]
        col_begin, col_end = col_starts[s], col_starts[s + 1]
        row_short = row_end - window(row_begin, 128, total) <= 128
        col_short = col_end - window(col_begin, 128, total) <= 128
        for row_span in (128, 256):
            for col_span in (128, 256):
                if same and row_span != col_span:
                    continue
                wanted = row_short if row_span == 128 else jnp.logical_not(row_short)
                if not same:
                    other = col_short if col_span == 128 else jnp.logical_not(col_short)
                    wanted = jnp.logical_and(wanted, other)

                @pl.when(wanted)
                def _(row_span=row_span, col_span=col_span):
                    row_base = window(row_begin, row_span, total)
                    col_base = window(col_begin, col_span, total)
                    work(
                        s,
                        pl.ds(row_base, row_span),
                        pl.ds(col_base, col_span),
                        inside(row_base, row_span, row_begin, row_end),
                        inside(col_base, col_span, col_begin, col_end),
                        row_span,
                    )

        return carry

    lax.fori_loop(0, SEGMENTS, segment, 0)


def attend_forward(row_starts, col_starts, q_ref, k_ref, v_ref, out_ref, sums_ref):
    total, model = q_ref.shape
    width = model // HEADS
    group = 256 // width
    scales = head_masks(width, group, 1.0 / math.sqrt(width))
    parts = [slice(g * 256, (g + 1) * 256) for g in range(HEADS // group)]

    def work(s, rows, cols, row_mask, col_mask, span):
        raw = []
        for lanes in parts:
            query, keys = q_ref[rows, lanes], k_ref[cols, lanes]
            stacked = jnp.concatenate([query * scale for scale in scales], axis=0)
            raw.append(dot_nt(keys, stacked))
        turned = [v_ref[cols, lanes].T for lanes in parts]
        probs = []
        for g, item in enumerate(raw):
            scores = jnp.where(col_mask, item, mask_fill)
            largest = jnp.max(scores, axis=0, keepdims=True)
            expo = jnp.exp(scores - largest)
            totals = jnp.sum(expo, axis=0, keepdims=True)
            sums_ref[pl.ds(len(parts) * s + g, 1), : group * span] = largest + jnp.log(totals)
            probs.append((expo * (1.0 / totals)).astype(LOW))
        mixed = [
            [
                dot_nn(side[h * width : (h + 1) * width], prob[:, h * span : (h + 1) * span])
                for h in range(group)
            ]
            for side, prob in zip(turned, probs)
        ]
        for lanes, items in zip(parts, mixed):
            value = jnp.concatenate(items, axis=0).T
            old = out_ref[rows, lanes].astype(FULL)
            out_ref[rows, lanes] = jnp.where(row_mask, value, old).astype(LOW)

    each_span(row_starts, col_starts, total, row_starts is col_starts, work)


def attend_backward(
    row_starts, col_starts, q_ref, k_ref, v_ref, grad_ref, sums_ref, dq_ref, dk_ref, dv_ref
):
    total, model = q_ref.shape
    width = model // HEADS
    group = 256 // width
    factor = 1.0 / math.sqrt(width)
    scales = head_masks(width, group, factor)
    picks = head_masks(width, group, 1.0)
    parts = [slice(g * 256, (g + 1) * 256) for g in range(HEADS // group)]

    def work(s, rows, cols, row_mask, col_mask, span):
        stacks, grads, raw, grad_probs = [], [], [], []
        for lanes in parts:
            query, keys, values = q_ref[rows, lanes], k_ref[cols, lanes], v_ref[cols, lanes]
            grad = jnp.where(row_mask, grad_ref[rows, lanes].astype(FULL), 0.0).astype(LOW)
            stacks.append(jnp.concatenate([query * scale for scale in scales], axis=0))
            grads.append(jnp.concatenate([grad * item for item in picks], axis=0))
            raw.append(dot_nt(keys, stacks[-1]))
            grad_probs.append(dot_nt(values, grads[-1]))
        grad_values, grad_scores = [], []
        for g, (item, grad_prob) in enumerate(zip(raw, grad_probs)):
            scores = jnp.where(col_mask, item, mask_fill)
            log_sums = sums_ref[pl.ds(len(parts) * s + g, 1), : group * span]
            probs = jnp.exp(scores - log_sums)
            grad_values.append(dot_nn(probs.astype(LOW), grads[g]))
            weighted = probs * grad_prob
            inner = jnp.sum(weighted, axis=0, keepdims=True)
            grad_scores.append((weighted - probs * inner).astype(LOW))
        grad_keys, grad_queries = [], []
        for lanes, item, stacked in zip(parts, grad_scores, stacks):
            grad_keys.append(dot_nn(item, stacked))
            turned = k_ref[cols, lanes].T
            grad_queries.append(
                [
                    dot_nn(turned[h * width : (h + 1) * width], item[:, h * span : (h + 1) * span])
                    for h in range(group)
                ]
            )
        for g, lanes in enumerate(parts):
            grad_query = jnp.concatenate(grad_queries[g], axis=0).T * factor
            for ref, place, mask, value in (
                (dq_ref, rows, row_mask, grad_query),
                (dk_ref, cols, col_mask, grad_keys[g]),
                (dv_ref, cols, col_mask, grad_values[g]),
            ):
                old = ref[place, lanes].astype(FULL)
                ref[place, lanes] = jnp.where(mask, value, old).astype(LOW)

    each_span(row_starts, col_starts, total, row_starts is col_starts, work)


def normalize(values):
    center = values - jnp.mean(values, axis=-1, keepdims=True)
    inverse = lax.rsqrt(jnp.mean(center * center, axis=-1, keepdims=True) + norm_eps)
    return center * inverse, inverse


def normalize_back(grad, gain, unit, inverse):
    scaled = grad * (1.0 + gain)
    mean = jnp.mean(scaled, axis=-1, keepdims=True)
    along = jnp.mean(scaled * unit, axis=-1, keepdims=True)
    return (scaled - mean - unit * along) * inverse


def column_sum(values):
    return jnp.sum(values.astype(FULL), axis=0, keepdims=True)


STEP_ROWS = 512


def row_steps(total, step, size=256):
    def run(i, carry):
        step(pl.ds(pl.multiple_of(i * size, size), size))
        return carry

    lax.fori_loop(0, total // size, run, 0)


def load_weights(place, depth, sources, targets, semaphores):
    if len(sources) == 1:
        offset = 0
        for target, semaphore in zip(targets, semaphores):
            source = sources[0].at[:, offset : offset + target.shape[1]]
            offset += target.shape[1]
            pltpu.make_async_copy(source, target, semaphore).start()
        return
    half = len(sources) // 2
    for k, source in enumerate(sources):
        base = (k % half) * 2 * depth + k // half
        for layer in range(depth):
            other = place ^ (base + 2 * layer)
            offset = 0
            for target, semaphore in zip(targets, semaphores):
                rows = source.shape[1]
                span = target.shape[1]
                to_rows = pl.ds(pl.multiple_of(other * rows, rows), rows)
                pltpu.make_async_copy(
                    source.at[layer, :, offset : offset + span], target.at[to_rows, :], semaphore
                ).start()
                offset += span


def await_weights(target, semaphore):
    pltpu.make_async_copy(target, target, semaphore).wait()


def store_grad(refs, core, lanes, value):
    value = value.astype(LOW)
    if len(refs) == 1:
        refs[0][:, lanes] = value
        return
    sent, kept = refs
    chips, rows = kept.shape[0], kept.shape[1]
    parts = value.reshape(chips, 2, rows, value.shape[1])
    first = core == 0
    kept[:, :, lanes] = jnp.where(first, parts[:, 0], parts[:, 1])
    sent[:, :, lanes] = jnp.where(first, parts[:, 1], parts[:, 0])


def self_forward_kernel(count, depth, place, row_starts, tokens, *rest):
    sources = rest[:count]
    weights, vectors, queries, keys, values, mixed, sums, semaphores = rest[count:]
    model = tokens.shape[1]
    load_weights(place[0], depth, sources, [weights], [semaphores.at[0]])
    await_weights(weights, semaphores.at[0])
    turned = weights[:, 3 * model : 3 * model + 128].astype(FULL).T
    vectors[...] = turned[: vectors.shape[0]]

    def project(rows):
        block = tokens[rows, :]
        queries[rows, :] = (dot_nn(block, weights[:, :model]) + vectors[0:1, :]).astype(LOW)
        keys[rows, :] = dot_nn(block, weights[:, model : 2 * model]).astype(LOW)
        values[rows, :] = (
            dot_nn(block, weights[:, 2 * model : 3 * model]) + vectors[1:2, :]
        ).astype(LOW)

    row_steps(tokens.shape[0], project)
    attend_forward(row_starts, row_starts, queries, keys, values, mixed, sums)


def cross_project_kernel(count, depth, place, tokens, encoded, mixed, vectors, *rest):
    sources = rest[:count]
    weights, unit_one, inverse_one, queries, keys, values, semaphores = rest[count:]
    model = tokens.shape[1]
    load_weights(place[0], depth, sources, [weights], [semaphores.at[0]])
    await_weights(weights, semaphores.at[0])

    def project(rows):
        block = encoded[rows, :]
        keys[rows, :] = dot_nn(block, weights[:, 2 * model : 3 * model]).astype(LOW)
        values[rows, :] = (
            dot_nn(block, weights[:, 3 * model : 4 * model]) + vectors[4:5, :]
        ).astype(LOW)
        summed = tokens[rows, :].astype(FULL) + dot_nn(mixed[rows, :], weights[:, :model])
        unit, inverse = normalize(summed + vectors[2:3, :])
        unit_one[rows, :] = unit
        inverse_one[rows, :] = inverse
        low = (unit * (1.0 + vectors[7:8, :]) + vectors[10:11, :]).astype(LOW)
        queries[rows, :] = (dot_nn(low, weights[:, model : 2 * model]) + vectors[3:4, :]).astype(LOW)

    row_steps(tokens.shape[0], project, 512)


def cross_attend_kernel(row_starts, col_starts, queries, keys, values, cross_mixed, sums):
    attend_forward(row_starts, col_starts, queries, keys, values, cross_mixed, sums)


def cross_finish_kernel(unit_one, cross_mixed, weights, vectors, unit_two, inverse_two):
    model = cross_mixed.shape[1]

    def finish(rows):
        first = unit_one[rows, :] * (1.0 + vectors[7:8, :]) + vectors[10:11, :]
        summed = first + dot_nn(cross_mixed[rows, :], weights[:, 4 * model : 5 * model])
        unit, inverse = normalize(summed + vectors[5:6, :])
        unit_two[rows, :] = unit
        inverse_two[rows, :] = inverse

    row_steps(unit_one.shape[0], finish, 512)


gelu_scale = math.sqrt(2.0 / math.pi)
gelu_cubic = 0.044715


def ffn_kernel(count, depth, blocks, place, unit_two, inverse_two, cotangent, vectors, *rest):
    sources = rest[:count]
    (
        layer_out, grad_sum, grad_out, sums, bias_sums, *grads,
        first_weights, second_weights, hidden, grad_ffn, grad_pre, slopes, semaphores,
    ) = rest[count:]
    model = unit_two.shape[1]
    pieces = blocks
    load_ffn(place[0], depth, sources, first_weights, second_weights, semaphores)
    sums[...] = jnp.zeros_like(sums)
    bias_sums[...] = jnp.zeros_like(bias_sums)
    await_weights(first_weights, semaphores.at[0])
    await_weights(second_weights, semaphores.at[1])

    def step(rows):
        unit = unit_two[rows, :]
        second = unit * (1.0 + vectors[8:9, :]) + vectors[11:12, :]
        low = second.astype(LOW)
        total = second + vectors[6:7, :]
        for j in range(pieces):
            lanes = slice(j * model, (j + 1) * model)
            pre = dot_nn(low, first_block(first_weights, j, model)) + vectors[13 + j : 14 + j, :]
            square = pre * pre
            bend = jnp.tanh(gelu_scale * pre * (1.0 + gelu_cubic * square))
            half = 0.5 * (1.0 + bend)
            value = (pre * half).astype(LOW)
            hidden[rows, lanes] = value
            inner = gelu_scale * (1.0 + 3.0 * gelu_cubic * square)
            slopes[:, lanes] = half + 0.5 * pre * (1.0 - bend * bend) * inner
            total = total + dot_nn(value, second_block(second_weights, j, model))
        unit_three, inverse_three = normalize(total)
        layer_out[rows, :] = (unit_three * (1.0 + vectors[9:10, :]) + vectors[12:13, :]).astype(LOW)
        upper = cotangent[rows, :].astype(FULL)
        third = normalize_back(upper, vectors[9:10, :], unit_three, inverse_three)
        third_low = third.astype(LOW)
        grad_ffn[rows, :] = third_low
        sums[0:1, :] += column_sum(third_low)
        sums[1:2, :] += column_sum(upper * unit_three)
        sums[2:3, :] += column_sum(upper)
        below = third
        for j in range(pieces):
            lanes = slice(j * model, (j + 1) * model)
            pre = (dot_nt(third_low, second_block(second_weights, j, model)) * slopes[:, lanes]).astype(LOW)
            grad_pre[rows, lanes] = pre
            bias_sums[j : j + 1, :] += column_sum(pre)
            below = below + dot_nt(pre, first_block(first_weights, j, model))
        sums[3:4, :] += column_sum(below * unit)
        sums[4:5, :] += column_sum(below)
        second_sum = normalize_back(below, vectors[8:9, :], unit, inverse_two[rows, :])
        grad_sum[rows, :] = second_sum
        out_low = second_sum.astype(LOW)
        grad_out[rows, :] = out_low
        sums[5:6, :] += column_sum(out_low)

    row_steps(unit_two.shape[0], step, STEP_ROWS)
    core = place[0] % 2
    second_low = (unit_two[...] * (1.0 + vectors[8:9, :]) + vectors[11:12, :]).astype(LOW)

    def block_grads(j, carry):
        lanes = pl.ds(pl.multiple_of(j * model, model), model)
        store_grad(grads, core, lanes, dot_tn(second_low, grad_pre[:, lanes]))
        store_ffn_out(grads, core, j, pieces, dot_tn(hidden[:, lanes], grad_ffn[...]))
        return carry

    lax.fori_loop(0, pieces, block_grads, 0)


def load_ffn(place, depth, sources, first_weights, second_weights, semaphores):
    if len(sources) == 1:
        first_width = first_weights.shape[1]
        pltpu.make_async_copy(
            sources[0].at[:, :first_width], first_weights, semaphores.at[0]
        ).start()
        pieces = first_width // first_weights.shape[0]
        model = first_weights.shape[0]
        for j in range(pieces):
            pltpu.make_async_copy(
                sources[0].at[:, first_width + j * model : first_width + (j + 1) * model],
                second_weights.at[pl.ds(j * model, model), :],
                semaphores.at[1],
            ).start()
        return
    half = len(sources) // 2
    for k, source in enumerate(sources):
        base = (k % half) * 2 * depth + k // half
        pieces, rows = source.shape[1] // 2, source.shape[2]
        for layer in range(depth):
            other = place ^ (base + 2 * layer)
            to_rows = pl.ds(pl.multiple_of(other * rows, rows), rows)
            pltpu.make_async_copy(
                source.at[layer, :pieces], first_weights.at[:, to_rows, :], semaphores.at[0]
            ).start()
            pltpu.make_async_copy(
                source.at[layer, pieces:],
                second_weights.at[pl.ds(other * pieces, pieces)],
                semaphores.at[1],
            ).start()


def first_block(ref, j, model):
    return ref[j] if len(ref.shape) == 3 else ref[:, j * model : (j + 1) * model]


def second_block(ref, j, model):
    if len(ref.shape) == 2:
        return ref[j * model : (j + 1) * model, :]
    count = model // ref.shape[1]
    return ref[j * count : (j + 1) * count].reshape(model, model)


def store_ffn_out(refs, core, block, pieces, value):
    value = value.astype(LOW)
    model = value.shape[1]
    if len(refs) == 1:
        offset = pl.multiple_of((pieces + block) * model, model)
        refs[0][:, pl.ds(offset, model)] = value
        return
    sent, kept = refs
    rows = kept.shape[1]
    chips = kept.shape[0] // pieces
    parts = value.reshape(chips, 2, pieces, rows, model)
    first = core == 0
    place = pl.ds(block * chips, chips)
    for j in range(pieces):
        lanes = slice((pieces + j) * model, (pieces + j + 1) * model)
        kept[place, :, lanes] = jnp.where(first, parts[:, 0, j], parts[:, 1, j])
        sent[place, :, lanes] = jnp.where(first, parts[:, 1, j], parts[:, 0, j])


def cross_backward_kernel(
    row_starts, col_starts, queries, keys, values, grad_out, weights, sums_in, dq, dk, dv, grad_mixed
):
    model = queries.shape[1]

    def project(rows):
        low = dot_nt(grad_out[rows, :], weights[:, 4 * model : 5 * model]).astype(LOW)
        grad_mixed[rows, :] = low

    row_steps(queries.shape[0], project)
    attend_backward(row_starts, col_starts, queries, keys, values, grad_mixed, sums_in, dq, dk, dv)


def cross_grads_kernel(
    place, dq, dk, dv, weights, vectors, grad_sum, unit_one, inverse_one,
    encoded, cross_mixed, grad_out,
    first_sum, self_low, grad_mixed, sums, encoded_grad, *grads,
):
    model = dq.shape[1]
    sums[...] = jnp.zeros_like(sums)

    def finish(rows):
        query, key, value = dq[rows, :], dk[rows, :], dv[rows, :]
        sums[0:1, :] += column_sum(query)
        sums[1:2, :] += column_sum(value)
        encoded_grad[rows, :] = dot_nt(key, weights[:, 2 * model : 3 * model]) + dot_nt(
            value, weights[:, 3 * model : 4 * model]
        )
        upper = grad_sum[rows, :] + dot_nt(query, weights[:, model : 2 * model])
        unit = unit_one[rows, :]
        sums[2:3, :] += column_sum(upper * unit)
        sums[3:4, :] += column_sum(upper)
        below = normalize_back(upper, vectors[7:8, :], unit, inverse_one[rows, :])
        first_sum[rows, :] = below
        low = below.astype(LOW)
        self_low[rows, :] = low
        sums[4:5, :] += column_sum(low)
        grad_mixed[rows, :] = dot_nt(low, weights[:, :model]).astype(LOW)

    row_steps(dq.shape[0], finish)
    core = place[0] % 2
    first_low = (unit_one[...] * (1.0 + vectors[7:8, :]) + vectors[10:11, :]).astype(LOW)
    pairs = ((first_low, dq), (encoded, dk), (encoded, dv), (cross_mixed, grad_out))
    for j, (left, right) in enumerate(pairs):
        lanes = slice(j * model, (j + 1) * model)
        store_grad(grads, core, lanes, dot_tn(left[...], right[...]))


def self_backward_kernel(
    place, row_starts, queries, keys, values, grad_mixed, sums_in, tokens, mixed, self_low,
    cross_sums, ffn_sums, bias_sums, dq, dk, dv, *rest,
):
    *grads, stack = rest
    attend_backward(row_starts, row_starts, queries, keys, values, grad_mixed, sums_in, dq, dk, dv)
    model = dq.shape[1]
    core = place[0] % 2
    pairs = ((tokens, dq), (tokens, dk), (tokens, dv), (mixed, self_low))
    for j, (left, right) in enumerate(pairs):
        lanes = slice(j * model, (j + 1) * model)
        store_grad(grads, core, lanes, dot_tn(left[...], right[...]))
    stack[...] = jnp.zeros_like(stack)
    stack[0:1, :] = column_sum(dq[...])
    stack[1:2, :] = column_sum(dv[...])
    order = (
        (2, cross_sums, 4), (3, cross_sums, 0), (4, cross_sums, 1), (5, ffn_sums, 5),
        (6, ffn_sums, 0), (7, cross_sums, 2), (8, ffn_sums, 3), (9, ffn_sums, 1),
        (10, cross_sums, 3), (11, ffn_sums, 4), (12, ffn_sums, 2),
    )
    for to, ref, at in order:
        stack[to : to + 1, :] = ref[at : at + 1, :]
    extra = bias_sums.shape[0]
    stack[13 : 13 + extra, :] = bias_sums[...]
    start = len(pairs) * model
    store_grad(grads, core, slice(start, start + 128), stack[...].T)


def tokens_grad_kernel(dq, dk, dv, first_sum, weights, tokens_grad):
    model = dq.shape[1]

    def finish(rows):
        below = first_sum[rows, :] + dot_nt(dq[rows, :], weights[:, :model])
        below = below + dot_nt(dk[rows, :], weights[:, model : 2 * model])
        tokens_grad[rows, :] = below + dot_nt(dv[rows, :], weights[:, 2 * model : 3 * model])

    row_steps(dq.shape[0], finish, 512)


def fold_core_kernel(shape, place, kept, received, own, *sends):
    dp_count, depth = shape
    at = place[0] // (2 * depth)
    for k, ref in enumerate((own, *sends)):
        spot = pl.ds((at ^ k) * depth, depth)
        value = kept[spot].astype(FULL) + received[spot].astype(FULL)
        ref[...] = value.astype(ref.dtype)


def fold_square_kernel(shape, place, kept, *rest):
    dp_count, depth = shape
    received, outs = rest[: dp_count - 1], rest[dp_count - 1 :]
    at = place[0] // 2 % depth
    for k, ref in enumerate(outs):
        spot = pl.ds(at ^ k, 1)
        value = kept[spot]
        for item in received:
            value = value + item[spot].astype(FULL)
        ref[...] = value[0].astype(ref.dtype)


def fold_halves_kernel(depth, place, kept, received, keep_first, send_first, keep_second, send_second):
    at = place[0] // (2 * depth)
    half = kept.shape[2] // 2
    low, high = slice(0, half), slice(half, 2 * half)
    for ref, lanes, offsets in (
        (keep_first, low, (0, 1)),
        (send_first, low, (2, 3)),
        (keep_second, high, (0, 2)),
        (send_second, high, (1, 3)),
    ):
        for slot, k in enumerate(offsets):
            spot = pl.ds((at ^ k) * depth, depth)
            value = kept[spot, :, lanes].astype(FULL) + received[spot, :, lanes].astype(FULL)
            ref[slot] = value.astype(ref.dtype)


def fold_pairs_kernel(keep_first, got_first, keep_second, got_second, *outs):
    own_first, send_first, own_second, send_second = outs
    own_first[...] = keep_first[0] + got_first[0].astype(FULL)
    send_first[...] = (keep_first[1] + got_first[1].astype(FULL)).astype(LOW)
    own_second[...] = keep_second[0] + got_second[0].astype(FULL)
    send_second[...] = (keep_second[1] + got_second[1].astype(FULL)).astype(LOW)


def fold_layers_kernel(depth, place, first, got_first, second, got_second, cross, *rest):
    *got_cross, keep, send = rest
    at = place[0] // 2 % depth
    half = first.shape[2]
    for ref, offsets in ((keep, (0, 1)), (send, (2, 3))):
        for slot, k in enumerate(offsets):
            spot = pl.ds(at ^ k, 1)
            value = first[spot] + got_first[spot].astype(FULL)
            ref[slot, :, :half] = value[0].astype(ref.dtype)
            value = second[spot] + got_second[spot].astype(FULL)
            ref[slot, :, half : 2 * half] = value[0].astype(ref.dtype)
            value = cross[spot]
            for item in got_cross:
                value = value + item[spot].astype(FULL)
            ref[slot, :, 2 * half :] = value[0].astype(ref.dtype)


def fold_last_kernel(keep, got, own, send):
    own[...] = keep[0] + got[0].astype(FULL)
    send[...] = (keep[1] + got[1].astype(FULL)).astype(LOW)


def update_into(outs, index, state, grad, rate):
    for ref, value in zip(outs, adamw(state[0][index], grad, state[1][index], state[2][index], rate)):
        ref[index] = value


def ffn_update_kernel(grad_scale, own, got, *rest):
    first_state, second_state, outs = rest[:3], rest[3:6], rest[6:]
    rows, width = first_state[0].shape
    model = second_state[0].shape[1]
    grad = (own[:, :width] + got[:, :width].astype(FULL)) * grad_scale
    update_into(outs[:4], (slice(None), slice(None)), first_state, grad, 0.04)
    for j in range(second_state[0].shape[0] // rows):
        lanes = slice(width + j * model, width + (j + 1) * model)
        grad = (own[:, lanes] + got[:, lanes].astype(FULL)) * grad_scale
        index = (slice(j * rows, (j + 1) * rows), slice(None))
        update_into(outs[4:], index, second_state, grad, 0.02)


def final_update_kernel(grad_scale, start, own, got, kept, *rest):
    moved, states, outs = rest[:-21], rest[-21:-12], rest[-12:]
    qkv_state, out_state, vector_state = states[:3], states[3:6], states[6:]
    model = qkv_state[0].shape[2]

    def self_grad(lanes):
        value = kept[:, lanes]
        for item in moved:
            value = value + item[:, lanes].astype(FULL)
        return value * grad_scale

    def cross_grad(index):
        lanes = slice(start + index * model, start + (index + 1) * model)
        return (own[:, lanes] + got[:, lanes].astype(FULL)) * grad_scale

    for j in range(4):
        grad = self_grad(slice(j * model, (j + 1) * model))
        if j < 3:
            update_into(outs[:4], j, qkv_state, grad, 0.04)
            update_into(outs[:4], 3 + j, qkv_state, cross_grad(j), 0.04)
        else:
            update_into(outs[4:8], 0, out_state, grad, 0.3)
            update_into(outs[4:8], 1, out_state, cross_grad(j), 0.3)
    grad = self_grad(slice(4 * model, 4 * model + vector_state[0].shape[1]))
    update_into(outs[8:], (slice(None), slice(None)), vector_state, grad, 0.35)


LIMITS = {
    "fold_halves": 16,
    "fold_pairs": 14,
    "fold_layers": 12,
    "fold_last": 8,
    "ffn_update": 8,
    "final_update": 10,
    "fold_core": 12,
    "fold_square": 10,
    "self_forward": 14,
    "cross_project": 14,
    "cross_attend": 10,
    "cross_finish": 9,
    "ffn": 32.8,
    "cross_backward": 13,
    "cross_grads": 20,
    "self_backward": 16,
    "tokens_grad": 11,
}


def out_kind(item):
    if len(item) == 3:
        return pltpu.VMEM(item[0], item[1])
    return jax.ShapeDtypeStruct(*item)


def keep(item):
    return (item[0], item[1], True)


def limit(name):
    return pltpu.CompilerParams(vmem_limit_bytes=int(LIMITS[name] * (1 << 20)))


def pinned(sources):
    if len(sources) == 1:
        return sources
    return [pltpu.with_memory_space_constraint(item, pltpu.VMEM) for item in sources]


def source_spec(sources):
    return pl.BlockSpec(memory_space=pltpu.VMEM if len(sources) > 1 else pl.ANY)


def call(kernel, name, scalars, arrays, outs, flops, sources=(), scratch=()):
    specs = [pl.BlockSpec(memory_space=pltpu.SMEM)] * len(scalars)
    specs += [pl.BlockSpec(memory_space=pltpu.VMEM)] * len(arrays)
    specs += [source_spec(sources)] * len(sources)
    shapes = [out_kind(item) for item in outs]
    moved = sum(item.size * item.dtype.itemsize for item in [*arrays, *sources])
    return pl.pallas_call(
        kernel,
        out_shape=shapes,
        in_specs=specs,
        out_specs=[pl.BlockSpec(memory_space=pltpu.VMEM)] * len(outs),
        scratch_shapes=list(scratch),
        compiler_params=limit(name),
        cost_estimate=pl.CostEstimate(flops=flops, transcendentals=0, bytes_accessed=moved),
        name=name,
    )(*scalars, *arrays, *pinned(sources))


def segment_starts(ids):
    marks = jnp.arange(SEGMENTS + 1, dtype=ids.dtype)
    return jnp.sum((ids[None, :] < marks[:, None]).astype(jnp.int32), axis=1)


def adamw(master, grad, first, second, rate):
    first_new = beta_first * first + (1.0 - beta_first) * grad
    second_new = beta_second * second + (1.0 - beta_second) * grad * grad
    first_hat = first_new / (1.0 - beta_first**STEP)
    second_hat = second_new / (1.0 - beta_second**STEP)
    master_new = master - rate * (
        first_hat / (jnp.sqrt(second_hat) + adam_eps) + weight_decay * master
    )
    return (first_new, second_new, master_new, master_new.astype(jnp.bfloat16))


AXES = ("dp", "fsdp")


def exchange(values, offset):
    count = lax.axis_size("dp") * lax.axis_size("fsdp")
    return lax.ppermute(values, AXES, [(i, i ^ offset) for i in range(count)])


def after(value, *others):
    return lax.optimization_barrier((value, *others))[0]


def layer_stack(piece):
    depth = lax.axis_size("fsdp") // 2
    return jnp.stack([piece] + [exchange(piece, 2 * k) for k in range(1, depth)])


def layer_double(piece, gate=None):
    stack, step = piece[None], 1
    while step < lax.axis_size("fsdp") // 2:
        if gate is not None and step > 1:
            stack = after(stack, gate)
        stack = jnp.concatenate([stack, exchange(stack, 2 * step)])
        step *= 2
    return stack


def square_list(stack):
    dp_count, fsdp_count = lax.axis_size("dp"), lax.axis_size("fsdp")
    return [stack] + [exchange(stack, fsdp_count * k) for k in range(1, dp_count)]


def forward_list(stack):
    stride, near = lax.axis_size("fsdp"), [stack]
    for k in range(1, lax.axis_size("dp")):
        near.append(None if k & (k - 1) else exchange(stack, stride * k))
    return near


def forward_rest(near, gate):
    stride = lax.axis_size("fsdp")
    for k, item in enumerate(near):
        if item is None:
            high = 1 << (k.bit_length() - 1)
            near[k] = exchange(after(near[k - high], gate), stride * high)
    return near


def core_list(near):
    return near + [exchange(item, 1) for item in near]


def ordered(parts, place):
    half = len(parts) // 2
    both = jnp.stack([jnp.stack(parts[:half]), jnp.stack(parts[half:])], axis=2)
    flat = both.reshape((-1,) + both.shape[3:])
    return flat[jnp.arange(flat.shape[0]) ^ place]


def pick(values, index, axis):
    return lax.dynamic_index_in_dim(values, index, axis, keepdims=False)


def split_core(grads):
    if len(grads) == 2:
        return grads
    count = lax.axis_size("dp") * lax.axis_size("fsdp")
    core = lax.axis_index("fsdp") % 2
    parts = grads[0].reshape((count // 2, 2, -1) + grads[0].shape[1:])
    return pick(parts, 1 - core, 1), pick(parts, core, 1)


def fold_core(spot, kept, received):
    dp_count, depth = lax.axis_size("dp"), lax.axis_size("fsdp") // 2
    shape = (depth,) + kept.shape[1:]
    if kept.shape[1] % 16:
        place = lax.axis_index("dp")
        pair = (kept.astype(FULL) + received.astype(FULL)).reshape((dp_count,) + shape)
        sends = [pick(pair, place ^ k, 0).astype(LOW) for k in range(1, dp_count)]
        return pick(pair, place, 0), sends
    own, *sends = call(
        functools.partial(fold_core_kernel, (dp_count, depth)), "fold_core", [spot],
        [kept, received], [(shape, FULL)] + [(shape, LOW)] * (dp_count - 1), kept.size,
    )
    return own, sends


def fold_square(spot, kept, received):
    dp_count, depth = lax.axis_size("dp"), lax.axis_size("fsdp") // 2
    shape = kept.shape[1:]
    if kept.shape[1] % 16:
        place = lax.axis_index("fsdp") // 2
        square = add_all(kept, received)
        sends = [pick(square, place ^ k, 0).astype(LOW) for k in range(1, depth)]
        return pick(square, place, 0), sends
    own, *sends = call(
        functools.partial(fold_square_kernel, (dp_count, depth)), "fold_square", [spot],
        [kept, *received], [(shape, FULL)] + [(shape, LOW)] * (depth - 1), kept.size,
    )
    return own, sends


def move_square(sends):
    stride = lax.axis_size("fsdp")
    return [exchange(item, stride * (k + 1)) for k, item in enumerate(sends)]


def move_layers(sends):
    return [exchange(item, 2 * (k + 1)) for k, item in enumerate(sends)]


def add_all(kept, moved):
    for item in moved:
        kept = kept + item.astype(FULL)
    return kept


def body(
    tokens,
    encoded,
    cotangent,
    target_ids,
    source_ids,
    qkv_master,
    qkv_first,
    qkv_second,
    out_master,
    out_first,
    out_second,
    ffn_in_master,
    ffn_in_first,
    ffn_in_second,
    ffn_out_master,
    ffn_out_first,
    ffn_out_second,
    vector_master,
    vector_first,
    vector_second,
):
    total, model = tokens.shape
    dp_count, fsdp_count = lax.axis_size("dp"), lax.axis_size("fsdp")
    count, depth = dp_count * fsdp_count, fsdp_count // 2
    rows = model // count
    aligned = rows % 16 == 0
    place = lax.axis_index("dp") * fsdp_count + lax.axis_index("fsdp")
    spot = place.reshape(1).astype(jnp.int32)
    low_qkv = after(qkv_master, spot).astype(LOW)
    low_out = out_master.astype(LOW)
    low_vector = jnp.pad(vector_master.astype(LOW).T, ((0, 0), (0, 128 - vector_master.shape[0])))
    pieces = ffn_in_master.shape[1] // model

    def to_columns(values):
        return values.reshape(-1, rows, model).transpose(1, 0, 2).reshape(rows, -1)

    self_piece = jnp.concatenate([low_qkv[0], low_qkv[1], low_qkv[2], low_vector], axis=1)
    cross_piece = jnp.concatenate([low_out[0], low_qkv[3], low_qkv[4], low_qkv[5], low_out[1]], axis=1)
    ffn_piece = jnp.concatenate(
        [ffn_in_master.astype(LOW), to_columns(ffn_out_master.astype(LOW))], axis=1
    )
    if aligned:
        ffn_piece = jnp.concatenate(
            [
                ffn_in_master.astype(LOW).reshape(rows, pieces, model).transpose(1, 0, 2),
                ffn_out_master.astype(LOW).reshape(pieces, rows, model),
            ]
        )
    row_starts, col_starts = segment_starts(target_ids[0]), segment_starts(source_ids[0])

    def sources_of(parts):
        if aligned:
            return parts
        flat = ordered(parts, place)
        return [flat.reshape(model, -1)]

    def ffn_sources_of(parts):
        if aligned:
            return parts
        flat = ordered(parts, place)
        width = pieces * model
        second = flat[:, :, width:].reshape(count, rows, pieces, model).transpose(0, 2, 1, 3)
        second = second.reshape(pieces, model, model).transpose(1, 0, 2).reshape(model, -1)
        return [jnp.concatenate([flat[:, :, :width].reshape(model, -1), second], axis=1)]

    wide, tall, thin = ((total, model), LOW), ((total, model), FULL), ((total, 1), FULL)
    log_sums = ((SEGMENTS * (model // 256), 1024), FULL)
    small = ((8, model), FULL)
    unit = 2 * total * model * model
    attend = 2 * SEGMENTS * HEADS * 256 * 256 * 256
    wait_one, wait_two = pltpu.SemaphoreType.DMA((1,)), pltpu.SemaphoreType.DMA((2,))

    def grad_outs(columns):
        if aligned:
            return [((count // 2, rows, columns), LOW)] * 2
        return [((model, columns), LOW)]

    self_stack = layer_stack(self_piece)
    self_near = square_list(self_stack)
    cross_own = layer_double(after(cross_piece, self_stack))
    ffn_own = layer_double(after(ffn_piece, self_stack), cross_own)
    self_parts = core_list(self_near)
    cross_columns = cross_piece.shape[1]
    cross_near = square_list(cross_own)
    ffn_near = forward_list(ffn_own)

    sources = sources_of(self_parts)
    (
        self_weights, vectors, queries, keys, values, mixed, self_sums,
    ) = call(
        functools.partial(self_forward_kernel, len(sources), depth), "self_forward",
        [spot, row_starts], [after(tokens, cross_own)],
        [
            keep(((model, self_piece.shape[1]), LOW)), ((24, model), FULL),
            keep(wide), keep(wide), keep(wide), keep(wide), keep(log_sums),
        ],
        3 * unit + 2 * attend, sources, [wait_one],
    )
    sources = sources_of(core_list([after(item, mixed) for item in cross_near]))
    cross_weights, unit_one, inverse_one, cross_queries, cross_keys, cross_values = call(
        functools.partial(cross_project_kernel, len(sources), depth), "cross_project", [spot],
        [tokens, encoded, mixed, vectors],
        [
            keep(((model, cross_columns), LOW)), keep(tall), thin, keep(wide), keep(wide),
            keep(wide),
        ],
        4 * unit, sources, [wait_one],
    )
    ffn_near = forward_rest(ffn_near, cross_queries)
    cross_mixed, cross_log = call(
        cross_attend_kernel, "cross_attend", [row_starts, col_starts],
        [cross_queries, cross_keys, cross_values], [keep(wide), keep(log_sums)], 2 * attend,
    )
    unit_two, inverse_two = call(
        cross_finish_kernel, "cross_finish", [], [unit_one, cross_mixed, cross_weights, vectors],
        [keep(tall), thin], unit,
    )
    gates = [mixed] * (dp_count // 2) + [cross_mixed] * (dp_count // 2)
    sources = ffn_sources_of(core_list([after(*pair) for pair in zip(ffn_near, gates)]))
    hidden = pieces * model
    if aligned:
        ffn_scratch = [
            pltpu.VMEM((pieces, model, model), LOW), pltpu.VMEM((count * pieces, rows, model), LOW),
        ]
    else:
        ffn_scratch = [pltpu.VMEM((model, hidden), LOW), pltpu.VMEM((hidden, model), LOW)]
    (
        layer_out, grad_sum, grad_cross_out, ffn_sums, bias_sums, *ffn_grads
    ) = call(
        functools.partial(ffn_kernel, len(sources), depth, pieces), "ffn", [spot],
        [unit_two, inverse_two, cotangent, vectors],
        [wide, keep(tall), keep(wide), small, small, *grad_outs(2 * hidden)],
        (5 * pieces + 1) * unit, sources,
        [
            *ffn_scratch,
            pltpu.VMEM((total, hidden), LOW), pltpu.VMEM((total, model), LOW),
            pltpu.VMEM((total, hidden), LOW),
            pltpu.VMEM((STEP_ROWS, hidden), FULL), wait_two,
        ],
    )
    if not aligned:
        first, second = ffn_grads[0][:, :hidden], ffn_grads[0][:, hidden:]
        second = second.reshape(model, pieces, model).transpose(1, 0, 2)
        second = second.reshape(count, pieces, rows, model).transpose(0, 2, 1, 3)
        ffn_grads = [jnp.concatenate([first, second.reshape(model, -1)], axis=1)]
    sent, kept = split_core(ffn_grads)
    ffn_moved = exchange(sent, 1)
    cross_dq, cross_dk, cross_dv = call(
        cross_backward_kernel, "cross_backward", [row_starts, col_starts],
        [
            cross_queries, cross_keys, cross_values, after(grad_cross_out, sent), cross_weights,
            cross_log,
        ],
        [keep(wide), keep(wide), keep(wide)], 5 * attend, (), [pltpu.VMEM((total, model), LOW)],
    )
    fast = aligned and dp_count == 4 and depth == 4
    ffn_moved = after(ffn_moved, cross_dq)
    if fast:
        pair = (2, depth, rows, hidden)
        keep_first, send_first, keep_second, send_second = call(
            functools.partial(fold_halves_kernel, depth), "fold_halves", [spot], [kept, ffn_moved],
            [(pair, FULL), (pair, LOW), (pair, FULL), (pair, LOW)], 1,
        )
        ffn_sends = [send_first, send_second]
        got_first = exchange(send_first, 2 * fsdp_count)
        got_second = exchange(send_second, fsdp_count)
    else:
        ffn_kept, ffn_sends = fold_core(spot, kept, ffn_moved)
        ffn_moved = move_square(ffn_sends)
    first_sum, self_low, grad_mixed, cross_vector, encoded_grad, *cross_grads = call(
        cross_grads_kernel, "cross_grads", [spot],
        [
            after(cross_dq, *ffn_sends), cross_dk, cross_dv, cross_weights, vectors, grad_sum,
            unit_one, inverse_one, encoded, cross_mixed, grad_cross_out,
        ],
        [keep(tall), keep(wide), keep(wide), small, tall, *grad_outs(4 * model)], 8 * unit,
    )
    sent, kept = split_core(cross_grads)
    ffn_sends = [sent]
    if fast:
        half = (depth, rows, hidden)
        own_first, send_first, own_second, send_second = call(
            fold_pairs_kernel, "fold_pairs", [],
            [keep_first, after(got_first, sent), keep_second, got_second],
            [(half, FULL), (half, LOW), (half, FULL), (half, LOW)], 1,
        )
        ffn_sends = [send_first, send_second]
        got_first = exchange(send_first, fsdp_count)
        got_second = exchange(send_second, 2 * fsdp_count)
    cross_moved = exchange(after(sent, *ffn_sends), 1)
    cross_kept, cross_sends = fold_core(spot, kept, cross_moved)
    cross_moved = move_square(cross_sends)
    self_dq, self_dk, self_dv, *self_grads = call(
        self_backward_kernel, "self_backward", [spot, row_starts],
        [
            queries, keys, values, after(grad_mixed, *cross_sends, *ffn_sends), self_sums,
            tokens, mixed, self_low, cross_vector, ffn_sums, bias_sums,
        ],
        [keep(wide), keep(wide), keep(wide), *grad_outs(4 * model + 128)],
        5 * attend + 4 * unit, (), [pltpu.VMEM((128, model), FULL)],
    )
    sent, kept = split_core(self_grads)
    if fast:
        wide_pair = (2, rows, 2 * hidden + 4 * model)
        layer_keep, layer_send = call(
            functools.partial(fold_layers_kernel, depth), "fold_layers", [spot],
            [own_first, after(got_first, sent), own_second, got_second, cross_kept, *cross_moved],
            [(wide_pair, FULL), (wide_pair, LOW)], 1,
        )
        ffn_sends = [layer_send]
        layer_got = exchange(layer_send, 4)
        self_moved = exchange(after(sent, layer_send), 1)
    else:
        self_moved = exchange(sent, 1)
        ffn_kept, ffn_sends = fold_square(spot, ffn_kept, [after(item, sent) for item in ffn_moved])
        ffn_moved = move_layers(ffn_sends)
    (tokens_grad,) = call(
        tokens_grad_kernel, "tokens_grad", [],
        [after(self_dq, *ffn_sends), self_dk, self_dv, first_sum, self_weights], [tall], 3 * unit,
    )
    self_kept, self_sends = fold_core(spot, kept, after(self_moved, tokens_grad))
    self_moved = move_square(self_sends)
    grad_scale = 1.0 / math.sqrt(total * count)
    if fast:
        wide_row = wide_pair[1:]
        self_kept, self_sends = fold_square(spot, self_kept, self_moved)
        self_moved = move_layers(self_sends)
        layer_own, layer_send = call(
            fold_last_kernel, "fold_last", [], [layer_keep, after(layer_got, *self_sends)],
            [(wide_row, FULL), (wide_row, LOW)], 1,
        )
        layer_got = exchange(layer_send, 2)
        kinds = [FULL, FULL, FULL, LOW]
        ffn_out_state = (ffn_out_master, ffn_out_first, ffn_out_second)
        ffn_in_state = (ffn_in_master, ffn_in_first, ffn_in_second)
        ffn_new = call(
            functools.partial(ffn_update_kernel, grad_scale), "ffn_update", [],
            [layer_own, layer_got, *ffn_in_state, *ffn_out_state],
            [(ffn_in_master.shape, kind) for kind in kinds]
            + [(ffn_out_master.shape, kind) for kind in kinds], 1,
        )
        states = [
            qkv_master, qkv_first, qkv_second, out_master, out_first, out_second,
            vector_master.T, vector_first.T, vector_second.T,
        ]
        final_new = call(
            functools.partial(final_update_kernel, grad_scale, 2 * hidden), "final_update", [],
            [layer_own, layer_got, self_kept, *self_moved, *states],
            [(item.shape, kind) for item in states[::3] for kind in kinds], 1,
        )
        return (
            layer_out, tokens_grad, encoded_grad, *final_new[:8], *ffn_new,
            *[item.T for item in final_new[8:]],
        )
    cross_kept, cross_sends = fold_square(
        spot, cross_kept, [after(item, *self_sends) for item in cross_moved]
    )
    cross_moved = move_layers(cross_sends)
    ffn_total = add_all(ffn_kept, ffn_moved)
    cross_total = add_all(cross_kept, cross_moved)
    self_kept, self_sends = fold_square(
        spot, self_kept, [after(item, *cross_sends) for item in self_moved]
    )
    self_moved = move_layers(self_sends)
    self_total = add_all(self_kept, self_moved)

    def block(values, index):
        return values[:, index * model : (index + 1) * model]

    summed_qkv = jnp.stack(
        [block(self_total, i) for i in range(3)] + [block(cross_total, i) for i in range(3)]
    )
    summed_out = jnp.stack([block(self_total, 3), block(cross_total, 3)])
    summed_ffn_in = ffn_total[:, :hidden]
    summed_ffn_out = (
        ffn_total[:, hidden:].reshape(rows, pieces, model).transpose(1, 0, 2).reshape(-1, model)
    )
    summed_vector = self_total[:, 4 * model : 4 * model + vector_master.shape[0]].T
    qkv_first_new, qkv_second_new, qkv_master_new, qkv_copy = adamw(
        qkv_master, summed_qkv * grad_scale, qkv_first, qkv_second, 0.04
    )
    out_first_new, out_second_new, out_master_new, out_copy = adamw(
        out_master, summed_out * grad_scale, out_first, out_second, 0.3
    )
    ffn_in_first_new, ffn_in_second_new, ffn_in_master_new, ffn_in_copy = adamw(
        ffn_in_master, summed_ffn_in * grad_scale, ffn_in_first, ffn_in_second, 0.04
    )
    ffn_out_first_new, ffn_out_second_new, ffn_out_master_new, ffn_out_copy = adamw(
        ffn_out_master, summed_ffn_out * grad_scale, ffn_out_first, ffn_out_second, 0.02
    )
    vector_first_new, vector_second_new, vector_master_new, vector_copy = adamw(
        vector_master, summed_vector * grad_scale, vector_first, vector_second, 0.35
    )
    return (
        layer_out,
        tokens_grad,
        encoded_grad,
        qkv_first_new,
        qkv_second_new,
        qkv_master_new,
        qkv_copy,
        out_first_new,
        out_second_new,
        out_master_new,
        out_copy,
        ffn_in_first_new,
        ffn_in_second_new,
        ffn_in_master_new,
        ffn_in_copy,
        ffn_out_first_new,
        ffn_out_second_new,
        ffn_out_master_new,
        ffn_out_copy,
        vector_first_new,
        vector_second_new,
        vector_master_new,
        vector_copy,
    )


def solution(mesh):
    return jax.shard_map(
        body,
        mesh=mesh,
        in_specs=(
            P(("dp", "fsdp"), None),
            P(("dp", "fsdp"), None),
            P(("dp", "fsdp"), None),
            P(("dp", "fsdp"), None),
            P(("dp", "fsdp"), None),
            P(None, ("dp", "fsdp"), None),
            P(None, ("dp", "fsdp"), None),
            P(None, ("dp", "fsdp"), None),
            P(None, ("dp", "fsdp"), None),
            P(None, ("dp", "fsdp"), None),
            P(None, ("dp", "fsdp"), None),
            P(("dp", "fsdp"), None),
            P(("dp", "fsdp"), None),
            P(("dp", "fsdp"), None),
            P(("dp", "fsdp"), None),
            P(("dp", "fsdp"), None),
            P(("dp", "fsdp"), None),
            P(None, ("dp", "fsdp")),
            P(None, ("dp", "fsdp")),
            P(None, ("dp", "fsdp")),
        ),
        out_specs=(
            P(("dp", "fsdp"), None),
            P(("dp", "fsdp"), None),
            P(("dp", "fsdp"), None),
            P(None, ("dp", "fsdp"), None),
            P(None, ("dp", "fsdp"), None),
            P(None, ("dp", "fsdp"), None),
            P(None, ("dp", "fsdp"), None),
            P(None, ("dp", "fsdp"), None),
            P(None, ("dp", "fsdp"), None),
            P(None, ("dp", "fsdp"), None),
            P(None, ("dp", "fsdp"), None),
            P(("dp", "fsdp"), None),
            P(("dp", "fsdp"), None),
            P(("dp", "fsdp"), None),
            P(("dp", "fsdp"), None),
            P(("dp", "fsdp"), None),
            P(("dp", "fsdp"), None),
            P(("dp", "fsdp"), None),
            P(("dp", "fsdp"), None),
            P(None, ("dp", "fsdp")),
            P(None, ("dp", "fsdp")),
            P(None, ("dp", "fsdp")),
            P(None, ("dp", "fsdp")),
        ),
        check_vma=False,
    )
```

```python
import functools
import math

import jax
import jax.numpy as jnp
from jax import lax
from jax.experimental import pallas as pl
from jax.experimental.pallas import tpu as pltpu
from jax.sharding import PartitionSpec as P

HEADS = 8
STEP = 5
SEGMENTS = 10
norm_eps = 1e-05
beta_first = 0.5
beta_second = 0.5
adam_eps = 1e-08
weight_decay = 0.01
mask_fill = -1000000000.0
LOW = jnp.bfloat16
FULL = jnp.float32


def dot_nn(left, right):
    return lax.dot_general(left, right, (((1,), (0,)), ((), ())), preferred_element_type=FULL)


def dot_nt(left, right):
    return lax.dot_general(left, right, (((1,), (1,)), ((), ())), preferred_element_type=FULL)


def dot_tn(left, right):
    return lax.dot_general(left, right, (((0,), (0,)), ((), ())), preferred_element_type=FULL)


def head_masks(width, group, factor):
    lane = lax.broadcasted_iota(jnp.int32, (1, group * width), 1) // width
    return [jnp.where(lane == h, factor, 0.0).astype(LOW) for h in range(group)]


def window(start, size, total):
    return pl.multiple_of(jnp.minimum(start // 16 * 16, total - size), 16)


def inside(base, size, begin, end):
    place = lax.broadcasted_iota(jnp.int32, (size, 1), 0) + base
    return (place >= begin) & (place < end)


def each_span(row_starts, col_starts, total, same, work):
    def segment(s, carry):
        row_begin, row_end = row_starts[s], row_starts[s + 1]
        col_begin, col_end = col_starts[s], col_starts[s + 1]
        row_short = row_end - window(row_begin, 128, total) <= 128
        col_short = col_end - window(col_begin, 128, total) <= 128
        for row_span in (128, 256):
            for col_span in (128, 256):
                if same and row_span != col_span:
                    continue
                wanted = row_short if row_span == 128 else jnp.logical_not(row_short)
                if not same:
                    other = col_short if col_span == 128 else jnp.logical_not(col_short)
                    wanted = jnp.logical_and(wanted, other)

                @pl.when(wanted)
                def _(row_span=row_span, col_span=col_span):
                    row_base = window(row_begin, row_span, total)
                    col_base = window(col_begin, col_span, total)
                    work(
                        s,
                        pl.ds(row_base, row_span),
                        pl.ds(col_base, col_span),
                        inside(row_base, row_span, row_begin, row_end),
                        inside(col_base, col_span, col_begin, col_end),
                        row_span,
                    )

        return carry

    lax.fori_loop(0, SEGMENTS, segment, 0)


def attend_forward(row_starts, col_starts, q_ref, k_ref, v_ref, out_ref, sums_ref):
    total, model = q_ref.shape
    width = model // HEADS
    group = 256 // width
    scales = head_masks(width, group, 1.0 / math.sqrt(width))
    parts = [slice(g * 256, (g + 1) * 256) for g in range(HEADS // group)]

    def work(s, rows, cols, row_mask, col_mask, span):
        raw = []
        for lanes in parts:
            query, keys = q_ref[rows, lanes], k_ref[cols, lanes]
            stacked = jnp.concatenate([query * scale for scale in scales], axis=0)
            raw.append(dot_nt(keys, stacked))
        turned = [v_ref[cols, lanes].T for lanes in parts]
        probs = []
        for g, item in enumerate(raw):
            scores = jnp.where(col_mask, item, mask_fill)
            largest = jnp.max(scores, axis=0, keepdims=True)
            expo = jnp.exp(scores - largest)
            totals = jnp.sum(expo, axis=0, keepdims=True)
            sums_ref[pl.ds(len(parts) * s + g, 1), : group * span] = largest + jnp.log(totals)
            probs.append((expo * (1.0 / totals)).astype(LOW))
        mixed = [
            [
                dot_nn(side[h * width : (h + 1) * width], prob[:, h * span : (h + 1) * span])
                for h in range(group)
            ]
            for side, prob in zip(turned, probs)
        ]
        for lanes, items in zip(parts, mixed):
            value = jnp.concatenate(items, axis=0).T
            old = out_ref[rows, lanes].astype(FULL)
            out_ref[rows, lanes] = jnp.where(row_mask, value, old).astype(LOW)

    each_span(row_starts, col_starts, total, row_starts is col_starts, work)


def attend_backward(
    row_starts, col_starts, q_ref, k_ref, v_ref, grad_ref, sums_ref, dq_ref, dk_ref, dv_ref
):
    total, model = q_ref.shape
    width = model // HEADS
    group = 256 // width
    factor = 1.0 / math.sqrt(width)
    scales = head_masks(width, group, factor)
    picks = head_masks(width, group, 1.0)
    parts = [slice(g * 256, (g + 1) * 256) for g in range(HEADS // group)]

    def work(s, rows, cols, row_mask, col_mask, span):
        stacks, grads, raw, grad_probs = [], [], [], []
        for lanes in parts:
            query, keys, values = q_ref[rows, lanes], k_ref[cols, lanes], v_ref[cols, lanes]
            grad = jnp.where(row_mask, grad_ref[rows, lanes].astype(FULL), 0.0).astype(LOW)
            stacks.append(jnp.concatenate([query * scale for scale in scales], axis=0))
            grads.append(jnp.concatenate([grad * item for item in picks], axis=0))
            raw.append(dot_nt(keys, stacks[-1]))
            grad_probs.append(dot_nt(values, grads[-1]))
        grad_values, grad_scores = [], []
        for g, (item, grad_prob) in enumerate(zip(raw, grad_probs)):
            scores = jnp.where(col_mask, item, mask_fill)
            log_sums = sums_ref[pl.ds(len(parts) * s + g, 1), : group * span]
            probs = jnp.exp(scores - log_sums)
            grad_values.append(dot_nn(probs.astype(LOW), grads[g]))
            weighted = probs * grad_prob
            inner = jnp.sum(weighted, axis=0, keepdims=True)
            grad_scores.append((weighted - probs * inner).astype(LOW))
        grad_keys, grad_queries = [], []
        for lanes, item, stacked in zip(parts, grad_scores, stacks):
            grad_keys.append(dot_nn(item, stacked))
            turned = k_ref[cols, lanes].T
            grad_queries.append(
                [
                    dot_nn(turned[h * width : (h + 1) * width], item[:, h * span : (h + 1) * span])
                    for h in range(group)
                ]
            )
        for g, lanes in enumerate(parts):
            grad_query = jnp.concatenate(grad_queries[g], axis=0).T * factor
            for ref, place, mask, value in (
                (dq_ref, rows, row_mask, grad_query),
                (dk_ref, cols, col_mask, grad_keys[g]),
                (dv_ref, cols, col_mask, grad_values[g]),
            ):
                old = ref[place, lanes].astype(FULL)
                ref[place, lanes] = jnp.where(mask, value, old).astype(LOW)

    each_span(row_starts, col_starts, total, row_starts is col_starts, work)


def normalize(values):
    center = values - jnp.mean(values, axis=-1, keepdims=True)
    inverse = lax.rsqrt(jnp.mean(center * center, axis=-1, keepdims=True) + norm_eps)
    return center * inverse, inverse


def normalize_back(grad, gain, unit, inverse):
    scaled = grad * (1.0 + gain)
    mean = jnp.mean(scaled, axis=-1, keepdims=True)
    along = jnp.mean(scaled * unit, axis=-1, keepdims=True)
    return (scaled - mean - unit * along) * inverse


def column_sum(values):
    return jnp.sum(values.astype(FULL), axis=0, keepdims=True)


STEP_ROWS = 512


def row_steps(total, step, size=256):
    def run(i, carry):
        step(pl.ds(pl.multiple_of(i * size, size), size))
        return carry

    lax.fori_loop(0, total // size, run, 0)


def load_weights(place, depth, sources, targets, semaphores):
    if len(sources) == 1:
        offset = 0
        for target, semaphore in zip(targets, semaphores):
            source = sources[0].at[:, offset : offset + target.shape[1]]
            offset += target.shape[1]
            pltpu.make_async_copy(source, target, semaphore).start()
        return
    half = len(sources) // 2
    for k, source in enumerate(sources):
        base = (k % half) * 2 * depth + k // half
        for layer in range(depth):
            other = place ^ (base + 2 * layer)
            offset = 0
            for target, semaphore in zip(targets, semaphores):
                rows = source.shape[1]
                span = target.shape[1]
                to_rows = pl.ds(pl.multiple_of(other * rows, rows), rows)
                pltpu.make_async_copy(
                    source.at[layer, :, offset : offset + span], target.at[to_rows, :], semaphore
                ).start()
                offset += span


def await_weights(target, semaphore):
    pltpu.make_async_copy(target, target, semaphore).wait()


def store_grad(refs, core, lanes, value):
    value = value.astype(LOW)
    if len(refs) == 1:
        refs[0][:, lanes] = value
        return
    sent, kept = refs
    chips, rows = kept.shape[0], kept.shape[1]
    parts = value.reshape(chips, 2, rows, value.shape[1])
    first = core == 0
    kept[:, :, lanes] = jnp.where(first, parts[:, 0], parts[:, 1])
    sent[:, :, lanes] = jnp.where(first, parts[:, 1], parts[:, 0])


def self_forward_kernel(count, depth, place, row_starts, tokens, *rest):
    sources = rest[:count]
    weights, vectors, queries, keys, values, mixed, sums, semaphores = rest[count:]
    model = tokens.shape[1]
    load_weights(place[0], depth, sources, [weights], [semaphores.at[0]])
    await_weights(weights, semaphores.at[0])
    turned = weights[:, 3 * model : 3 * model + 128].astype(FULL).T
    vectors[...] = turned[: vectors.shape[0]]

    def project(rows):
        block = tokens[rows, :]
        queries[rows, :] = (dot_nn(block, weights[:, :model]) + vectors[0:1, :]).astype(LOW)
        keys[rows, :] = dot_nn(block, weights[:, model : 2 * model]).astype(LOW)
        values[rows, :] = (
            dot_nn(block, weights[:, 2 * model : 3 * model]) + vectors[1:2, :]
        ).astype(LOW)

    row_steps(tokens.shape[0], project, 512)
    attend_forward(row_starts, row_starts, queries, keys, values, mixed, sums)


def cross_project_kernel(count, depth, place, tokens, encoded, mixed, vectors, *rest):
    sources = rest[:count]
    weights, unit_one, inverse_one, queries, keys, values, semaphores = rest[count:]
    model = tokens.shape[1]
    load_weights(place[0], depth, sources, [weights], [semaphores.at[0]])
    await_weights(weights, semaphores.at[0])

    def project(rows):
        block = encoded[rows, :]
        keys[rows, :] = dot_nn(block, weights[:, 2 * model : 3 * model]).astype(LOW)
        values[rows, :] = (
            dot_nn(block, weights[:, 3 * model : 4 * model]) + vectors[4:5, :]
        ).astype(LOW)
        summed = tokens[rows, :].astype(FULL) + dot_nn(mixed[rows, :], weights[:, :model])
        unit, inverse = normalize(summed + vectors[2:3, :])
        unit_one[rows, :] = unit
        inverse_one[rows, :] = inverse
        low = (unit * (1.0 + vectors[7:8, :]) + vectors[10:11, :]).astype(LOW)
        queries[rows, :] = (dot_nn(low, weights[:, model : 2 * model]) + vectors[3:4, :]).astype(LOW)

    row_steps(tokens.shape[0], project, 512)


def cross_attend_kernel(row_starts, col_starts, queries, keys, values, cross_mixed, sums):
    attend_forward(row_starts, col_starts, queries, keys, values, cross_mixed, sums)


def cross_finish_kernel(unit_one, cross_mixed, weights, vectors, unit_two, inverse_two):
    model = cross_mixed.shape[1]

    def finish(rows):
        first = unit_one[rows, :] * (1.0 + vectors[7:8, :]) + vectors[10:11, :]
        summed = first + dot_nn(cross_mixed[rows, :], weights[:, 4 * model : 5 * model])
        unit, inverse = normalize(summed + vectors[5:6, :])
        unit_two[rows, :] = unit
        inverse_two[rows, :] = inverse

    row_steps(unit_one.shape[0], finish, 512)


gelu_scale = math.sqrt(2.0 / math.pi)
gelu_cubic = 0.044715


def ffn_kernel(count, depth, blocks, place, unit_two, inverse_two, cotangent, vectors, *rest):
    sources = rest[:count]
    (
        layer_out, grad_sum, grad_out, sums, bias_sums, *grads,
        first_weights, second_weights, hidden, grad_ffn, grad_pre, slopes, semaphores,
    ) = rest[count:]
    model = unit_two.shape[1]
    pieces = blocks
    load_ffn(place[0], depth, sources, first_weights, second_weights, semaphores)
    sums[...] = jnp.zeros_like(sums)
    bias_sums[...] = jnp.zeros_like(bias_sums)
    await_weights(first_weights, semaphores.at[0])
    await_weights(second_weights, semaphores.at[1])

    def step(rows):
        unit = unit_two[rows, :]
        second = unit * (1.0 + vectors[8:9, :]) + vectors[11:12, :]
        low = second.astype(LOW)
        total = second + vectors[6:7, :]
        for j in range(pieces):
            lanes = slice(j * model, (j + 1) * model)
            pre = dot_nn(low, first_block(first_weights, j, model)) + vectors[13 + j : 14 + j, :]
            square = pre * pre
            bend = jnp.tanh(gelu_scale * pre * (1.0 + gelu_cubic * square))
            half = 0.5 * (1.0 + bend)
            value = (pre * half).astype(LOW)
            hidden[rows, lanes] = value
            inner = gelu_scale * (1.0 + 3.0 * gelu_cubic * square)
            slopes[:, lanes] = half + 0.5 * pre * (1.0 - bend * bend) * inner
            total = total + dot_nn(value, second_block(second_weights, j, model))
        unit_three, inverse_three = normalize(total)
        layer_out[rows, :] = (unit_three * (1.0 + vectors[9:10, :]) + vectors[12:13, :]).astype(LOW)
        upper = cotangent[rows, :].astype(FULL)
        third = normalize_back(upper, vectors[9:10, :], unit_three, inverse_three)
        third_low = third.astype(LOW)
        grad_ffn[rows, :] = third_low
        sums[0:1, :] += column_sum(third_low)
        sums[1:2, :] += column_sum(upper * unit_three)
        sums[2:3, :] += column_sum(upper)
        below = third
        for j in range(pieces):
            lanes = slice(j * model, (j + 1) * model)
            pre = (dot_nt(third_low, second_block(second_weights, j, model)) * slopes[:, lanes]).astype(LOW)
            grad_pre[rows, lanes] = pre
            bias_sums[j : j + 1, :] += column_sum(pre)
            below = below + dot_nt(pre, first_block(first_weights, j, model))
        sums[3:4, :] += column_sum(below * unit)
        sums[4:5, :] += column_sum(below)
        second_sum = normalize_back(below, vectors[8:9, :], unit, inverse_two[rows, :])
        grad_sum[rows, :] = second_sum
        out_low = second_sum.astype(LOW)
        grad_out[rows, :] = out_low
        sums[5:6, :] += column_sum(out_low)

    row_steps(unit_two.shape[0], step, STEP_ROWS)
    core = place[0] % 2
    second_low = (unit_two[...] * (1.0 + vectors[8:9, :]) + vectors[11:12, :]).astype(LOW)

    def block_grads(j, carry):
        lanes = pl.ds(pl.multiple_of(j * model, model), model)
        store_grad(grads, core, lanes, dot_tn(second_low, grad_pre[:, lanes]))
        store_ffn_out(grads, core, j, pieces, dot_tn(hidden[:, lanes], grad_ffn[...]))
        return carry

    lax.fori_loop(0, pieces, block_grads, 0)


def load_ffn(place, depth, sources, first_weights, second_weights, semaphores):
    if len(sources) == 1:
        first_width = first_weights.shape[1]
        pltpu.make_async_copy(
            sources[0].at[:, :first_width], first_weights, semaphores.at[0]
        ).start()
        pieces = first_width // first_weights.shape[0]
        model = first_weights.shape[0]
        for j in range(pieces):
            pltpu.make_async_copy(
                sources[0].at[:, first_width + j * model : first_width + (j + 1) * model],
                second_weights.at[pl.ds(j * model, model), :],
                semaphores.at[1],
            ).start()
        return
    half = len(sources) // 2
    for k, source in enumerate(sources):
        base = (k % half) * 2 * depth + k // half
        pieces, rows = source.shape[1] // 2, source.shape[2]
        for layer in range(depth):
            other = place ^ (base + 2 * layer)
            to_rows = pl.ds(pl.multiple_of(other * rows, rows), rows)
            pltpu.make_async_copy(
                source.at[layer, :pieces], first_weights.at[:, to_rows, :], semaphores.at[0]
            ).start()
            pltpu.make_async_copy(
                source.at[layer, pieces:],
                second_weights.at[pl.ds(other * pieces, pieces)],
                semaphores.at[1],
            ).start()


def first_block(ref, j, model):
    return ref[j] if len(ref.shape) == 3 else ref[:, j * model : (j + 1) * model]


def second_block(ref, j, model):
    if len(ref.shape) == 2:
        return ref[j * model : (j + 1) * model, :]
    count = model // ref.shape[1]
    return ref[j * count : (j + 1) * count].reshape(model, model)


def store_ffn_out(refs, core, block, pieces, value):
    value = value.astype(LOW)
    model = value.shape[1]
    if len(refs) == 1:
        offset = pl.multiple_of((pieces + block) * model, model)
        refs[0][:, pl.ds(offset, model)] = value
        return
    sent, kept = refs
    rows = kept.shape[1]
    chips = kept.shape[0] // pieces
    parts = value.reshape(chips, 2, pieces, rows, model)
    first = core == 0
    place = pl.ds(block * chips, chips)
    for j in range(pieces):
        lanes = slice((pieces + j) * model, (pieces + j + 1) * model)
        kept[place, :, lanes] = jnp.where(first, parts[:, 0, j], parts[:, 1, j])
        sent[place, :, lanes] = jnp.where(first, parts[:, 1, j], parts[:, 0, j])


def cross_backward_kernel(
    row_starts, col_starts, queries, keys, values, grad_out, weights, sums_in, dq, dk, dv, grad_mixed
):
    model = queries.shape[1]

    def project(rows):
        low = dot_nt(grad_out[rows, :], weights[:, 4 * model : 5 * model]).astype(LOW)
        grad_mixed[rows, :] = low

    row_steps(queries.shape[0], project)
    attend_backward(row_starts, col_starts, queries, keys, values, grad_mixed, sums_in, dq, dk, dv)


def cross_grads_kernel(
    place, dq, dk, dv, weights, vectors, grad_sum, unit_one, inverse_one,
    encoded, cross_mixed, grad_out,
    first_sum, self_low, grad_mixed, sums, encoded_grad, *grads,
):
    model = dq.shape[1]
    sums[...] = jnp.zeros_like(sums)

    def finish(rows):
        query, key, value = dq[rows, :], dk[rows, :], dv[rows, :]
        sums[0:1, :] += column_sum(query)
        sums[1:2, :] += column_sum(value)
        encoded_grad[rows, :] = dot_nt(key, weights[:, 2 * model : 3 * model]) + dot_nt(
            value, weights[:, 3 * model : 4 * model]
        )
        upper = grad_sum[rows, :] + dot_nt(query, weights[:, model : 2 * model])
        unit = unit_one[rows, :]
        sums[2:3, :] += column_sum(upper * unit)
        sums[3:4, :] += column_sum(upper)
        below = normalize_back(upper, vectors[7:8, :], unit, inverse_one[rows, :])
        first_sum[rows, :] = below
        low = below.astype(LOW)
        self_low[rows, :] = low
        sums[4:5, :] += column_sum(low)
        grad_mixed[rows, :] = dot_nt(low, weights[:, :model]).astype(LOW)

    row_steps(dq.shape[0], finish, 512)
    core = place[0] % 2
    first_low = (unit_one[...] * (1.0 + vectors[7:8, :]) + vectors[10:11, :]).astype(LOW)
    pairs = ((first_low, dq), (encoded, dk), (encoded, dv), (cross_mixed, grad_out))
    for j, (left, right) in enumerate(pairs):
        lanes = slice(j * model, (j + 1) * model)
        store_grad(grads, core, lanes, dot_tn(left[...], right[...]))


def self_backward_kernel(
    place, row_starts, queries, keys, values, grad_mixed, sums_in, tokens, mixed, self_low,
    cross_sums, ffn_sums, bias_sums, dq, dk, dv, *rest,
):
    *grads, stack = rest
    attend_backward(row_starts, row_starts, queries, keys, values, grad_mixed, sums_in, dq, dk, dv)
    model = dq.shape[1]
    core = place[0] % 2
    pairs = ((tokens, dq), (tokens, dk), (tokens, dv), (mixed, self_low))
    for j, (left, right) in enumerate(pairs):
        lanes = slice(j * model, (j + 1) * model)
        store_grad(grads, core, lanes, dot_tn(left[...], right[...]))
    stack[...] = jnp.zeros_like(stack)
    stack[0:1, :] = column_sum(dq[...])
    stack[1:2, :] = column_sum(dv[...])
    order = (
        (2, cross_sums, 4), (3, cross_sums, 0), (4, cross_sums, 1), (5, ffn_sums, 5),
        (6, ffn_sums, 0), (7, cross_sums, 2), (8, ffn_sums, 3), (9, ffn_sums, 1),
        (10, cross_sums, 3), (11, ffn_sums, 4), (12, ffn_sums, 2),
    )
    for to, ref, at in order:
        stack[to : to + 1, :] = ref[at : at + 1, :]
    extra = bias_sums.shape[0]
    stack[13 : 13 + extra, :] = bias_sums[...]
    start = len(pairs) * model
    store_grad(grads, core, slice(start, start + 128), stack[...].T)


def tokens_grad_kernel(dq, dk, dv, first_sum, weights, tokens_grad):
    model = dq.shape[1]

    def finish(rows):
        below = first_sum[rows, :] + dot_nt(dq[rows, :], weights[:, :model])
        below = below + dot_nt(dk[rows, :], weights[:, model : 2 * model])
        tokens_grad[rows, :] = below + dot_nt(dv[rows, :], weights[:, 2 * model : 3 * model])

    row_steps(dq.shape[0], finish, 512)


def fold_core_kernel(shape, place, kept, received, own, *sends):
    dp_count, depth = shape
    at = place[0] // (2 * depth)
    for k, ref in enumerate((own, *sends)):
        spot = pl.ds((at ^ k) * depth, depth)
        value = kept[spot].astype(FULL) + received[spot].astype(FULL)
        ref[...] = value.astype(ref.dtype)


def fold_square_kernel(shape, place, kept, *rest):
    dp_count, depth = shape
    received, outs = rest[: dp_count - 1], rest[dp_count - 1 :]
    at = place[0] // 2 % depth
    for k, ref in enumerate(outs):
        spot = pl.ds(at ^ k, 1)
        value = kept[spot]
        for item in received:
            value = value + item[spot].astype(FULL)
        ref[...] = value[0].astype(ref.dtype)


def fold_halves_kernel(depth, place, kept, received, keep_first, send_first, keep_second, send_second):
    at = place[0] // (2 * depth)
    half = kept.shape[2] // 2
    low, high = slice(0, half), slice(half, 2 * half)
    for ref, lanes, offsets in (
        (keep_first, low, (0, 1)),
        (send_first, low, (2, 3)),
        (keep_second, high, (0, 2)),
        (send_second, high, (1, 3)),
    ):
        for slot, k in enumerate(offsets):
            spot = pl.ds((at ^ k) * depth, depth)
            value = kept[spot, :, lanes].astype(FULL) + received[spot, :, lanes].astype(FULL)
            ref[slot] = value.astype(ref.dtype)


def fold_pairs_kernel(keep_first, got_first, keep_second, got_second, *outs):
    own_first, send_first, own_second, send_second = outs
    own_first[...] = keep_first[0] + got_first[0].astype(FULL)
    send_first[...] = (keep_first[1] + got_first[1].astype(FULL)).astype(LOW)
    own_second[...] = keep_second[0] + got_second[0].astype(FULL)
    send_second[...] = (keep_second[1] + got_second[1].astype(FULL)).astype(LOW)


def fold_layers_kernel(depth, place, first, got_first, second, got_second, cross, *rest):
    *got_cross, keep, send = rest
    at = place[0] // 2 % depth
    half = first.shape[2]
    for ref, offsets in ((keep, (0, 1)), (send, (2, 3))):
        for slot, k in enumerate(offsets):
            spot = pl.ds(at ^ k, 1)
            value = first[spot] + got_first[spot].astype(FULL)
            ref[slot, :, :half] = value[0].astype(ref.dtype)
            value = second[spot] + got_second[spot].astype(FULL)
            ref[slot, :, half : 2 * half] = value[0].astype(ref.dtype)
            value = cross[spot]
            for item in got_cross:
                value = value + item[spot].astype(FULL)
            ref[slot, :, 2 * half :] = value[0].astype(ref.dtype)


def fold_last_kernel(keep, got, own, send):
    own[...] = keep[0] + got[0].astype(FULL)
    send[...] = (keep[1] + got[1].astype(FULL)).astype(LOW)


def update_into(outs, index, state, grad, rate):
    for ref, value in zip(outs, adamw(state[0][index], grad, state[1][index], state[2][index], rate)):
        ref[index] = value


def ffn_update_kernel(grad_scale, own, got, *rest):
    first_state, second_state, outs = rest[:3], rest[3:6], rest[6:]
    rows, width = first_state[0].shape
    model = second_state[0].shape[1]
    grad = (own[:, :width] + got[:, :width].astype(FULL)) * grad_scale
    update_into(outs[:4], (slice(None), slice(None)), first_state, grad, 0.04)
    for j in range(second_state[0].shape[0] // rows):
        lanes = slice(width + j * model, width + (j + 1) * model)
        grad = (own[:, lanes] + got[:, lanes].astype(FULL)) * grad_scale
        index = (slice(j * rows, (j + 1) * rows), slice(None))
        update_into(outs[4:], index, second_state, grad, 0.02)


def final_update_kernel(grad_scale, start, own, got, kept, *rest):
    moved, states, outs = rest[:-21], rest[-21:-12], rest[-12:]
    qkv_state, out_state, vector_state = states[:3], states[3:6], states[6:]
    model = qkv_state[0].shape[2]

    def self_grad(lanes):
        value = kept[:, lanes]
        for item in moved:
            value = value + item[:, lanes].astype(FULL)
        return value * grad_scale

    def cross_grad(index):
        lanes = slice(start + index * model, start + (index + 1) * model)
        return (own[:, lanes] + got[:, lanes].astype(FULL)) * grad_scale

    for j in range(4):
        grad = self_grad(slice(j * model, (j + 1) * model))
        if j < 3:
            update_into(outs[:4], j, qkv_state, grad, 0.04)
            update_into(outs[:4], 3 + j, qkv_state, cross_grad(j), 0.04)
        else:
            update_into(outs[4:8], 0, out_state, grad, 0.3)
            update_into(outs[4:8], 1, out_state, cross_grad(j), 0.3)
    grad = self_grad(slice(4 * model, 4 * model + vector_state[0].shape[1]))
    update_into(outs[8:], (slice(None), slice(None)), vector_state, grad, 0.35)


LIMITS = {
    "fold_halves": 16,
    "fold_pairs": 14,
    "fold_layers": 12,
    "fold_last": 8,
    "ffn_update": 8,
    "final_update": 10,
    "fold_core": 12,
    "fold_square": 10,
    "self_forward": 14,
    "cross_project": 14,
    "cross_attend": 10,
    "cross_finish": 9,
    "ffn": 32.8,
    "cross_backward": 13,
    "cross_grads": 20,
    "self_backward": 16,
    "tokens_grad": 11,
}


def out_kind(item):
    if len(item) == 3:
        return pltpu.VMEM(item[0], item[1])
    return jax.ShapeDtypeStruct(*item)


def keep(item):
    return (item[0], item[1], True)


def limit(name):
    return pltpu.CompilerParams(vmem_limit_bytes=int(LIMITS[name] * (1 << 20)))


def pinned(sources):
    if len(sources) == 1:
        return sources
    return [pltpu.with_memory_space_constraint(item, pltpu.VMEM) for item in sources]


def source_spec(sources):
    return pl.BlockSpec(memory_space=pltpu.VMEM if len(sources) > 1 else pl.ANY)


def call(kernel, name, scalars, arrays, outs, flops, sources=(), scratch=()):
    specs = [pl.BlockSpec(memory_space=pltpu.SMEM)] * len(scalars)
    specs += [pl.BlockSpec(memory_space=pltpu.VMEM)] * len(arrays)
    specs += [source_spec(sources)] * len(sources)
    shapes = [out_kind(item) for item in outs]
    moved = sum(item.size * item.dtype.itemsize for item in [*arrays, *sources])
    return pl.pallas_call(
        kernel,
        out_shape=shapes,
        in_specs=specs,
        out_specs=[pl.BlockSpec(memory_space=pltpu.VMEM)] * len(outs),
        scratch_shapes=list(scratch),
        compiler_params=limit(name),
        cost_estimate=pl.CostEstimate(flops=flops, transcendentals=0, bytes_accessed=moved),
        name=name,
    )(*scalars, *arrays, *pinned(sources))


def segment_starts(ids):
    marks = jnp.arange(SEGMENTS + 1, dtype=ids.dtype)
    return jnp.sum((ids[None, :] < marks[:, None]).astype(jnp.int32), axis=1)


def adamw(master, grad, first, second, rate):
    first_new = beta_first * first + (1.0 - beta_first) * grad
    second_new = beta_second * second + (1.0 - beta_second) * grad * grad
    first_hat = first_new / (1.0 - beta_first**STEP)
    second_hat = second_new / (1.0 - beta_second**STEP)
    master_new = master - rate * (
        first_hat / (jnp.sqrt(second_hat) + adam_eps) + weight_decay * master
    )
    return (first_new, second_new, master_new, master_new.astype(jnp.bfloat16))


AXES = ("dp", "fsdp")


def exchange(values, offset):
    count = lax.axis_size("dp") * lax.axis_size("fsdp")
    return lax.ppermute(values, AXES, [(i, i ^ offset) for i in range(count)])


def after(value, *others):
    return lax.optimization_barrier((value, *others))[0]


def layer_stack(piece):
    depth = lax.axis_size("fsdp") // 2
    return jnp.stack([piece] + [exchange(piece, 2 * k) for k in range(1, depth)])


def layer_double(piece, gate=None):
    stack, step = piece[None], 1
    while step < lax.axis_size("fsdp") // 2:
        if gate is not None and step > 1:
            stack = after(stack, gate)
        stack = jnp.concatenate([stack, exchange(stack, 2 * step)])
        step *= 2
    return stack


def square_list(stack):
    dp_count, fsdp_count = lax.axis_size("dp"), lax.axis_size("fsdp")
    return [stack] + [exchange(stack, fsdp_count * k) for k in range(1, dp_count)]


def forward_list(stack):
    stride, near = lax.axis_size("fsdp"), [stack]
    for k in range(1, lax.axis_size("dp")):
        near.append(None if k & (k - 1) else exchange(stack, stride * k))
    return near


def forward_rest(near, gate):
    stride = lax.axis_size("fsdp")
    for k, item in enumerate(near):
        if item is None:
            high = 1 << (k.bit_length() - 1)
            near[k] = exchange(after(near[k - high], gate), stride * high)
    return near


def core_list(near):
    return near + [exchange(item, 1) for item in near]


def ordered(parts, place):
    half = len(parts) // 2
    both = jnp.stack([jnp.stack(parts[:half]), jnp.stack(parts[half:])], axis=2)
    flat = both.reshape((-1,) + both.shape[3:])
    return flat[jnp.arange(flat.shape[0]) ^ place]


def pick(values, index, axis):
    return lax.dynamic_index_in_dim(values, index, axis, keepdims=False)


def split_core(grads):
    if len(grads) == 2:
        return grads
    count = lax.axis_size("dp") * lax.axis_size("fsdp")
    core = lax.axis_index("fsdp") % 2
    parts = grads[0].reshape((count // 2, 2, -1) + grads[0].shape[1:])
    return pick(parts, 1 - core, 1), pick(parts, core, 1)


def fold_core(spot, kept, received):
    dp_count, depth = lax.axis_size("dp"), lax.axis_size("fsdp") // 2
    shape = (depth,) + kept.shape[1:]
    if kept.shape[1] % 16:
        place = lax.axis_index("dp")
        pair = (kept.astype(FULL) + received.astype(FULL)).reshape((dp_count,) + shape)
        sends = [pick(pair, place ^ k, 0).astype(LOW) for k in range(1, dp_count)]
        return pick(pair, place, 0), sends
    own, *sends = call(
        functools.partial(fold_core_kernel, (dp_count, depth)), "fold_core", [spot],
        [kept, received], [(shape, FULL)] + [(shape, LOW)] * (dp_count - 1), kept.size,
    )
    return own, sends


def fold_square(spot, kept, received):
    dp_count, depth = lax.axis_size("dp"), lax.axis_size("fsdp") // 2
    shape = kept.shape[1:]
    if kept.shape[1] % 16:
        place = lax.axis_index("fsdp") // 2
        square = add_all(kept, received)
        sends = [pick(square, place ^ k, 0).astype(LOW) for k in range(1, depth)]
        return pick(square, place, 0), sends
    own, *sends = call(
        functools.partial(fold_square_kernel, (dp_count, depth)), "fold_square", [spot],
        [kept, *received], [(shape, FULL)] + [(shape, LOW)] * (depth - 1), kept.size,
    )
    return own, sends


def move_square(sends):
    stride = lax.axis_size("fsdp")
    return [exchange(item, stride * (k + 1)) for k, item in enumerate(sends)]


def move_layers(sends):
    return [exchange(item, 2 * (k + 1)) for k, item in enumerate(sends)]


def add_all(kept, moved):
    for item in moved:
        kept = kept + item.astype(FULL)
    return kept


def body(
    tokens,
    encoded,
    cotangent,
    target_ids,
    source_ids,
    qkv_master,
    qkv_first,
    qkv_second,
    out_master,
    out_first,
    out_second,
    ffn_in_master,
    ffn_in_first,
    ffn_in_second,
    ffn_out_master,
    ffn_out_first,
    ffn_out_second,
    vector_master,
    vector_first,
    vector_second,
):
    total, model = tokens.shape
    dp_count, fsdp_count = lax.axis_size("dp"), lax.axis_size("fsdp")
    count, depth = dp_count * fsdp_count, fsdp_count // 2
    rows = model // count
    aligned = rows % 16 == 0
    place = lax.axis_index("dp") * fsdp_count + lax.axis_index("fsdp")
    spot = place.reshape(1).astype(jnp.int32)
    low_qkv = after(qkv_master, spot).astype(LOW)
    low_out = out_master.astype(LOW)
    low_vector = jnp.pad(vector_master.astype(LOW).T, ((0, 0), (0, 128 - vector_master.shape[0])))
    pieces = ffn_in_master.shape[1] // model

    def to_columns(values):
        return values.reshape(-1, rows, model).transpose(1, 0, 2).reshape(rows, -1)

    self_piece = jnp.concatenate([low_qkv[0], low_qkv[1], low_qkv[2], low_vector], axis=1)
    cross_piece = jnp.concatenate([low_out[0], low_qkv[3], low_qkv[4], low_qkv[5], low_out[1]], axis=1)
    ffn_piece = jnp.concatenate(
        [ffn_in_master.astype(LOW), to_columns(ffn_out_master.astype(LOW))], axis=1
    )
    if aligned:
        ffn_piece = jnp.concatenate(
            [
                ffn_in_master.astype(LOW).reshape(rows, pieces, model).transpose(1, 0, 2),
                ffn_out_master.astype(LOW).reshape(pieces, rows, model),
            ]
        )
    row_starts, col_starts = segment_starts(target_ids[0]), segment_starts(source_ids[0])

    def sources_of(parts):
        if aligned:
            return parts
        flat = ordered(parts, place)
        return [flat.reshape(model, -1)]

    def ffn_sources_of(parts):
        if aligned:
            return parts
        flat = ordered(parts, place)
        width = pieces * model
        second = flat[:, :, width:].reshape(count, rows, pieces, model).transpose(0, 2, 1, 3)
        second = second.reshape(pieces, model, model).transpose(1, 0, 2).reshape(model, -1)
        return [jnp.concatenate([flat[:, :, :width].reshape(model, -1), second], axis=1)]

    wide, tall, thin = ((total, model), LOW), ((total, model), FULL), ((total, 1), FULL)
    log_sums = ((SEGMENTS * (model // 256), 1024), FULL)
    small = ((8, model), FULL)
    unit = 2 * total * model * model
    attend = 2 * SEGMENTS * HEADS * 256 * 256 * 256
    wait_one, wait_two = pltpu.SemaphoreType.DMA((1,)), pltpu.SemaphoreType.DMA((2,))

    def grad_outs(columns):
        if aligned:
            return [((count // 2, rows, columns), LOW)] * 2
        return [((model, columns), LOW)]

    self_stack = layer_stack(self_piece)
    self_near = square_list(self_stack)
    cross_own = layer_double(after(cross_piece, self_stack))
    ffn_own = layer_double(after(ffn_piece, self_stack), cross_own)
    self_parts = core_list(self_near)
    cross_columns = cross_piece.shape[1]
    cross_near = square_list(cross_own)
    ffn_near = forward_list(ffn_own)

    sources = sources_of(self_parts)
    (
        self_weights, vectors, queries, keys, values, mixed, self_sums,
    ) = call(
        functools.partial(self_forward_kernel, len(sources), depth), "self_forward",
        [spot, row_starts], [after(tokens, cross_own)],
        [
            keep(((model, self_piece.shape[1]), LOW)), ((24, model), FULL),
            keep(wide), keep(wide), keep(wide), keep(wide), keep(log_sums),
        ],
        3 * unit + 2 * attend, sources, [wait_one],
    )
    sources = sources_of(core_list([after(item, mixed) for item in cross_near]))
    cross_weights, unit_one, inverse_one, cross_queries, cross_keys, cross_values = call(
        functools.partial(cross_project_kernel, len(sources), depth), "cross_project", [spot],
        [tokens, encoded, mixed, vectors],
        [
            keep(((model, cross_columns), LOW)), keep(tall), thin, keep(wide), keep(wide),
            keep(wide),
        ],
        4 * unit, sources, [wait_one],
    )
    ffn_near = forward_rest(ffn_near, cross_queries)
    cross_mixed, cross_log = call(
        cross_attend_kernel, "cross_attend", [row_starts, col_starts],
        [cross_queries, cross_keys, cross_values], [keep(wide), keep(log_sums)], 2 * attend,
    )
    unit_two, inverse_two = call(
        cross_finish_kernel, "cross_finish", [], [unit_one, cross_mixed, cross_weights, vectors],
        [keep(tall), thin], unit,
    )
    gates = [mixed] * (dp_count // 2) + [cross_mixed] * (dp_count // 2)
    sources = ffn_sources_of(core_list([after(*pair) for pair in zip(ffn_near, gates)]))
    hidden = pieces * model
    if aligned:
        ffn_scratch = [
            pltpu.VMEM((pieces, model, model), LOW), pltpu.VMEM((count * pieces, rows, model), LOW),
        ]
    else:
        ffn_scratch = [pltpu.VMEM((model, hidden), LOW), pltpu.VMEM((hidden, model), LOW)]
    (
        layer_out, grad_sum, grad_cross_out, ffn_sums, bias_sums, *ffn_grads
    ) = call(
        functools.partial(ffn_kernel, len(sources), depth, pieces), "ffn", [spot],
        [unit_two, inverse_two, cotangent, vectors],
        [wide, keep(tall), keep(wide), small, small, *grad_outs(2 * hidden)],
        (5 * pieces + 1) * unit, sources,
        [
            *ffn_scratch,
            pltpu.VMEM((total, hidden), LOW), pltpu.VMEM((total, model), LOW),
            pltpu.VMEM((total, hidden), LOW),
            pltpu.VMEM((STEP_ROWS, hidden), FULL), wait_two,
        ],
    )
    if not aligned:
        first, second = ffn_grads[0][:, :hidden], ffn_grads[0][:, hidden:]
        second = second.reshape(model, pieces, model).transpose(1, 0, 2)
        second = second.reshape(count, pieces, rows, model).transpose(0, 2, 1, 3)
        ffn_grads = [jnp.concatenate([first, second.reshape(model, -1)], axis=1)]
    sent, kept = split_core(ffn_grads)
    ffn_moved = exchange(sent, 1)
    cross_dq, cross_dk, cross_dv = call(
        cross_backward_kernel, "cross_backward", [row_starts, col_starts],
        [
            cross_queries, cross_keys, cross_values, after(grad_cross_out, sent), cross_weights,
            cross_log,
        ],
        [keep(wide), keep(wide), keep(wide)], 5 * attend, (), [pltpu.VMEM((total, model), LOW)],
    )
    fast = aligned and dp_count == 4 and depth == 4
    ffn_moved = after(ffn_moved, cross_dq)
    if fast:
        pair = (2, depth, rows, hidden)
        keep_first, send_first, keep_second, send_second = call(
            functools.partial(fold_halves_kernel, depth), "fold_halves", [spot], [kept, ffn_moved],
            [(pair, FULL), (pair, LOW), (pair, FULL), (pair, LOW)], 1,
        )
        ffn_sends = [send_first, send_second]
        got_first = exchange(send_first, 2 * fsdp_count)
        got_second = exchange(send_second, fsdp_count)
    else:
        ffn_kept, ffn_sends = fold_core(spot, kept, ffn_moved)
        ffn_moved = move_square(ffn_sends)
    first_sum, self_low, grad_mixed, cross_vector, encoded_grad, *cross_grads = call(
        cross_grads_kernel, "cross_grads", [spot],
        [
            after(cross_dq, *ffn_sends), cross_dk, cross_dv, cross_weights, vectors, grad_sum,
            unit_one, inverse_one, encoded, cross_mixed, grad_cross_out,
        ],
        [keep(tall), keep(wide), keep(wide), small, tall, *grad_outs(4 * model)], 8 * unit,
    )
    sent, kept = split_core(cross_grads)
    ffn_sends = [sent]
    if fast:
        half = (depth, rows, hidden)
        own_first, send_first, own_second, send_second = call(
            fold_pairs_kernel, "fold_pairs", [],
            [keep_first, after(got_first, sent), keep_second, got_second],
            [(half, FULL), (half, LOW), (half, FULL), (half, LOW)], 1,
        )
        ffn_sends = [send_first, send_second]
        got_first = exchange(send_first, fsdp_count)
        got_second = exchange(send_second, 2 * fsdp_count)
    cross_moved = exchange(after(sent, *ffn_sends), 1)
    cross_kept, cross_sends = fold_core(spot, kept, cross_moved)
    cross_moved = move_square(cross_sends)
    self_dq, self_dk, self_dv, *self_grads = call(
        self_backward_kernel, "self_backward", [spot, row_starts],
        [
            queries, keys, values, after(grad_mixed, *cross_sends, *ffn_sends), self_sums,
            tokens, mixed, self_low, cross_vector, ffn_sums, bias_sums,
        ],
        [keep(wide), keep(wide), keep(wide), *grad_outs(4 * model + 128)],
        5 * attend + 4 * unit, (), [pltpu.VMEM((128, model), FULL)],
    )
    sent, kept = split_core(self_grads)
    if fast:
        wide_pair = (2, rows, 2 * hidden + 4 * model)
        layer_keep, layer_send = call(
            functools.partial(fold_layers_kernel, depth), "fold_layers", [spot],
            [own_first, after(got_first, sent), own_second, got_second, cross_kept, *cross_moved],
            [(wide_pair, FULL), (wide_pair, LOW)], 1,
        )
        ffn_sends = [layer_send]
        layer_got = exchange(layer_send, 4)
        self_moved = exchange(after(sent, layer_send), 1)
    else:
        self_moved = exchange(sent, 1)
        ffn_kept, ffn_sends = fold_square(spot, ffn_kept, [after(item, sent) for item in ffn_moved])
        ffn_moved = move_layers(ffn_sends)
    (tokens_grad,) = call(
        tokens_grad_kernel, "tokens_grad", [],
        [after(self_dq, *ffn_sends), self_dk, self_dv, first_sum, self_weights], [tall], 3 * unit,
    )
    self_kept, self_sends = fold_core(spot, kept, after(self_moved, tokens_grad))
    self_moved = move_square(self_sends)
    grad_scale = 1.0 / math.sqrt(total * count)
    if fast:
        wide_row = wide_pair[1:]
        self_kept, self_sends = fold_square(spot, self_kept, self_moved)
        self_moved = move_layers(self_sends)
        layer_own, layer_send = call(
            fold_last_kernel, "fold_last", [], [layer_keep, after(layer_got, *self_sends)],
            [(wide_row, FULL), (wide_row, LOW)], 1,
        )
        layer_got = exchange(layer_send, 2)
        kinds = [FULL, FULL, FULL, LOW]
        ffn_out_state = (ffn_out_master, ffn_out_first, ffn_out_second)
        ffn_in_state = (ffn_in_master, ffn_in_first, ffn_in_second)
        ffn_new = call(
            functools.partial(ffn_update_kernel, grad_scale), "ffn_update", [],
            [layer_own, layer_got, *ffn_in_state, *ffn_out_state],
            [(ffn_in_master.shape, kind) for kind in kinds]
            + [(ffn_out_master.shape, kind) for kind in kinds], 1,
        )
        states = [
            qkv_master, qkv_first, qkv_second, out_master, out_first, out_second,
            vector_master.T, vector_first.T, vector_second.T,
        ]
        final_new = call(
            functools.partial(final_update_kernel, grad_scale, 2 * hidden), "final_update", [],
            [layer_own, layer_got, self_kept, *self_moved, *states],
            [(item.shape, kind) for item in states[::3] for kind in kinds], 1,
        )
        return (
            layer_out, tokens_grad, encoded_grad, *final_new[:8], *ffn_new,
            *[item.T for item in final_new[8:]],
        )
    cross_kept, cross_sends = fold_square(
        spot, cross_kept, [after(item, *self_sends) for item in cross_moved]
    )
    cross_moved = move_layers(cross_sends)
    ffn_total = add_all(ffn_kept, ffn_moved)
    cross_total = add_all(cross_kept, cross_moved)
    self_kept, self_sends = fold_square(
        spot, self_kept, [after(item, *cross_sends) for item in self_moved]
    )
    self_moved = move_layers(self_sends)
    self_total = add_all(self_kept, self_moved)

    def block(values, index):
        return values[:, index * model : (index + 1) * model]

    summed_qkv = jnp.stack(
        [block(self_total, i) for i in range(3)] + [block(cross_total, i) for i in range(3)]
    )
    summed_out = jnp.stack([block(self_total, 3), block(cross_total, 3)])
    summed_ffn_in = ffn_total[:, :hidden]
    summed_ffn_out = (
        ffn_total[:, hidden:].reshape(rows, pieces, model).transpose(1, 0, 2).reshape(-1, model)
    )
    summed_vector = self_total[:, 4 * model : 4 * model + vector_master.shape[0]].T
    qkv_first_new, qkv_second_new, qkv_master_new, qkv_copy = adamw(
        qkv_master, summed_qkv * grad_scale, qkv_first, qkv_second, 0.04
    )
    out_first_new, out_second_new, out_master_new, out_copy = adamw(
        out_master, summed_out * grad_scale, out_first, out_second, 0.3
    )
    ffn_in_first_new, ffn_in_second_new, ffn_in_master_new, ffn_in_copy = adamw(
        ffn_in_master, summed_ffn_in * grad_scale, ffn_in_first, ffn_in_second, 0.04
    )
    ffn_out_first_new, ffn_out_second_new, ffn_out_master_new, ffn_out_copy = adamw(
        ffn_out_master, summed_ffn_out * grad_scale, ffn_out_first, ffn_out_second, 0.02
    )
    vector_first_new, vector_second_new, vector_master_new, vector_copy = adamw(
        vector_master, summed_vector * grad_scale, vector_first, vector_second, 0.35
    )
    return (
        layer_out,
        tokens_grad,
        encoded_grad,
        qkv_first_new,
        qkv_second_new,
        qkv_master_new,
        qkv_copy,
        out_first_new,
        out_second_new,
        out_master_new,
        out_copy,
        ffn_in_first_new,
        ffn_in_second_new,
        ffn_in_master_new,
        ffn_in_copy,
        ffn_out_first_new,
        ffn_out_second_new,
        ffn_out_master_new,
        ffn_out_copy,
        vector_first_new,
        vector_second_new,
        vector_master_new,
        vector_copy,
    )


def solution(mesh):
    return jax.shard_map(
        body,
        mesh=mesh,
        in_specs=(
            P(("dp", "fsdp"), None),
            P(("dp", "fsdp"), None),
            P(("dp", "fsdp"), None),
            P(("dp", "fsdp"), None),
            P(("dp", "fsdp"), None),
            P(None, ("dp", "fsdp"), None),
            P(None, ("dp", "fsdp"), None),
            P(None, ("dp", "fsdp"), None),
            P(None, ("dp", "fsdp"), None),
            P(None, ("dp", "fsdp"), None),
            P(None, ("dp", "fsdp"), None),
            P(("dp", "fsdp"), None),
            P(("dp", "fsdp"), None),
            P(("dp", "fsdp"), None),
            P(("dp", "fsdp"), None),
            P(("dp", "fsdp"), None),
            P(("dp", "fsdp"), None),
            P(None, ("dp", "fsdp")),
            P(None, ("dp", "fsdp")),
            P(None, ("dp", "fsdp")),
        ),
        out_specs=(
            P(("dp", "fsdp"), None),
            P(("dp", "fsdp"), None),
            P(("dp", "fsdp"), None),
            P(None, ("dp", "fsdp"), None),
            P(None, ("dp", "fsdp"), None),
            P(None, ("dp", "fsdp"), None),
            P(None, ("dp", "fsdp"), None),
            P(None, ("dp", "fsdp"), None),
            P(None, ("dp", "fsdp"), None),
            P(None, ("dp", "fsdp"), None),
            P(None, ("dp", "fsdp"), None),
            P(("dp", "fsdp"), None),
            P(("dp", "fsdp"), None),
            P(("dp", "fsdp"), None),
            P(("dp", "fsdp"), None),
            P(("dp", "fsdp"), None),
            P(("dp", "fsdp"), None),
            P(("dp", "fsdp"), None),
            P(("dp", "fsdp"), None),
            P(None, ("dp", "fsdp")),
            P(None, ("dp", "fsdp")),
            P(None, ("dp", "fsdp")),
            P(None, ("dp", "fsdp")),
        ),
        check_vma=False,
    )
```
